32 devices in a mesh: dp: 8 (over z, y), tensor: 4 (over x, core).
Axes of the slice: x: 2, y: 2, z: 4, core: 2. Of those that a mesh axis runs over, the one named last changes fastest.
Arguments:
- tokens: bfloat16 [16384, 768], P(('dp', 'tensor')), may hold values from -6 to 6
- grad_out: bfloat16 [16384, 768], P(('dp', 'tensor')), may hold values from -6 to 6
- seg_ids: int32 [16, 1024], P('dp'), may hold values from 0 to 5, never falling along the last dimension, each value on 1 to 800 neighbouring positions
- w_qkv: bfloat16 [3, 768, 768], P(None, 'dp', 'tensor'), may hold values from -0.21875 to 0.21875
- b_qv: bfloat16 [2, 768], P(None, ('tensor', 'dp')), may hold values from -3 to 3
- w_out: bfloat16 [768, 768], P('tensor', 'dp'), may hold values from -1.75 to 1.75
- w_up: bfloat16 [768, 3072], P('dp', 'tensor'), may hold values from -0.21875 to 0.21875
- b_up: bfloat16 [3072], P(('tensor', 'dp')), may hold values from -3 to 3
- w_down: bfloat16 [3072, 768], P('tensor', 'dp'), may hold values from -0.21875 to 0.21875
- b_out: float32 [768], P(('dp', 'tensor')), may hold values from -2 to 2
- b_down: float32 [768], P(('dp', 'tensor')), may hold values from -2 to 2
- g_one: float32 [768], P(('dp', 'tensor')), may hold values from 0.5 to 1.5
- s_one: float32 [768], P(('dp', 'tensor')), may hold values from -2 to 2
- g_two: float32 [768], P(('dp', 'tensor')), may hold values from 0.5 to 1.5
- s_two: float32 [768], P(('dp', 'tensor')), may hold values from -2 to 2
Outputs:
- layer_out: bfloat16 [16384, 768], P(('dp', 'tensor'))
- input_grad: bfloat16 [16384, 768], P(('dp', 'tensor'))
- grad_qkv: float32 [3, 768, 768], P(None, 'dp', 'tensor')
- grad_bias_qv: float32 [2, 768], P(None, ('tensor', 'dp'))
- grad_out_proj: float32 [768, 768], P('tensor', 'dp')
- grad_up: float32 [768, 3072], P('dp', 'tensor')
- grad_bias_up: float32 [3072], P(('tensor', 'dp'))
- grad_down: float32 [3072, 768], P('tensor', 'dp')
- grad_bias_out: float32 [768], P(('dp', 'tensor'))
- grad_bias_down: float32 [768], P(('dp', 'tensor'))
- grad_gain_one: float32 [768], P(('dp', 'tensor'))
- grad_shift_one: float32 [768], P(('dp', 'tensor'))
- grad_gain_two: float32 [768], P(('dp', 'tensor'))
- grad_shift_two: float32 [768], P(('dp', 'tensor'))
The draws below stay inside these ranges and needn't reach their ends.
Inputs may be any that keep to these rules, and one draw needn't show every extreme that they name: `seg_ids`: within a sequence the ids never fall; each document spans 1 to 800 tokens, and the longest one of a draw spans exactly 800.
All inputs are finite; a program needn't handle non-finite values.
Results may differ from the reference program's by a relative error of at most 0.024.
Values may be sent and summed in bfloat16 or wider, within the bound.
No kernel may reach another device: no remote copies, remote signals or barrier semaphores. Data moves between devices by JAX's collectives and lax.ppermute only.
A program may use at most 128 MiB of HBM per device.

```python
import math
import jax
import jax.numpy as jnp
import numpy as np
from jax import lax

D = 768
HEADS = 12
HD = 64
FF = 3072
SEQ = 1024
NSEQ = 16
TOKENS = 16384
DOCS = 6
DOC_MOST = 800


def levels(own_key, dims, shards, smallest, high):
    level = 1.0
    for axis_at, shards_of in shards:
        heights = jax.random.uniform(jax.random.fold_in(jax.random.fold_in(own_key, 6), axis_at), (shards_of,), jnp.float32, smallest / len(shards), high / len(shards))
        level = level * jnp.repeat(jnp.exp(heights), dims[axis_at] // shards_of).reshape((-1,) + (1,) * (len(dims) - 1 - axis_at))
    return level


def length_profile(number_of, total, limit, slope):
    portions = [(1 << 20) // math.isqrt(grade ** slope) + 1 for grade in range(2, number_of + 1)]
    spare, given = total - limit - (number_of - 1), [1] * (number_of - 1)
    while spare > 0:
        movable = [i for i in range(number_of - 1) if given[i] < limit]
        mass, left = sum([portions[i] for i in movable]), spare
        for i in movable:
            extra = min(limit - given[i], max(1, left * portions[i] // mass), spare)
            given[i] = given[i] + extra
            spare = spare - extra
    return np.array([limit] + given)


def uneven(rng, amount, total, bound, skew):
    if amount == 2:
        one = jax.random.randint(rng, (), max(1, total - bound), min(bound, total - 1) + 1)
        return jnp.stack([one, total - one])
    lengths = jnp.asarray(length_profile(amount, total, bound, skew), jnp.int32)
    couples = (amount - 1) // 2
    source_of, sink = lengths[1:1 + 2 * couples:2], lengths[2:2 + 2 * couples:2]
    room = jnp.minimum(source_of - 1, bound - sink)
    passed = jax.random.randint(jax.random.fold_in(rng, 1), (couples,), 0, 1 << 20) % (room + 1)
    lengths = lengths.at[1:1 + 2 * couples:2].set(source_of - passed).at[2:2 + 2 * couples:2].set(sink + passed)
    return lengths[jax.random.permutation(jax.random.fold_in(rng, 2), amount)]


def gaussian(own_key, shape, spread, bound, cuts=(), kind=jnp.bfloat16):
    array = spread * jax.random.normal(own_key, shape, jnp.float32)
    if cuts:
        array = array * levels(own_key, shape, cuts, -0.22, 0.18)
    return jnp.clip(array, -bound, bound).astype(kind)


def setup_inputs(seed: int = 0) -> dict:
    splits = jax.random.split(jax.random.key(seed), 16)
    return {
        "tokens": gaussian(splits[0], (TOKENS, D), 1.0, 6.0, ((0, 32),)),
        "grad_out": gaussian(splits[1], (TOKENS, D), 1.0, 6.0, ((0, 32),)),
        "seg_ids": jax.vmap(lambda own: jnp.searchsorted(jnp.cumsum(uneven(own, DOCS, SEQ, DOC_MOST, 2)), jnp.arange(SEQ), side="right"))(jax.random.split(splits[2], NSEQ)).reshape((NSEQ, SEQ)).astype(jnp.int32),
        "w_qkv": gaussian(splits[3], (3, D, D), D ** -0.5, 0.21875, ((1, 8), (2, 4))),
        "b_qv": gaussian(splits[4], (2, D), 0.5, 3.0, ((1, 32),)),
        "w_out": gaussian(splits[5], (D, D), (D // 64) ** -0.5, 1.75, ((0, 4), (1, 8))),
        "w_up": gaussian(splits[6], (D, FF), D ** -0.5, 0.21875, ((0, 8), (1, 4))),
        "b_up": gaussian(splits[7], (FF,), 0.5, 3.0, ((0, 32),)),
        "w_down": gaussian(splits[8], (FF, D), (FF // 4) ** -0.5, 0.21875, ((0, 4), (1, 8))),
        "b_out": gaussian(splits[9], (D,), 0.3, 2.0, ((0, 32),), jnp.float32),
        "b_down": gaussian(splits[10], (D,), 0.3, 2.0, ((0, 32),), jnp.float32),
        "g_one": jnp.clip(1.0 + 0.1 * jax.random.normal(splits[11], (D,), jnp.float32), 0.5, 1.5),
        "s_one": gaussian(splits[12], (D,), 0.3, 2.0, ((0, 32),), jnp.float32),
        "g_two": jnp.clip(1.0 + 0.1 * jax.random.normal(splits[13], (D,), jnp.float32), 0.5, 1.5),
        "s_two": gaussian(splits[14], (D,), 0.3, 2.0, ((0, 32),), jnp.float32),
    }


HIGH = lax.Precision.HIGHEST
EPSILON = 1e-05
ROOT_HALF = 0.7071067811865476

@jax.custom_vjp
def low(v):
    return lax.optimization_barrier(v.astype(jnp.bfloat16)).astype(jnp.float32)

@jax.custom_vjp
def low_back(v):
    return v

def low_keep(v):
    return (low(v), None)

def low_pass(kept, grad):
    return (grad,)

def back_keep(v):
    return (v, None)

def back_low(kept, grad):
    return (low(grad),)
low.defvjp(low_keep, low_pass)
low_back.defvjp(back_keep, back_low)

def norm_rows(r, gain, shift):
    mean = lax.optimization_barrier(jnp.mean(r, axis=-1, keepdims=True))
    cent = r - mean
    var = lax.optimization_barrier(jnp.mean(cent * cent, axis=-1, keepdims=True))
    return cent * lax.rsqrt(var + EPSILON) * gain + shift

def gelu_exact(u):
    return 0.5 * u * (1.0 + lax.erf(u * ROOT_HALF))

def forward(xs, seg, w_qkv, b_qv, w_out, w_up, b_up, w_down, b_out, b_down, g_one, s_one, g_two, s_two):
    count = xs.shape[0]
    flat = xs.reshape(count * SEQ, D)
    proj = jnp.einsum('td,jde->jte', flat, w_qkv, precision=HIGH)
    biases = jnp.stack([b_qv[0], jnp.zeros_like(b_qv[0]), b_qv[1]])
    proj = low_back(low(proj + biases[:, None, :]))
    heads = proj.reshape(3, count, SEQ, HEADS, HD)
    raw = jnp.einsum('nqhd,nkhd->nhqk', heads[0], heads[1], precision=HIGH)
    scores = low_back(raw * 0.125)
    same = seg[:, None, :, None] == seg[:, None, None, :]
    scores = jnp.where(same, scores, -1000000000.0)
    top = lax.optimization_barrier(jnp.max(scores, axis=-1, keepdims=True))
    expo = jnp.exp(scores - top)
    probs = low(expo / lax.optimization_barrier(jnp.sum(expo, axis=-1, keepdims=True)))
    context = jnp.einsum('nhqk,nkhd->nqhd', probs, heads[2], precision=HIGH)
    context = low_back(low(context.reshape(count * SEQ, D)))
    attn = low_back(jnp.dot(context, w_out, precision=HIGH) + b_out)
    first = flat + attn
    normed = norm_rows(first, g_one, s_one)
    up = low_back(jnp.dot(low(normed), w_up, precision=HIGH) + b_up)
    hidden = low(gelu_exact(up))
    branch = low_back(jnp.dot(hidden, w_down, precision=HIGH) + b_down)
    second = normed + branch
    return norm_rows(second, g_two, s_two).reshape(count, SEQ, D)

def reference(tokens, grad_out, seg_ids, w_qkv, b_qv, w_out, w_up, b_up, w_down, b_out, b_down, g_one, s_one, g_two, s_two):
    params = tuple((p.astype(jnp.float32) for p in (w_qkv, b_qv, w_out, w_up, b_up, w_down, b_out, b_down, g_one, s_one, g_two, s_two)))
    steps = NSEQ // 4
    xs = tokens.astype(jnp.float32).reshape(steps, 4, SEQ, D)
    gs = grad_out.astype(jnp.float32).reshape(steps, 4, SEQ, D)
    ss = seg_ids.reshape(steps, 4, SEQ)

    def step(acc, item):
        xin, gin, sin = item

        def apply(xx, *pp):
            return forward(xx, sin, *pp)
        yout, pull = jax.vjp(apply, xin, *params)
        grads = pull(gin)
        acc = tuple((a + b for a, b in zip(acc, grads[1:])))
        return (acc, (yout, grads[0]))
    zeros = tuple((jnp.zeros_like(p) for p in params))
    acc, (ys, dxs) = lax.scan(step, zeros, (xs, gs, ss))
    layer_out = ys.reshape(TOKENS, D).astype(jnp.bfloat16)
    input_grad = dxs.reshape(TOKENS, D).astype(jnp.bfloat16)
    return (layer_out, input_grad, acc[0], acc[1], acc[2], acc[3], acc[4], acc[5], acc[6], acc[7], acc[8], acc[9], acc[10], acc[11])
```

```python
import functools

import jax
import jax.numpy as jnp
from jax import lax
from jax.experimental import pallas as pl
from jax.experimental.pallas import tpu as pltpu
from jax.sharding import Mesh, PartitionSpec as P

HD = 64
LANES = 128
EPSILON = 1e-05
ROOT_HALF = 0.7071067811865476
INV_ROOT_TWO_PI = 0.3989422804014327
F32 = jnp.float32
BF16 = jnp.bfloat16


def dot(a, b, dims):
    return lax.dot_general(a, b, (dims, ((), ())), preferred_element_type=F32)


def dot_nn(a, b):
    return dot(a, b, ((1,), (0,)))


def dot_nt(a, b):
    return dot(a, b, ((1,), (1,)))


def dot_tn(a, b):
    return dot(a, b, ((0,), (0,)))


def attention_forward_kernel(width, seg_q_ref, seg_k_ref, q_ref, k_ref, v_ref, ctx_ref, lse_ref):
    lane = lax.broadcasted_iota(jnp.int32, (1, LANES), 1)
    bias = jnp.where(seg_q_ref[...] == seg_k_ref[...], 0.0, -1000000000.0)
    block = q_ref.shape[0]
    stats = jnp.zeros((block, LANES), F32)
    for pair in range(width // LANES):
        cols = slice(pair * LANES, (pair + 1) * LANES)
        q2 = q_ref[:, cols] * jnp.asarray(0.125, BF16)
        k2 = k_ref[:, cols]
        v2 = v_ref[:, cols]
        outs = []
        for half in range(2):
            mine = (lane // HD) == half
            qm = jnp.where(mine, q2, jnp.zeros_like(q2))
            s = dot_nt(qm, k2) + bias
            top = jnp.max(s, axis=-1, keepdims=True)
            e = jnp.exp(s - top)
            total = jnp.sum(e, axis=-1, keepdims=True)
            o = dot_nn(e.astype(BF16), v2) * (1.0 / total)
            outs.append(o)
            stats = jnp.where(lane == 2 * pair + half, top + jnp.log(total), stats)
        ctx_ref[:, cols] = jnp.where(lane < HD, outs[0], outs[1]).astype(BF16)
    lse_ref[...] = stats.T[: lse_ref.shape[0], :]


def attention_forward(qkv, seg_col, seg_row, block):
    rows, triple = qkv.shape
    width = triple // 3
    return pl.pallas_call(
        functools.partial(attention_forward_kernel, width),
        grid=(rows // block,),
        in_specs=[
            pl.BlockSpec((block, 1), lambda i: (i, 0)),
            pl.BlockSpec((1, rows), lambda i: (0, 0)),
            pl.BlockSpec((block, width), lambda i: (i, 0)),
            pl.BlockSpec((rows, width), lambda i: (0, 1)),
            pl.BlockSpec((rows, width), lambda i: (0, 2)),
        ],
        out_specs=[
            pl.BlockSpec((block, width), lambda i: (i, 0)),
            pl.BlockSpec((8, block), lambda i: (0, i)),
        ],
        out_shape=[
            jax.ShapeDtypeStruct((rows, width), BF16),
            jax.ShapeDtypeStruct((8, rows), F32),
        ],
        cost_estimate=pl.CostEstimate(
            flops=4 * rows * rows * width * 4,
            bytes_accessed=8 * rows * width,
            transcendentals=rows * rows * width // HD,
        ),
        name="attention_forward",
    )(seg_col, seg_row, qkv, qkv, qkv)


def attention_backward_kernel(
    width, seg_k_ref, seg_q_ref, q_ref, k_ref, v_ref, ctx_ref, lse_ref, d_ref, out_ref, dk_ref, dv_ref
):
    step = pl.program_id(0)
    block = q_ref.shape[0]
    lane = lax.broadcasted_iota(jnp.int32, (1, LANES), 1)

    @pl.when(step == 0)
    def _():
        dk_ref[...] = jnp.zeros_like(dk_ref)
        dv_ref[...] = jnp.zeros_like(dv_ref)

    bias = jnp.where(seg_k_ref[...] == seg_q_ref[...], 0.0, -1000000000.0)
    for pair in range(width // LANES):
        cols = slice(pair * LANES, (pair + 1) * LANES)
        q2 = q_ref[:, cols] * jnp.asarray(0.125, BF16)
        k2 = k_ref[:, cols]
        v2 = v_ref[:, cols]
        d2 = d_ref[:, cols]
        prod = (d2.astype(F32) * ctx_ref[:, cols].astype(F32)).T
        kt = (k2 * jnp.asarray(0.125, BF16)).T
        row = lax.broadcasted_iota(jnp.int32, (LANES, 1), 0)
        dq = None
        dk = None
        dv = None
        for half in range(2):
            mine = (lane // HD) == half
            qm = jnp.where(mine, q2, jnp.zeros_like(q2))
            dm = jnp.where(mine, d2, jnp.zeros_like(d2))
            ktm = jnp.where((row // HD) == half, kt, jnp.zeros_like(kt))
            inner = jnp.sum(prod[half * HD : (half + 1) * HD, :], axis=0, keepdims=True)
            head = 2 * pair + half
            lse = lse_ref[head : head + 1, :]
            p = jnp.exp(dot_nt(k2, qm) + bias - lse)
            dp = dot_nt(v2, dm)
            ds = (p * (dp - inner)).astype(BF16)
            dv_h = dot_nn(p.astype(BF16), dm)
            dk_h = dot_nn(ds, qm)
            dq_h = dot_nn(ktm, ds)
            dv = dv_h if dv is None else dv + dv_h
            dk = dk_h if dk is None else dk + dk_h
            dq = dq_h if dq is None else dq + dq_h
        dk_ref[:, cols] += dk
        dv_ref[:, cols] += dv
        out_ref[pl.ds(pl.multiple_of(step * block, block), block), cols] = dq.T.astype(BF16)

    @pl.when(step == pl.num_programs(0) - 1)
    def _():
        out_ref[:, width : 2 * width] = dk_ref[...].astype(BF16)
        out_ref[:, 2 * width : 3 * width] = dv_ref[...].astype(BF16)


def attention_backward(qkv, ctx, lse, d_ctx, seg_col, seg_row, block):
    rows, triple = qkv.shape
    width = triple // 3
    return pl.pallas_call(
        functools.partial(attention_backward_kernel, width),
        grid=(rows // block,),
        in_specs=[
            pl.BlockSpec((rows, 1), lambda i: (0, 0)),
            pl.BlockSpec((1, block), lambda i: (0, i)),
            pl.BlockSpec((block, width), lambda i: (i, 0)),
            pl.BlockSpec((rows, width), lambda i: (0, 1)),
            pl.BlockSpec((rows, width), lambda i: (0, 2)),
            pl.BlockSpec((block, width), lambda i: (i, 0)),
            pl.BlockSpec((8, block), lambda i: (0, i)),
            pl.BlockSpec((block, width), lambda i: (i, 0)),
        ],
        out_specs=pl.BlockSpec((rows, triple), lambda i: (0, 0)),
        out_shape=jax.ShapeDtypeStruct((rows, triple), BF16),
        scratch_shapes=[pltpu.VMEM((rows, width), F32), pltpu.VMEM((rows, width), F32)],
        cost_estimate=pl.CostEstimate(
            flops=10 * rows * rows * width * 4,
            bytes_accessed=16 * rows * width,
            transcendentals=rows * rows * width // HD,
        ),
        name="attention_backward",
    )(seg_col, seg_row, qkv, qkv, qkv, ctx, lse, d_ctx)


def normalize(r):
    mean = jnp.mean(r, axis=-1, keepdims=True)
    cent = r - mean
    var = jnp.mean(cent * cent, axis=-1, keepdims=True)
    inv = lax.rsqrt(var + EPSILON)
    return cent * inv, inv


def normalize_back(hat, inv, gain, d_out):
    d_hat = d_out * gain
    first = jnp.mean(d_hat, axis=-1, keepdims=True)
    second = jnp.mean(d_hat * hat, axis=-1, keepdims=True)
    return inv * (d_hat - first - hat * second)


def swap(a):
    return lax.ppermute(a, "c", [(0, 1), (1, 0)])


def pair_gather(a):
    return jnp.concatenate([a, swap(a)], axis=0)


def pair_sum(full, rows):
    return full[:rows] + swap(full[rows:].astype(BF16)).astype(F32)


def gather_units(a):
    ndp = lax.axis_size("dp")
    nx = lax.axis_size("x")
    g = lax.all_gather(a, ("dp", "x"), axis=0, tiled=False)
    g = g.reshape(ndp, nx, *a.shape)
    return jnp.transpose(g, (1, 0, 2, 3)).reshape(nx, ndp * a.shape[0], a.shape[1])


def scatter_units(g):
    ndp = lax.axis_size("dp")
    nx, model, cols = g.shape
    g = g.reshape(nx, ndp, model // ndp, cols)
    g = jnp.transpose(g, (1, 0, 2, 3)).reshape(ndp * nx * (model // ndp), cols)
    return lax.psum_scatter(g, ("dp", "x"), scatter_dimension=0, tiled=True)


def local(
    tokens, grad_out, seg_ids, w_qkv, b_qv, w_out, w_up, b_up, w_down, b_out, b_down, g_one, s_one, g_two, s_two
):
    ndp = lax.axis_size("dp")
    nx = lax.axis_size("x")
    parity = lax.axis_index("c")
    which = lax.axis_index("x")
    rows, model = tokens.shape
    piece = model // ndp
    part = w_qkv.shape[2]
    width = nx * part

    seg = lax.dynamic_index_in_dim(seg_ids, which, 0, keepdims=False)
    seg_two = seg.reshape(2, rows)
    seg_rel = jnp.concatenate(
        [
            lax.dynamic_index_in_dim(seg_two, parity, 0, keepdims=False),
            lax.dynamic_index_in_dim(seg_two, 1 - parity, 0, keepdims=False),
        ]
    )
    seg_col = seg_rel[:, None]
    seg_row = seg_rel[None, :]

    unit_a = jnp.concatenate([w_qkv[0], w_qkv[1], w_qkv[2], w_out.T], axis=1)
    a_full = gather_units(unit_a)
    b_full = gather_units(w_up)
    c_full = gather_units(w_down.T)
    slim = model // (ndp * nx * 2)
    small = jnp.concatenate(
        [
            b_out,
            b_down,
            g_one,
            s_one,
            g_two,
            s_two,
            b_qv.reshape(-1).astype(F32),
            b_up.astype(F32),
        ]
    )
    small = lax.all_gather(small, ("dp", "x", "c"), axis=0, tiled=False)
    vectors = jnp.transpose(small[:, : 6 * slim].reshape(ndp * nx * 2, 6, slim), (1, 0, 2)).reshape(6, model)
    bout_f, bdown_f, gone_f, sone_f, gtwo_f, stwo_f = [vectors[i : i + 1] for i in range(6)]
    wide = small[:, 6 * slim :].reshape(ndp, nx, 2, -1)
    wide = lax.dynamic_index_in_dim(wide, parity, 2, keepdims=False)
    qv = part // ndp
    bias_qv = jnp.transpose(wide[:, :, : 2 * qv].reshape(ndp, nx, 2, qv), (2, 1, 0, 3)).reshape(2, width)
    bias_qkv = jnp.concatenate([bias_qv[0], jnp.zeros((width,), F32), bias_qv[1]])[None]
    bias_up = jnp.transpose(wide[:, :, 2 * qv :], (1, 0, 2)).reshape(1, nx * model)

    x_own = tokens
    x_full = pair_gather(x_own)
    w_all = jnp.concatenate([a_full[i][:, j * part : (j + 1) * part] for j in range(3) for i in range(nx)], axis=1)
    o_t = jnp.concatenate([a_full[i][:, 3 * part :] for i in range(nx)], axis=1)
    b_all = jnp.concatenate([b_full[i] for i in range(nx)], axis=1)
    c_all = jnp.concatenate([c_full[i] for i in range(nx)], axis=1)

    qkv = (dot_nn(x_full, w_all) + bias_qkv).astype(BF16)
    block = 256
    ctx, lse = attention_forward(qkv, seg_col, seg_row, block)
    attn = pair_sum(dot_nt(ctx, o_t), rows)
    first = x_own.astype(F32) + attn + bout_f
    hat_one, inv_one = normalize(first)
    normed = hat_one * gone_f + sone_f
    normed_full = pair_gather(normed.astype(BF16))
    up = dot_nn(normed_full, b_all) + bias_up
    cdf = 0.5 * (1.0 + lax.erf(up * ROOT_HALF))
    hidden = (up * cdf).astype(BF16)
    slope = (cdf + up * (jnp.exp(-0.5 * up * up) * INV_ROOT_TWO_PI)).astype(BF16)
    branch = pair_sum(dot_nt(hidden, c_all), rows)
    second = normed + branch + bdown_f
    hat_two, inv_two = normalize(second)
    layer_out = (hat_two * gtwo_f + stwo_f).astype(BF16)

    g_in = grad_out.astype(F32)
    d_gain_two = jnp.sum(g_in * hat_two, axis=0)
    d_shift_two = jnp.sum(g_in, axis=0)
    d_second = normalize_back(hat_two, inv_two, gtwo_f, g_in)
    d_branch = d_second.astype(BF16)
    d_bias_down = jnp.sum(d_branch.astype(F32), axis=0)
    db_full = pair_gather(d_branch)
    grad_c = dot_tn(db_full, hidden).astype(BF16)
    d_hidden = dot_nn(db_full, c_all)
    d_up = (d_hidden * slope.astype(F32)).astype(BF16)
    d_bias_up = jnp.sum(d_up.astype(F32), axis=0)
    grad_b = dot_tn(normed_full, d_up).astype(BF16)
    d_normed = d_second + pair_sum(dot_nt(d_up, b_all), rows)
    d_gain_one = jnp.sum(d_normed * hat_one, axis=0)
    d_shift_one = jnp.sum(d_normed, axis=0)
    d_first = normalize_back(hat_one, inv_one, gone_f, d_normed)
    d_attn = d_first.astype(BF16)
    d_bias_out = jnp.sum(d_attn.astype(F32), axis=0)
    da_full = pair_gather(d_attn)
    grad_o = dot_tn(da_full, ctx).astype(BF16)
    d_ctx = dot_nn(da_full, o_t).astype(BF16)
    d_qkv = attention_backward(qkv, ctx, lse, d_ctx, seg_col, seg_row, block)
    d_bias_qkv = jnp.sum(d_qkv.astype(F32), axis=0)
    grad_w = dot_tn(x_full, d_qkv).astype(BF16)
    input_grad = (d_first + pair_sum(dot_nt(d_qkv, w_all), rows)).astype(BF16)

    unit_ga = jnp.stack(
        [
            jnp.concatenate(
                [grad_w[:, j * width + i * part : j * width + (i + 1) * part] for j in range(3)]
                + [grad_o[:, i * part : (i + 1) * part]],
                axis=1,
            )
            for i in range(nx)
        ]
    )
    ga = scatter_units(unit_ga).astype(F32)
    gb = scatter_units(jnp.stack([grad_b[:, i * model : (i + 1) * model] for i in range(nx)])).astype(F32)
    gc = scatter_units(jnp.stack([grad_c[:, i * model : (i + 1) * model] for i in range(nx)])).astype(F32)
    g_qkv = jnp.stack([ga[:, j * part : (j + 1) * part] for j in range(3)])
    g_out = ga[:, 3 * part :].T

    sums = jnp.stack([d_bias_out, d_bias_down, d_gain_one, d_shift_one, d_gain_two, d_shift_two])
    sums = jnp.transpose(sums.reshape(6, ndp * nx * 2, slim), (1, 0, 2)).reshape(ndp, nx, 2, 6 * slim)
    d_bqv = jnp.stack([d_bias_qkv[:width], d_bias_qkv[2 * width :]]).reshape(2, nx, ndp, qv)
    d_bqv = jnp.transpose(d_bqv, (2, 1, 0, 3)).reshape(ndp, nx, 1, 2 * qv)
    d_bup = jnp.transpose(d_bias_up.reshape(nx, ndp, piece), (1, 0, 2))[:, :, None]
    tail = jnp.concatenate([d_bqv, d_bup], axis=-1)
    tail = jnp.where(lax.broadcasted_iota(jnp.int32, (1, 1, 2, 1), 2) == parity, tail, 0.0)
    packed = jnp.concatenate([sums, tail], axis=-1).reshape(ndp * nx * 2, -1)
    mine = lax.psum_scatter(packed, ("dp", "x", "c"), scatter_dimension=0, tiled=True)[0]
    six = [mine[i * slim : (i + 1) * slim] for i in range(6)]
    g_bqv = mine[6 * slim : 6 * slim + 2 * qv].reshape(2, qv)
    g_bup = mine[6 * slim + 2 * qv :]
    return (layer_out, input_grad, g_qkv, g_bqv, g_out, gb, g_bup, gc.T, *six)


def solution(mesh):
    ndp, nt = mesh.devices.shape
    fine = Mesh(mesh.devices.reshape(ndp, nt // 2, 2), ("dp", "x", "c"))
    tensor = ("x", "c")
    every = ("dp", "x", "c")
    row = P(every, None)
    vec = P(every)
    return jax.shard_map(
        local,
        mesh=fine,
        in_specs=(
            row,
            row,
            P("dp", None),
            P(None, "dp", tensor),
            P(None, ("x", "c", "dp")),
            P(tensor, "dp"),
            P("dp", tensor),
            P(("x", "c", "dp")),
            P(tensor, "dp"),
            vec,
            vec,
            vec,
            vec,
            vec,
            vec,
        ),
        out_specs=(
            row,
            row,
            P(None, "dp", tensor),
            P(None, ("x", "c", "dp")),
            P(tensor, "dp"),
            P("dp", tensor),
            P(("x", "c", "dp")),
            P(tensor, "dp"),
            vec,
            vec,
            vec,
            vec,
            vec,
            vec,
        ),
        check_vma=False,
    )
```

```python
import functools

import jax
import jax.numpy as jnp
from jax import lax
from jax.experimental import pallas as pl
from jax.experimental.pallas import tpu as pltpu
from jax.sharding import Mesh, PartitionSpec as P

HD = 64
LANES = 128
EPSILON = 1e-05
ROOT_HALF = 0.7071067811865476
INV_ROOT_TWO_PI = 0.3989422804014327
F32 = jnp.float32
BF16 = jnp.bfloat16


def dot(a, b, dims):
    return lax.dot_general(a, b, (dims, ((), ())), preferred_element_type=F32)


def dot_nn(a, b):
    return dot(a, b, ((1,), (0,)))


def dot_nt(a, b):
    return dot(a, b, ((1,), (1,)))


def dot_tn(a, b):
    return dot(a, b, ((0,), (0,)))


def attention_forward_kernel(width, seg_q_ref, seg_k_ref, q_ref, k_ref, v_ref, ctx_ref, lse_ref):
    lane = lax.broadcasted_iota(jnp.int32, (1, LANES), 1)
    bias = jnp.where(seg_q_ref[...] == seg_k_ref[...], 0.0, -1000000000.0)
    block = q_ref.shape[0]
    stats = jnp.zeros((block, LANES), F32)
    for pair in range(width // LANES):
        cols = slice(pair * LANES, (pair + 1) * LANES)
        q2 = q_ref[:, cols] * jnp.asarray(0.125, BF16)
        k2 = k_ref[:, cols]
        v2 = v_ref[:, cols]
        outs = []
        for half in range(2):
            mine = (lane // HD) == half
            qm = jnp.where(mine, q2, jnp.zeros_like(q2))
            s = dot_nt(qm, k2) + bias
            top = jnp.max(s, axis=-1, keepdims=True)
            e = jnp.exp(s - top)
            total = jnp.sum(e, axis=-1, keepdims=True)
            o = dot_nn(e.astype(BF16), v2) * (1.0 / total)
            outs.append(o)
            stats = jnp.where(lane == 2 * pair + half, top + jnp.log(total), stats)
        ctx_ref[:, cols] = jnp.where(lane < HD, outs[0], outs[1]).astype(BF16)
    lse_ref[...] = stats.T[: lse_ref.shape[0], :]


def attention_forward(qkv, seg_col, seg_row, block):
    rows, triple = qkv.shape
    width = triple // 3
    return pl.pallas_call(
        functools.partial(attention_forward_kernel, width),
        grid=(rows // block,),
        in_specs=[
            pl.BlockSpec((block, 1), lambda i: (i, 0)),
            pl.BlockSpec((1, rows), lambda i: (0, 0)),
            pl.BlockSpec((block, width), lambda i: (i, 0)),
            pl.BlockSpec((rows, width), lambda i: (0, 1)),
            pl.BlockSpec((rows, width), lambda i: (0, 2)),
        ],
        out_specs=[
            pl.BlockSpec((block, width), lambda i: (i, 0)),
            pl.BlockSpec((8, block), lambda i: (0, i)),
        ],
        out_shape=[
            jax.ShapeDtypeStruct((rows, width), BF16),
            jax.ShapeDtypeStruct((8, rows), F32),
        ],
        cost_estimate=pl.CostEstimate(
            flops=4 * rows * rows * width * 4,
            bytes_accessed=8 * rows * width,
            transcendentals=rows * rows * width // HD,
        ),
        name="attention_forward",
    )(seg_col, seg_row, qkv, qkv, qkv)


def attention_backward_kernel(
    width, seg_k_ref, seg_q_ref, q_ref, k_ref, v_ref, ctx_ref, lse_ref, d_ref, out_ref, dk_ref, dv_ref
):
    step = pl.program_id(0)
    block = q_ref.shape[0]
    lane = lax.broadcasted_iota(jnp.int32, (1, LANES), 1)

    @pl.when(step == 0)
    def _():
        dk_ref[...] = jnp.zeros_like(dk_ref)
        dv_ref[...] = jnp.zeros_like(dv_ref)

    bias = jnp.where(seg_k_ref[...] == seg_q_ref[...], 0.0, -1000000000.0)
    for pair in range(width // LANES):
        cols = slice(pair * LANES, (pair + 1) * LANES)
        q2 = q_ref[:, cols] * jnp.asarray(0.125, BF16)
        k2 = k_ref[:, cols]
        v2 = v_ref[:, cols]
        d2 = d_ref[:, cols]
        prod = (d2.astype(F32) * ctx_ref[:, cols].astype(F32)).T
        kt = (k2 * jnp.asarray(0.125, BF16)).T
        row = lax.broadcasted_iota(jnp.int32, (LANES, 1), 0)
        dq = None
        dk = None
        dv = None
        for half in range(2):
            mine = (lane // HD) == half
            qm = jnp.where(mine, q2, jnp.zeros_like(q2))
            dm = jnp.where(mine, d2, jnp.zeros_like(d2))
            ktm = jnp.where((row // HD) == half, kt, jnp.zeros_like(kt))
            inner = jnp.sum(prod[half * HD : (half + 1) * HD, :], axis=0, keepdims=True)
            head = 2 * pair + half
            lse = lse_ref[head : head + 1, :]
            p = jnp.exp(dot_nt(k2, qm) + bias - lse)
            dp = dot_nt(v2, dm)
            ds = (p * (dp - inner)).astype(BF16)
            dv_h = dot_nn(p.astype(BF16), dm)
            dk_h = dot_nn(ds, qm)
            dq_h = dot_nn(ktm, ds)
            dv = dv_h if dv is None else dv + dv_h
            dk = dk_h if dk is None else dk + dk_h
            dq = dq_h if dq is None else dq + dq_h
        dk_ref[:, cols] += dk
        dv_ref[:, cols] += dv
        out_ref[pl.ds(pl.multiple_of(step * block, block), block), cols] = dq.T.astype(BF16)

    @pl.when(step == pl.num_programs(0) - 1)
    def _():
        out_ref[:, width : 2 * width] = dk_ref[...].astype(BF16)
        out_ref[:, 2 * width : 3 * width] = dv_ref[...].astype(BF16)


def attention_backward(qkv, ctx, lse, d_ctx, seg_col, seg_row, block):
    rows, triple = qkv.shape
    width = triple // 3
    return pl.pallas_call(
        functools.partial(attention_backward_kernel, width),
        grid=(rows // block,),
        in_specs=[
            pl.BlockSpec((rows, 1), lambda i: (0, 0)),
            pl.BlockSpec((1, block), lambda i: (0, i)),
            pl.BlockSpec((block, width), lambda i: (i, 0)),
            pl.BlockSpec((rows, width), lambda i: (0, 1)),
            pl.BlockSpec((rows, width), lambda i: (0, 2)),
            pl.BlockSpec((block, width), lambda i: (i, 0)),
            pl.BlockSpec((8, block), lambda i: (0, i)),
            pl.BlockSpec((block, width), lambda i: (i, 0)),
        ],
        out_specs=pl.BlockSpec((rows, triple), lambda i: (0, 0)),
        out_shape=jax.ShapeDtypeStruct((rows, triple), BF16),
        scratch_shapes=[pltpu.VMEM((rows, width), F32), pltpu.VMEM((rows, width), F32)],
        cost_estimate=pl.CostEstimate(
            flops=10 * rows * rows * width * 4,
            bytes_accessed=16 * rows * width,
            transcendentals=rows * rows * width // HD,
        ),
        name="attention_backward",
    )(seg_col, seg_row, qkv, qkv, qkv, ctx, lse, d_ctx)


def normalize(r):
    mean = jnp.mean(r, axis=-1, keepdims=True)
    cent = r - mean
    var = jnp.mean(cent * cent, axis=-1, keepdims=True)
    inv = lax.rsqrt(var + EPSILON)
    return cent * inv, inv


def normalize_back(hat, inv, gain, d_out):
    d_hat = d_out * gain
    first = jnp.mean(d_hat, axis=-1, keepdims=True)
    second = jnp.mean(d_hat * hat, axis=-1, keepdims=True)
    return inv * (d_hat - first - hat * second)


def swap(a):
    return lax.ppermute(a, "c", [(0, 1), (1, 0)])


def pair_gather(a):
    return jnp.concatenate([a, swap(a)], axis=0)


def pair_sum(full, rows):
    return full[:rows] + swap(full[rows:].astype(BF16)).astype(F32)


def flip(a, axis, bit):
    n = lax.axis_size(axis)
    return lax.ppermute(a, axis, [(i, i ^ bit) for i in range(n)])


def double(a, axis, bit):
    return jnp.concatenate([a, flip(a, axis, bit)], axis=0)


def outer_bits(ndp):
    return [1 << k for k in range(1, ndp.bit_length() - 1)]


def gather_outer(a):
    a = a[None]
    for bit in outer_bits(lax.axis_size("dp")):
        a = double(a, "dp", bit)
    return a


def gather_x_then_inner(a):
    a = double(a, "x", 1)
    return a, flip(a, "dp", 1)


def gather_inner_then_x(a):
    a = double(a, "dp", 1)
    return a, flip(a, "x", 1)


def pick(a, index, axis):
    return lax.dynamic_index_in_dim(a, index, axis, keepdims=False)


def add(a, b):
    return (a.astype(F32) + b.astype(F32)).astype(BF16)


def scatter_outer(a):
    dp = lax.axis_index("dp")
    bits = outer_bits(lax.axis_size("dp"))
    for k, bit in reversed(list(enumerate(bits))):
        half = a.shape[0] // 2
        a = a.reshape(2, half, *a.shape[1:])
        mine = (dp >> (k + 1)) & 1
        sent = flip(pick(a, 1 - mine, 0), "dp", bit)
        kept = pick(a, mine, 0)
        a = add(kept, sent) if k else kept.astype(F32) + sent.astype(F32)
    return a[0]


def scatter_x_then_inner(own, other):
    dp = lax.axis_index("dp")
    a = add(own, flip(other, "x", 1))
    return add(pick(a, dp & 1, 1), flip(pick(a, 1 - (dp & 1), 1), "dp", 1))


def scatter_inner_then_x(own, other):
    dp = lax.axis_index("dp")
    a = jnp.stack([own, other])
    a = add(pick(a, dp & 1, 2), flip(pick(a, 1 - (dp & 1), 2), "dp", 1))
    return add(a[0], flip(a[1], "x", 1))


def unit_places(count, x_major):
    half = count // 2
    nz = half // 2
    places = []
    for j in range(count):
        late, early, z = j // half, (j % half) // nz, j % nz
        rx, ry = (early, late) if x_major else (late, early)
        places.append((2 * z + ry, rx))
    return places


def place_kernel(moves, out_count, dp_ref, *refs):
    ins, outs = refs[:-out_count], refs[-out_count:]
    dp = dp_ref[0]
    for source, unit, rel, kind, rows_from, rows, cols_from, cols, target, col in moves:
        value = ins[source][unit, rows_from : rows_from + rows, cols_from : cols_from + cols]
        at = jnp.bitwise_xor(dp, rel)
        if kind == "unit":
            outs[target][at, :, col : col + cols] = value
        else:
            outs[target][pl.ds(pl.multiple_of(at * rows, 16), rows), col : col + cols] = value


def place(pieces, moves, outs):
    dp = lax.axis_index("dp").astype(jnp.int32)
    ndp = lax.axis_size("dp")
    rows = min(m[5] for m in moves if m[3] == "rows")
    if rows % 16 == 0:
        whole = lambda s: pl.BlockSpec(s, lambda i, d: (0,) * len(s))
        return pl.pallas_call(
            functools.partial(place_kernel, moves, len(outs)),
            grid_spec=pltpu.PrefetchScalarGridSpec(
                num_scalar_prefetch=1,
                grid=(1,),
                in_specs=[whole(p.shape) for p in pieces],
                out_specs=[whole(s) for s in outs],
            ),
            out_shape=[jax.ShapeDtypeStruct(s, BF16) for s in outs],
            cost_estimate=pl.CostEstimate(flops=0, bytes_accessed=sum(2 * p.size * 2 for p in pieces), transcendentals=0),
            name="place_units",
        )(dp[None], *pieces)
    made = []
    for target, shape in enumerate(outs):
        mine = [m for m in moves if m[8] == target]
        columns = []
        for col in sorted({m[9] for m in mine}):
            units = sorted((m for m in mine if m[9] == col), key=lambda m: m[2])
            stack = jnp.stack([pieces[m[0]][m[1], m[4] : m[4] + m[5], m[6] : m[6] + m[7]] for m in units])
            stack = jnp.take(stack, jnp.bitwise_xor(jnp.arange(ndp), dp), axis=0)
            columns.append(stack if mine[0][3] == "unit" else stack.reshape(-1, stack.shape[-1]))
        made.append(jnp.concatenate(columns, axis=-1))
    return made


def place_wide(pieces, x_major, rows, cols, nx):
    per = pieces[0].shape[0]
    moves = []
    for j, (rel, rx) in enumerate(unit_places(2 * per, x_major)):
        moves.append((j // per, j % per, rel, "rows", 0, rows, 0, cols, 0, rx * cols))
    return place(pieces, moves, [(rows * lax.axis_size("dp"), nx * cols)])[0]


def place_attention(first, second, rows, part, nx):
    ndp = lax.axis_size("dp")
    extra = first[0].shape[1] - rows
    per = first[0].shape[0]
    width = nx * part
    moves = []
    for j, (rel, rx) in enumerate(unit_places(2 * per, True)):
        s, u = j // per, j % per
        moves.append((s, u, rel, "rows", 0, rows, 0, part, 0, rx * part))
        moves.append((s, u, rel, "rows", 0, rows, part, part, 0, width + rx * part))
        moves.append((s, u, rel, "unit", rows, extra, 0, 2 * part, 2, rx * 2 * part))
    for j, (rel, rx) in enumerate(unit_places(2 * per, False)):
        s, u = 2 + j // per, j % per
        moves.append((s, u, rel, "rows", 0, rows, 0, part, 0, 2 * width + rx * part))
        moves.append((s, u, rel, "rows", 0, rows, part, part, 1, rx * part))
    outs = [(rows * ndp, 3 * width), (rows * ndp, width), (ndp, extra, nx * 2 * part)]
    return place([*first, *second], moves, outs)


def local(
    tokens, grad_out, seg_ids, w_qkv, b_qv, w_out, w_up, b_up, w_down, b_out, b_down, g_one, s_one, g_two, s_two
):
    ndp = lax.axis_size("dp")
    nx = lax.axis_size("x")
    parity = lax.axis_index("c")
    which = lax.axis_index("x")
    rows, model = tokens.shape
    piece = model // ndp
    part = w_qkv.shape[2]
    width = nx * part

    seg = lax.dynamic_index_in_dim(seg_ids, which, 0, keepdims=False)
    seg_two = seg.reshape(2, rows)
    seg_rel = jnp.concatenate(
        [
            lax.dynamic_index_in_dim(seg_two, parity, 0, keepdims=False),
            lax.dynamic_index_in_dim(seg_two, 1 - parity, 0, keepdims=False),
        ]
    )
    seg_col = seg_rel[:, None]
    seg_row = seg_rel[None, :]

    slim = model // (ndp * nx * 2)
    qv = part // ndp
    extra = 8
    small = jnp.concatenate(
        [b_out, b_down, g_one, s_one, g_two, s_two, b_qv.reshape(-1).astype(F32), b_up.astype(F32)]
    )
    high = small.astype(BF16)
    middle = (small - high.astype(F32)).astype(BF16)
    low = (small - high.astype(F32) - middle.astype(F32)).astype(BF16)
    thirds = jnp.pad(jnp.stack([high, middle, low]), ((0, extra - 3), (0, 2 * part - small.shape[0])))
    unit_qk = jnp.concatenate([jnp.concatenate([w_qkv[0], w_qkv[1]], axis=1), thirds], axis=0)
    unit_vo = jnp.concatenate(
        [jnp.concatenate([w_qkv[2], w_out.T], axis=1), jnp.zeros((extra, 2 * part), BF16)], axis=0
    )
    units = gather_outer(jnp.stack([unit_qk, unit_vo]))
    qk_pieces = gather_x_then_inner(units[:, 0])
    vo_pieces = gather_inner_then_x(units[:, 1])
    w_all, o_t, ext = place_attention(qk_pieces, vo_pieces, piece, part, nx)
    units = gather_outer(jnp.stack([w_up, w_down.T]))
    b_all = place_wide(gather_x_then_inner(units[:, 0]), True, piece, model, nx)
    c_all = place_wide(gather_inner_then_x(units[:, 1]), False, piece, model, nx)

    ext = ext.astype(F32)
    ext = (ext[:, 0] + ext[:, 1] + ext[:, 2]).reshape(ndp, nx, 2 * part)
    six = ext[:, :, : 6 * slim]
    six = jnp.stack([six, swap(six)], axis=2)
    six = jnp.where(lax.broadcasted_iota(jnp.int32, (1, 1, 2, 1), 2) == parity, six[:, :, :1], six[:, :, 1:])
    six = jnp.where(which == 0, six, six[:, ::-1]).reshape(ndp * nx * 2, 6, slim)
    vectors = jnp.transpose(six, (1, 0, 2)).reshape(6, model)
    bout_f, bdown_f, gone_f, sone_f, gtwo_f, stwo_f = [vectors[i : i + 1] for i in range(6)]
    wide = ext[:, :, 6 * slim : 6 * slim + 2 * qv + piece]
    bias_qv = jnp.transpose(wide[:, :, : 2 * qv].reshape(ndp, nx, 2, qv), (2, 1, 0, 3)).reshape(2, width)
    bias_qkv = jnp.concatenate([bias_qv[0], jnp.zeros((width,), F32), bias_qv[1]])[None]
    bias_up = jnp.transpose(wide[:, :, 2 * qv :], (1, 0, 2)).reshape(1, nx * model)

    x_own = tokens
    x_full = pair_gather(x_own)
    qkv = (dot_nn(x_full, w_all) + bias_qkv).astype(BF16)
    block = 256
    ctx, lse = attention_forward(qkv, seg_col, seg_row, block)
    attn = pair_sum(dot_nt(ctx, o_t), rows)
    first = x_own.astype(F32) + attn + bout_f
    hat_one, inv_one = normalize(first)
    normed = hat_one * gone_f + sone_f
    normed_full = pair_gather(normed.astype(BF16))
    up = dot_nn(normed_full, b_all) + bias_up
    cdf = 0.5 * (1.0 + lax.erf(up * ROOT_HALF))
    hidden = (up * cdf).astype(BF16)
    slope = (cdf + up * (jnp.exp(-0.5 * up * up) * INV_ROOT_TWO_PI)).astype(BF16)
    branch = pair_sum(dot_nt(hidden, c_all), rows)
    second = normed + branch + bdown_f
    hat_two, inv_two = normalize(second)
    layer_out = (hat_two * gtwo_f + stwo_f).astype(BF16)

    g_in = grad_out.astype(F32)
    d_gain_two = jnp.sum(g_in * hat_two, axis=0)
    d_shift_two = jnp.sum(g_in, axis=0)
    d_second = normalize_back(hat_two, inv_two, gtwo_f, g_in)
    d_branch = d_second.astype(BF16)
    d_bias_down = jnp.sum(d_branch.astype(F32), axis=0)
    db_full = pair_gather(d_branch)
    grad_c = dot_tn(db_full, hidden).astype(BF16)
    d_hidden = dot_nn(db_full, c_all)
    d_up = (d_hidden * slope.astype(F32)).astype(BF16)
    d_bias_up = jnp.sum(d_up.astype(F32), axis=0)
    grad_b = dot_tn(normed_full, d_up).astype(BF16)
    d_normed = d_second + pair_sum(dot_nt(d_up, b_all), rows)
    d_gain_one = jnp.sum(d_normed * hat_one, axis=0)
    d_shift_one = jnp.sum(d_normed, axis=0)
    d_first = normalize_back(hat_one, inv_one, gone_f, d_normed)
    d_attn = d_first.astype(BF16)
    d_bias_out = jnp.sum(d_attn.astype(F32), axis=0)
    da_full = pair_gather(d_attn)
    grad_o = dot_tn(da_full, ctx).astype(BF16)
    d_ctx = dot_nn(da_full, o_t).astype(BF16)
    d_qkv = attention_backward(qkv, ctx, lse, d_ctx, seg_col, seg_row, block)
    d_bias_qkv = jnp.sum(d_qkv.astype(F32), axis=0)
    grad_w = dot_tn(x_full, d_qkv).astype(BF16)
    input_grad = (d_first + pair_sum(dot_nt(d_qkv, w_all), rows)).astype(BF16)

    split = lambda g, i: g[:, i * model : (i + 1) * model].reshape(ndp // 2, 2, piece, model)
    got_c = scatter_x_then_inner(split(grad_c, 0), split(grad_c, 1))
    got_b = scatter_inner_then_x(split(grad_b, 0), split(grad_b, 1))
    got = scatter_outer(jnp.stack([got_c, got_b], axis=1))
    gc, gb = got[0], got[1]

    sums = jnp.stack([d_bias_out, d_bias_down, d_gain_one, d_shift_one, d_gain_two, d_shift_two])
    sums = sums + swap(sums)
    sums = jnp.transpose(sums.reshape(6, ndp, nx, 2, slim), (3, 2, 1, 0, 4))
    sums = pick(sums, parity, 0).reshape(nx, ndp, 6 * slim)
    sums = jnp.where(which == 0, sums, sums[::-1])
    d_bqv = jnp.stack([d_bias_qkv[:width], d_bias_qkv[2 * width :]]).reshape(2, nx, ndp, qv)
    d_bqv = jnp.transpose(d_bqv, (1, 2, 0, 3)).reshape(nx, ndp, 2 * qv)
    d_bup = d_bias_up.reshape(nx, ndp, piece)
    packed = jnp.concatenate([sums, d_bqv, d_bup], axis=-1).astype(BF16)
    packed = jnp.pad(packed[:, :, None], ((0, 0), (0, 0), (0, extra - 1), (0, 2 * part - packed.shape[-1])))

    def columns(g, j, i):
        return g[:, j * width + i * part : j * width + (i + 1) * part]

    def attention_unit(left, right, tail):
        g = jnp.concatenate([left, right], axis=1).reshape(ndp, piece, 2 * part)
        g = jnp.concatenate([g, tail], axis=1)
        return g.reshape(ndp // 2, 2, piece + extra, 2 * part)

    got_qk = scatter_x_then_inner(
        *[attention_unit(columns(grad_w, 0, i), columns(grad_w, 1, i), packed[i]) for i in range(nx)]
    )
    got_vo = scatter_inner_then_x(
        *[attention_unit(columns(grad_w, 2, i), columns(grad_o, 0, i), jnp.zeros_like(packed[i])) for i in range(nx)]
    )
    got = scatter_outer(jnp.stack([got_qk, got_vo], axis=1))
    g_qkv = jnp.stack([got[0, :piece, :part], got[0, :piece, part:], got[1, :piece, :part]])
    g_out = got[1, :piece, part:].T
    mine = got[0, piece]
    six = [mine[i * slim : (i + 1) * slim] for i in range(6)]
    g_bqv = mine[6 * slim : 6 * slim + 2 * qv].reshape(2, qv)
    g_bup = mine[6 * slim + 2 * qv : 6 * slim + 2 * qv + piece]
    return (layer_out, input_grad, g_qkv, g_bqv, g_out, gb, g_bup, gc.T, *six)


def solution(mesh):
    ndp, nt = mesh.devices.shape
    fine = Mesh(mesh.devices.reshape(ndp, nt // 2, 2), ("dp", "x", "c"))
    tensor = ("x", "c")
    every = ("dp", "x", "c")
    row = P(every, None)
    vec = P(every)
    return jax.shard_map(
        local,
        mesh=fine,
        in_specs=(
            row,
            row,
            P("dp", None),
            P(None, "dp", tensor),
            P(None, ("x", "c", "dp")),
            P(tensor, "dp"),
            P("dp", tensor),
            P(("x", "c", "dp")),
            P(tensor, "dp"),
            vec,
            vec,
            vec,
            vec,
            vec,
            vec,
        ),
        out_specs=(
            row,
            row,
            P(None, "dp", tensor),
            P(None, ("x", "c", "dp")),
            P(tensor, "dp"),
            P("dp", tensor),
            P(("x", "c", "dp")),
            P(tensor, "dp"),
            vec,
            vec,
            vec,
            vec,
            vec,
            vec,
        ),
        check_vma=False,
    )
```

```python
import functools

import jax
import jax.numpy as jnp
from jax import lax
from jax.experimental import pallas as pl
from jax.experimental.pallas import tpu as pltpu
from jax.sharding import Mesh, PartitionSpec as P

HD = 64
LANES = 128
EPSILON = 1e-05
ROOT_HALF = 0.7071067811865476
INV_ROOT_TWO_PI = 0.3989422804014327
F32 = jnp.float32
BF16 = jnp.bfloat16


def dot(a, b, dims):
    return lax.dot_general(a, b, (dims, ((), ())), preferred_element_type=F32)


def dot_nn(a, b):
    return dot(a, b, ((1,), (0,)))


def dot_nt(a, b):
    return dot(a, b, ((1,), (1,)))


def dot_tn(a, b):
    return dot(a, b, ((0,), (0,)))


CHEAP = pl.CostEstimate(flops=1000, bytes_accessed=1000, transcendentals=0)


def attention_forward_kernel(width, seg_q_ref, seg_k_ref, q_ref, k_ref, v_ref, *refs):
    ctx_ref, lse_ref = refs[-2:]
    lane = lax.broadcasted_iota(jnp.int32, (1, LANES), 1)
    bias = jnp.where(seg_q_ref[...] == seg_k_ref[...], 0.0, -1000000000.0)
    block = q_ref.shape[0]
    stats = jnp.zeros((block, LANES), F32)
    for tile in range(width // LANES):
        cols = slice(tile * LANES, (tile + 1) * LANES)
        q2 = q_ref[:, cols] * jnp.asarray(0.125, BF16)
        k2 = k_ref[:, cols]
        v2 = v_ref[:, cols]
        outs = []
        for half in range(2):
            qm = jnp.where((lane // HD) == half, q2, jnp.zeros_like(q2))
            s = dot_nt(qm, k2) + bias
            top = jnp.max(s, axis=-1, keepdims=True)
            e = jnp.exp(s - top)
            total = jnp.sum(e, axis=-1, keepdims=True)
            outs.append(dot_nn(e.astype(BF16), v2) * (1.0 / total))
            stats = jnp.where(lane == 2 * tile + half, top + jnp.log(total), stats)
        ctx_ref[:, cols] = jnp.where(lane < HD, outs[0], outs[1]).astype(BF16)
    lse_ref[...] = stats.T[: lse_ref.shape[0], :]


def attention_forward(qkv, seg_col, seg_row, block, first, count, made):
    rows, triple = qkv.shape
    width = triple // 3
    return pl.pallas_call(
        functools.partial(attention_forward_kernel, width),
        grid=(count,),
        in_specs=[
            pl.BlockSpec((block, 1), lambda i: (first + i, 0)),
            pl.BlockSpec((1, rows), lambda i: (0, 0)),
            pl.BlockSpec((block, width), lambda i: (first + i, 0)),
            pl.BlockSpec((rows, width), lambda i: (0, 1)),
            pl.BlockSpec((rows, width), lambda i: (0, 2)),
        ]
        + [pl.BlockSpec(memory_space=pl.ANY)] * len(made),
        out_specs=[
            pl.BlockSpec((block, width), lambda i: (first + i, 0)),
            pl.BlockSpec((8, block), lambda i: (0, first + i)),
        ],
        out_shape=[
            jax.ShapeDtypeStruct((rows, width), BF16),
            jax.ShapeDtypeStruct((8, rows), F32),
        ],
        input_output_aliases={5 + i: i for i in range(len(made))},
        cost_estimate=CHEAP,
        name="attention_forward",
    )(seg_col, seg_row, qkv, qkv, qkv, *made)


def split_specs(block, columns, halves):
    return [
        pl.BlockSpec((block, columns), lambda i, *_: (jnp.minimum(i, halves - 1), 0)),
        pl.BlockSpec((block, columns), lambda i, *_: (jnp.maximum(i - halves, 0), 0)),
    ]


def either(step, halves, own_ref, other_ref):
    return jnp.where(step < halves, own_ref[...], other_ref[...])


def attention_backward_kernel(
    width, halves, seg_k_ref, seg_q_ref, q_ref, k_ref, v_ref, ctx_ref, lse_ref, own_ref, other_ref, out_ref, sum_ref, dk_ref, dv_ref
):
    step = pl.program_id(0)
    block = q_ref.shape[0]
    lane = lax.broadcasted_iota(jnp.int32, (1, LANES), 1)

    @pl.when(step == 0)
    def _():
        dk_ref[...] = jnp.zeros_like(dk_ref)
        dv_ref[...] = jnp.zeros_like(dv_ref)
        sum_ref[...] = jnp.zeros_like(sum_ref)

    bias = jnp.where(seg_k_ref[...] == seg_q_ref[...], 0.0, -1000000000.0)
    for pair in range(width // LANES):
        cols = slice(pair * LANES, (pair + 1) * LANES)
        q2 = q_ref[:, cols] * jnp.asarray(0.125, BF16)
        k2 = k_ref[:, cols]
        v2 = v_ref[:, cols]
        d2 = jnp.where(step < halves, own_ref[:, cols], other_ref[:, cols])
        prod = (d2.astype(F32) * ctx_ref[:, cols].astype(F32)).T
        kt = (k2 * jnp.asarray(0.125, BF16)).T
        row = lax.broadcasted_iota(jnp.int32, (LANES, 1), 0)
        dq = None
        dk = None
        dv = None
        for half in range(2):
            mine = (lane // HD) == half
            qm = jnp.where(mine, q2, jnp.zeros_like(q2))
            dm = jnp.where(mine, d2, jnp.zeros_like(d2))
            ktm = jnp.where((row // HD) == half, kt, jnp.zeros_like(kt))
            inner = jnp.sum(prod[half * HD : (half + 1) * HD, :], axis=0, keepdims=True)
            head = 2 * pair + half
            lse = lse_ref[head : head + 1, :]
            p = jnp.exp(dot_nt(k2, qm) + bias - lse)
            dp = dot_nt(v2, dm)
            ds = (p * (dp - inner)).astype(BF16)
            dv_h = dot_nn(p.astype(BF16), dm)
            dk_h = dot_nn(ds, qm)
            dq_h = dot_nn(ktm, ds)
            dv = dv_h if dv is None else dv + dv_h
            dk = dk_h if dk is None else dk + dk_h
            dq = dq_h if dq is None else dq + dq_h
        dk_ref[:, cols] += dk
        dv_ref[:, cols] += dv
        dq = dq.T.astype(BF16)
        out_ref[pl.ds(pl.multiple_of(step * block, block), block), cols] = dq
        sum_ref[:, cols] += jnp.sum(dq.astype(F32), axis=0, keepdims=True)

    @pl.when(step == pl.num_programs(0) - 1)
    def _():
        out_ref[:, width : 2 * width] = dk_ref[...].astype(BF16)
        dv = dv_ref[...].astype(BF16)
        out_ref[:, 2 * width : 3 * width] = dv
        sum_ref[:, width : 2 * width] = jnp.sum(dv.astype(F32), axis=0, keepdims=True)


def attention_backward(qkv, ctx, lse, d_own, d_other, seg_col, seg_row, block):
    rows, triple = qkv.shape
    width = triple // 3
    halves = rows // block // 2
    return pl.pallas_call(
        functools.partial(attention_backward_kernel, width, halves),
        grid=(rows // block,),
        in_specs=[
            pl.BlockSpec((rows, 1), lambda i: (0, 0)),
            pl.BlockSpec((1, block), lambda i: (0, i)),
            pl.BlockSpec((block, width), lambda i: (i, 0)),
            pl.BlockSpec((rows, width), lambda i: (0, 1)),
            pl.BlockSpec((rows, width), lambda i: (0, 2)),
            pl.BlockSpec((block, width), lambda i: (i, 0)),
            pl.BlockSpec((8, block), lambda i: (0, i)),
            *split_specs(block, width, halves),
        ],
        out_specs=[pl.BlockSpec((rows, triple), lambda i: (0, 0)), pl.BlockSpec((1, 2 * width), lambda i: (0, 0))],
        out_shape=[jax.ShapeDtypeStruct((rows, triple), BF16), jax.ShapeDtypeStruct((1, 2 * width), F32)],
        scratch_shapes=[pltpu.VMEM((rows, width), F32), pltpu.VMEM((rows, width), F32)],
        cost_estimate=CHEAP,
        name="attention_backward",
    )(seg_col, seg_row, qkv, qkv, qkv, ctx, lse, d_own, d_other)


def normalize(r):
    mean = jnp.mean(r, axis=-1, keepdims=True)
    cent = r - mean
    var = jnp.mean(cent * cent, axis=-1, keepdims=True)
    inv = lax.rsqrt(var + EPSILON)
    return cent * inv, inv


def normalize_back(hat, inv, gain, d_out):
    d_hat = d_out * gain
    first = jnp.mean(d_hat, axis=-1, keepdims=True)
    second = jnp.mean(d_hat * hat, axis=-1, keepdims=True)
    return inv * (d_hat - first - hat * second)


def swap(a):
    return lax.ppermute(a, "c", [(0, 1), (1, 0)])


def flip(a, axis, bit):
    n = lax.axis_size(axis)
    return lax.ppermute(a, axis, [(i, i ^ bit) for i in range(n)])


def turn(a, level):
    n, nx = lax.axis_size("dp"), lax.axis_size("x")
    pairs = []
    for d in range(n):
        for x in range(nx):
            for c in range(2):
                other = (d * nx + (x ^ 1)) if (c + level) % 2 == 0 else ((d ^ 1) * nx + x)
                pairs.append(((d * nx + x) * 2 + c, other * 2 + c))
    return lax.ppermute(a, ("dp", "x", "c"), pairs)


def tie(*values):
    return lax.optimization_barrier(values)


def add(*terms):
    return sum(t.astype(F32) for t in terms).astype(BF16)


def outer_bits():
    return lax.axis_size("dp").bit_length() - 2


def gather_far(near):
    parts = [near]
    for k in range(1, outer_bits()):
        held = jnp.concatenate(parts) if len(parts) > 1 else near
        parts.append(flip(held, "dp", 2 << k))
    return jnp.concatenate(parts[1:]) if len(parts) > 2 else parts[1]


class Spread:
    def __init__(self, units, outer):
        self.units, self.outer = units, outer

    def first(self):
        self.one = turn(self.units, 0)

    def second(self):
        self.two = turn(jnp.concatenate([self.units, self.one]), 1)

    def pieces(self):
        n = self.units.shape[0]
        index = [(0, u, self.outer + u, 0, 0) for u in range(n)]
        index += [(1, u, self.outer + u, 1, 0) for u in range(n)]
        index += [(2, a * n + u, self.outer + u, a, 1) for a in range(2) for u in range(n)]
        return [self.units, self.one, self.two], index


def joined(spreads):
    arrays, index = [], []
    for s in spreads:
        more, at = s.pieces()
        index += [(i + len(arrays), *rest) for i, *rest in at]
        arrays += more
    return arrays, index


def put_units(index, moves, where_ref, ins, outs, each=None):
    dp = where_ref[0]
    for parity in range(2):

        @pl.when(where_ref[1] == parity)
        def _():
            for array, unit, outer, first, second in index:
                rx, ry = (second, first) if parity else (first, second)
                to = jnp.bitwise_xor(dp, 2 * outer + ry)
                for lead, rows, col, cols, target, at in moves:
                    value = ins[array][(unit, *lead, slice(0, rows), slice(col, col + cols))]
                    outs[target][pl.ds(pl.multiple_of(to * rows, 16), rows), at[rx] : at[rx] + cols] = value
                if each is not None:
                    each(ins[array], unit, to, rx)


def prepare_kernel(piece, dp_ref, qkv_ref, out_ref, up_ref, down_ref, qv_ref, *refs):
    vectors, (a_ref, bc_ref, row_ref) = refs[:-3], refs[-3:]
    part = qkv_ref.shape[2]
    for j in range(3):
        a_ref[:piece, j * part : (j + 1) * part] = qkv_ref[j]
    a_ref[:piece, 3 * part :] = out_ref[...].T
    row_ref[...] = jnp.zeros_like(row_ref)
    at = 0
    for v in vectors:
        n = v.shape[1]
        row_ref[0:1, at : at + n] = v[...].astype(F32)
        at += n
    n = qv_ref.shape[1]
    lane = lax.broadcasted_iota(jnp.int32, (n, part), 1)
    spot = (lane == lax.broadcasted_iota(jnp.int32, (n, part), 0) + n * dp_ref[0]).astype(BF16)
    both = dot_nn(qv_ref[...], spot)
    row_ref[1:2, :part] = both[0:1]
    row_ref[1:2, part : 2 * part] = both[1:2]
    exact = row_ref[0:1, :]
    high = exact.astype(BF16).astype(F32)
    middle = (exact - high).astype(BF16).astype(F32)
    low = exact - high - middle
    line = lax.broadcasted_iota(jnp.int32, (8, 1), 0)
    rows = jnp.where(line == 0, high, 0.0) + jnp.where(line == 1, middle, 0.0)
    rows += jnp.where(line == 2, low, 0.0) + jnp.where(line == 3, row_ref[1:2, :], 0.0)
    a_ref[piece:, :] = rows.astype(BF16)
    bc_ref[0] = up_ref[...]
    bc_ref[1] = down_ref[...].T


def prepare(w_qkv, w_out, w_up, w_down, b_qv, vectors):
    piece, part = w_qkv.shape[1:]
    model = w_up.shape[1]
    dp = lax.axis_index("dp").astype(jnp.int32)
    if piece % 16 == 0:

        def whole(s):
            return pl.BlockSpec(s, lambda i, d: (0,) * len(s))

        given = [w_qkv, w_out, w_up, w_down, b_qv, *[v[None] for v in vectors]]
        shapes = [(piece + 8, model), (2, piece, model)]
        return pl.pallas_call(
            functools.partial(prepare_kernel, piece),
            grid_spec=pltpu.PrefetchScalarGridSpec(
                num_scalar_prefetch=1,
                grid=(1,),
                in_specs=[whole(v.shape) for v in given],
                out_specs=[whole(s) for s in shapes],
                scratch_shapes=[pltpu.VMEM((8, model), F32)],
            ),
            out_shape=[jax.ShapeDtypeStruct(s, BF16) for s in shapes],
            cost_estimate=CHEAP,
            name="prepare_units",
        )(dp[None], *given)
    row = jnp.concatenate([v.astype(F32) for v in vectors])
    row = jnp.pad(row, (0, model - row.shape[0]))
    high = row.astype(BF16)
    middle = (row - high.astype(F32)).astype(BF16)
    low = (row - high.astype(F32) - middle.astype(F32)).astype(BF16)
    keep = lax.broadcasted_iota(jnp.int32, (1, part // b_qv.shape[1], 1), 1) == dp
    spot = jnp.where(keep, b_qv[:, None, :], jnp.zeros((), BF16)).reshape(-1)
    spot = jnp.pad(spot, (0, model - spot.shape[0]))
    tail = jnp.pad(jnp.stack([high, middle, low, spot]), ((0, 4), (0, 0)))
    unit = jnp.concatenate([w_qkv[0], w_qkv[1], w_qkv[2], w_out.T], axis=1)
    return jnp.concatenate([unit, tail], axis=0), jnp.stack([w_up, w_down.T])


def project_kernel(index, moves, piece, part, halves, where_ref, own_ref, other_ref, *refs):
    ins, (out_ref, w_ref, o_ref, ext_ref, bias_ref) = refs[:-5], refs[-5:]
    width = 2 * part

    @pl.when(pl.program_id(0) == 0)
    def _():
        bias_ref[...] = jnp.zeros_like(bias_ref)

        def each(source, unit, to, rx):
            value = source[unit, piece:, : 2 * part]
            ext_ref[to, :, 2 * part * rx : 2 * part * (rx + 1)] = value
            value = value.astype(F32)[3:4]
            bias_ref[0:1, rx * part : (rx + 1) * part] += value[:, :part]
            at = 2 * width + rx * part
            bias_ref[0:1, at : at + part] += value[:, part:]

        put_units(index, moves, where_ref, ins, (w_ref, o_ref), each)

    x = either(pl.program_id(0), halves, own_ref, other_ref)
    out_ref[...] = (dot_nn(x, w_ref[...]) + bias_ref[0:1, :]).astype(BF16)


def feed_kernel(index, moves, halves, where_ref, own_ref, other_ref, bias_ref, *refs):
    ins, (hidden_ref, slope_ref, keep_ref, send_ref, b_ref, c_ref) = refs[:-6], refs[-6:]
    step = pl.program_id(0)

    @pl.when(step == 0)
    def _():
        put_units(index, moves, where_ref, ins, (b_ref, c_ref))

    up = dot_nn(either(step, halves, own_ref, other_ref), b_ref[...]) + bias_ref[...]
    hidden, slope = gelu_both(up)
    hidden_ref[...] = hidden
    slope_ref[...] = slope
    part = dot_nt(hidden, c_ref[...])

    @pl.when(step < halves)
    def _():
        keep_ref[...] = part

    @pl.when(step >= halves)
    def _():
        send_ref[...] = part.astype(BF16)


def gelu_both(up):
    cdf = 0.5 * (1.0 + lax.erf(up * ROOT_HALF))
    slope = cdf + up * (jnp.exp(-0.5 * up * up) * INV_ROOT_TWO_PI)
    return (up * cdf).astype(BF16), slope.astype(BF16)


def pull_kernel(halves, own_ref, other_ref, slope_ref, c_ref, b_ref, up_ref, keep_ref, send_ref, sum_ref):
    step = pl.program_id(0)
    d = either(step, halves, own_ref, other_ref)
    d_up = (dot_nn(d, c_ref[...]) * slope_ref[...].astype(F32)).astype(BF16)
    up_ref[...] = d_up
    part = dot_nt(d_up, b_ref[...])

    @pl.when(step == 0)
    def _():
        sum_ref[...] = jnp.zeros_like(sum_ref)

    sum_ref[...] += jnp.sum(d_up.astype(F32), axis=0, keepdims=True)

    @pl.when(step < halves)
    def _():
        keep_ref[...] = part

    @pl.when(step >= halves)
    def _():
        send_ref[...] = part.astype(BF16)


def ordered(spreads, moves):
    arrays, index = joined(spreads)
    order = jnp.bitwise_xor(jnp.arange(lax.axis_size("dp")), lax.axis_index("dp"))
    made = {}
    for lead, rows, col, cols, target, at in moves:
        for rx in range(2):
            both = []
            for swapped in range(2):
                units = {}
                for array, unit, outer, first, second in index:
                    x, y = (second, first) if swapped else (first, second)
                    if x == rx:
                        units[2 * outer + y] = arrays[array][(unit, *lead)][rows, col : col + cols]
                both.append(jnp.stack([units[k] for k in sorted(units)]))
            stack = jnp.take(jnp.where(lax.axis_index("c") == 0, both[0], both[1]), order, axis=0)
            made.setdefault(target, []).append((at[rx], stack))
    return [jnp.concatenate([m for _, m in sorted(made[t], key=lambda p: p[0])], axis=-1) for t in sorted(made)]


def project(spreads, own, other, piece, part, block):
    width = 2 * part
    rows, model = own.shape
    halves = rows // block
    moves = [((), piece, j * part, part, 0, (j * width, j * width + part)) for j in range(3)]
    moves.append(((), piece, 3 * part, part, 1, (0, part)))
    if piece % 16 == 0:
        arrays, index = joined(spreads)

        def whole(s):
            return pl.BlockSpec(s, lambda i, d: (0,) * len(s))

        shapes = [(model, 3 * width), (model, width), (model // piece, 8, 2 * width)]
        return pl.pallas_call(
            functools.partial(project_kernel, index, moves, piece, part, halves),
            grid_spec=pltpu.PrefetchScalarGridSpec(
                num_scalar_prefetch=1,
                grid=(2 * halves,),
                in_specs=split_specs(block, model, halves) + [whole(a.shape) for a in arrays],
                out_specs=[pl.BlockSpec((block, 3 * width), lambda i, d: (i, 0))] + [whole(s) for s in shapes],
                scratch_shapes=[pltpu.VMEM((8, 3 * width), F32)],
            ),
            out_shape=[jax.ShapeDtypeStruct(s, BF16) for s in [(2 * rows, 3 * width), *shapes]],
            cost_estimate=CHEAP,
            name="project_kernel",
        )(where(), own, other, *arrays)
    slices = [(lead, slice(0, n), *rest) for lead, n, *rest in moves]
    slices.append(((), slice(piece, piece + 8), 0, 2 * part, 2, (0, 2 * part)))
    w, o, ext = ordered(spreads, slices)
    bias = jnp.sum(ext[:, 3].astype(F32), axis=0).reshape(2, 2, part)
    bias = jnp.concatenate([bias[:, 0].reshape(-1), jnp.zeros((width,), F32), bias[:, 1].reshape(-1)])
    w, o = w.reshape(model, -1), o.reshape(model, -1)
    return (dot_nn(jnp.concatenate([own, other]), w) + bias[None]).astype(BF16), w, o, ext


def feed(spreads, own, other, bias, piece, block):
    rows, model = own.shape
    halves = rows // block
    moves = [((k,), piece, 0, model, k, (0, model)) for k in range(2)]
    if piece % 16 == 0:
        arrays, index = joined(spreads)

        def whole(s):
            return pl.BlockSpec(s, lambda i, d: (0,) * len(s))

        wide = pl.BlockSpec((block, 2 * model), lambda i, d: (i, 0))
        return pl.pallas_call(
            functools.partial(feed_kernel, index, moves, halves),
            grid_spec=pltpu.PrefetchScalarGridSpec(
                num_scalar_prefetch=1,
                grid=(2 * halves,),
                in_specs=split_specs(block, model, halves) + [whole(a.shape) for a in [bias, *arrays]],
                out_specs=[wide, wide, *split_specs(block, model, halves)] + [whole((model, 2 * model))] * 2,
            ),
            out_shape=[jax.ShapeDtypeStruct((2 * rows, 2 * model), BF16)] * 2
            + [jax.ShapeDtypeStruct((rows, model), F32), jax.ShapeDtypeStruct((rows, model), BF16)]
            + [jax.ShapeDtypeStruct((model, 2 * model), BF16)] * 2,
            cost_estimate=CHEAP,
            name="feed_kernel",
        )(where(), own, other, bias, *arrays)
    b, c = ordered(spreads, [(lead, slice(0, n), *rest) for lead, n, *rest in moves])
    b, c = b.reshape(model, -1), c.reshape(model, -1)
    hidden, slope = gelu_both(dot_nn(jnp.concatenate([own, other]), b) + bias)
    part = dot_nt(hidden, c)
    return hidden, slope, part[:rows], part[rows:].astype(BF16), b, c


def pull(own, other, slope, c, b, block):
    rows, model = own.shape
    wide = b.shape[1]
    halves = rows // block

    def whole(s):
        return pl.BlockSpec(s, lambda i: (0, 0))

    by_row = pl.BlockSpec((block, wide), lambda i: (i, 0))
    return pl.pallas_call(
        functools.partial(pull_kernel, halves),
        grid=(2 * halves,),
        in_specs=[*split_specs(block, model, halves), by_row, whole(c.shape), whole(b.shape)],
        out_specs=[by_row, *split_specs(block, model, halves), whole((1, wide))],
        out_shape=[
            jax.ShapeDtypeStruct((2 * rows, wide), BF16),
            jax.ShapeDtypeStruct((rows, model), F32),
            jax.ShapeDtypeStruct((rows, model), BF16),
            jax.ShapeDtypeStruct((1, wide), F32),
        ],
        cost_estimate=CHEAP,
        name="pull_kernel",
    )(own, other, slope, c, b)


def where():
    return jnp.stack([lax.axis_index("dp"), lax.axis_index("c")]).astype(jnp.int32)


def sum_kernel(parts, piece, extra, blocked, where_ref, *refs):
    ins = refs[: -3 - (1 if extra else 0)]
    ext_ref = refs[-4] if extra else None
    outs, acc = refs[-3:-1], refs[-1]
    dp = where_ref[0]
    outer = outs[0].shape[0] // 2

    def one_x(rx):
        for (own, other), right, cols, width, at in parts:
            start = 0 if blocked else cols[rx]
            lanes = slice(start, start + width)
            half = ins[own].shape[0]
            g = dot_tn(ins[own][...], ins[right][:half, lanes]) + dot_tn(ins[other][...], ins[right][half:, lanes])
            acc[:, at : at + width] = g.astype(BF16)
        for parity in range(2):

            @pl.when(where_ref[1] == parity)
            def _():
                for ry in range(2):
                    first, second = (ry, rx) if parity else (rx, ry)

                    def move(z, carry):
                        rows = pl.ds(pl.multiple_of(jnp.bitwise_xor(dp, 2 * z + ry) * piece, 16), piece)
                        outs[first][second * outer + z, :piece, :] = acc[rows, :]
                        if extra:
                            outs[first][second * outer + z, piece:, :] = ext_ref[rx]
                        return carry

                    lax.fori_loop(0, outer, move, 0)

    for rx in range(2):
        pl.when(pl.program_id(0) == rx)(functools.partial(one_x, rx))


def summed(arrays, parts, ext=None):
    ndp = lax.axis_size("dp")
    model = arrays[0].shape[1]
    piece = model // ndp
    width = max(p[4] + p[3] for p in parts)
    extra = 0 if ext is None else ext.shape[1]
    blocked = len(parts) == 1
    if piece % 16 == 0:

        def whole(s):
            return pl.BlockSpec(s, lambda i, d: (0,) * len(s))

        given = list(arrays) + ([] if ext is None else [ext])
        specs = [whole(a.shape) for a in given]
        if blocked:
            right = parts[0][1]
            specs[right] = pl.BlockSpec((arrays[right].shape[0], width), lambda i, d: (0, i))
        shape = (ndp, piece + extra, width)
        return pl.pallas_call(
            functools.partial(sum_kernel, parts, piece, extra, blocked),
            grid_spec=pltpu.PrefetchScalarGridSpec(
                num_scalar_prefetch=1,
                grid=(2,),
                in_specs=specs,
                out_specs=[whole(shape)] * 2,
                scratch_shapes=[pltpu.VMEM((model, width), BF16)],
            ),
            out_shape=[jax.ShapeDtypeStruct(shape, BF16)] * 2,
            cost_estimate=CHEAP,
            name="sum_units",
        )(where(), *given)
    order = jnp.bitwise_xor(jnp.arange(ndp), lax.axis_index("dp"))
    sides = []
    for rx in range(2):
        g = []
        for (own, other), r, c, w, _ in parts:
            left = jnp.concatenate([arrays[own], arrays[other]])
            g.append(dot_tn(left, arrays[r][:, c[rx] : c[rx] + w]).astype(BF16))
        g = jnp.concatenate(g, axis=1).reshape(ndp, piece, width)
        if extra:
            g = jnp.concatenate([g, jnp.broadcast_to(ext[rx][None], (ndp, extra, width))], axis=1)
        g = jnp.take(g, order, axis=0).reshape(ndp // 2, 2, piece + extra, width)
        sides.append(jnp.moveaxis(g, 1, 0))
    g = jnp.stack(sides)
    g = jnp.where(lax.axis_index("c") == 0, g, jnp.swapaxes(g, 0, 1))
    return g[0].reshape(ndp, piece + extra, width), g[1].reshape(ndp, piece + extra, width)


class Scatter:
    def __init__(self, pair):
        self.keep, self.send = pair

    def first(self):
        self.one = turn(self.send, 0)

    def second(self):
        half = self.keep.shape[0] // 2
        self.kept = add(self.keep[:half], self.one[:half])
        self.two = turn(add(self.keep[half:], self.one[half:]), 1)

    def third(self):
        total = add(self.kept, self.two)
        outer = total.shape[0]
        if outer <= 4:
            self.last = [total[0]]
            self.three = [flip(total[k], "dp", 2 * k) for k in range(1, outer)]
            return
        for k in reversed(range(outer_bits())):
            half = total.shape[0] // 2
            total = add(total[:half], flip(total[half:], "dp", 2 << k))
        self.last, self.three = [total[0]], []

    def result(self):
        return sum(t.astype(F32) for t in self.last + self.three)


def local(
    tokens, grad_out, seg_ids, w_qkv, b_qv, w_out, w_up, b_up, w_down, b_out, b_down, g_one, s_one, g_two, s_two
):
    ndp = lax.axis_size("dp")
    nx = lax.axis_size("x")
    parity = lax.axis_index("c")
    which = lax.axis_index("x")
    place_dp = lax.axis_index("dp")
    rows, model = tokens.shape
    piece = model // ndp
    part = w_qkv.shape[2]
    width = nx * part
    slim = model // (ndp * nx * 2)
    qv = part // ndp
    extra = 8
    block = 256

    unit_a, unit_bc = prepare(
        w_qkv, w_out, w_up, w_down, b_qv, [b_out, b_down, g_one, s_one, g_two, s_two, b_up]
    )
    a_near = Spread(jnp.stack([unit_a, flip(unit_a, "dp", 2)]), 0)
    bc_near = Spread(jnp.stack([unit_bc, flip(unit_bc, "dp", 2)]), 0)
    a_far = Spread(gather_far(a_near.units), 2)
    a_near.first()
    a_near.second()
    bc_near.first()
    a_far.units, bc_near.units = tie(a_far.units, bc_near.units)
    bc_far = Spread(gather_far(bc_near.units), 2)
    a_far.first()
    a_far.second()
    bc_near.second()

    seg = lax.dynamic_index_in_dim(seg_ids, which, 0, keepdims=False).reshape(2, rows)
    seg_rel = jnp.concatenate(
        [
            lax.dynamic_index_in_dim(seg, parity, 0, keepdims=False),
            lax.dynamic_index_in_dim(seg, 1 - parity, 0, keepdims=False),
        ]
    )
    seg_col = seg_rel[:, None]
    seg_row = seg_rel[None, :]
    x_other = swap(tokens)

    qkv, w_all, o_t, ext = project([a_near, a_far], tokens, x_other, piece, part, block)
    ext = ext[:, :3].astype(F32)
    ext = (ext[:, 0] + ext[:, 1] + ext[:, 2]).reshape(ndp, nx, 2 * part)
    bias_up = jnp.transpose(ext[:, :, 6 * slim : 6 * slim + piece], (1, 0, 2)).reshape(1, nx * model)
    six = ext[:, :, : 6 * slim]
    six = jnp.stack([six, swap(six)], axis=2)
    six = jnp.where(lax.broadcasted_iota(jnp.int32, (1, 1, 2, 1), 2) == parity, six[:, :, :1], six[:, :, 1:])
    six = jnp.where(which == 0, six, six[:, ::-1]).reshape(ndp * nx * 2, 6, slim)
    vectors = jnp.transpose(six, (1, 0, 2)).reshape(6, model)
    bout_f, bdown_f, gone_f, sone_f, gtwo_f, stwo_f = [vectors[i : i + 1] for i in range(6)]

    qkv, bc_far.units = tie(qkv, bc_far.units)
    bc_far.first()
    steps = rows // block
    made = attention_forward(qkv, seg_col, seg_row, block, steps, steps, ())
    *made, bc_far.one, bc_near.two = tie(*made, bc_far.one, bc_near.two)
    bc_far.second()
    attn_send = dot_nt(made[0][rows:], o_t).astype(BF16)
    ctx, lse = attention_forward(qkv, seg_col, seg_row, block, 0, steps, made)
    attn_send, ctx = tie(attn_send, ctx)
    attn = dot_nt(ctx[:rows], o_t) + swap(attn_send).astype(F32)
    first = tokens.astype(F32) + attn + bout_f
    hat_one, inv_one = normalize(first)
    normed = hat_one * gone_f + sone_f
    normed_low, bc_far.two = tie(normed.astype(BF16), bc_far.two)
    normed_other = swap(normed_low)
    hidden, slope, keep, send, b_all, c_all = feed([bc_near, bc_far], normed_low, normed_other, bias_up, piece, block)
    branch = keep + swap(send).astype(F32)
    second = normed + branch + bdown_f
    hat_two, inv_two = normalize(second)
    layer_out = (hat_two * gtwo_f + stwo_f).astype(BF16)

    g_in = grad_out.astype(F32)
    d_gain_two = jnp.sum(g_in * hat_two, axis=0)
    d_shift_two = jnp.sum(g_in, axis=0)
    d_second = normalize_back(hat_two, inv_two, gtwo_f, g_in)
    d_branch = d_second.astype(BF16)
    d_bias_down = jnp.sum(d_branch.astype(F32), axis=0)
    db_other = swap(d_branch)

    wide_part = [((0, 1), 2, (0, model), model, 0)]
    sc = Scatter(summed([d_branch, db_other, hidden], wide_part))
    sc.first()
    d_up, keep, send, d_bias_up = pull(d_branch, db_other, slope, c_all, b_all, block)
    sc.one, send, d_up = tie(sc.one, send, d_up)
    sc.second()
    sb = Scatter(summed([normed_low, normed_other, d_up], wide_part))
    d_normed = d_second + keep + swap(send).astype(F32)
    sc.two, sb.send, d_normed = tie(sc.two, sb.send, d_normed)
    sc.third()
    sb.first()
    d_gain_one = jnp.sum(d_normed * hat_one, axis=0)
    d_shift_one = jnp.sum(d_normed, axis=0)
    d_first = normalize_back(hat_one, inv_one, gone_f, d_normed)
    d_attn = d_first.astype(BF16)
    d_bias_out = jnp.sum(d_attn.astype(F32), axis=0)
    da_other = swap(d_attn)
    d_ctx = dot_nn(d_attn, o_t).astype(BF16)
    d_ctx_other = dot_nn(da_other, o_t).astype(BF16)
    sums = jnp.stack([d_bias_out, d_bias_down, d_gain_one, d_shift_one, d_gain_two, d_shift_two])
    sums = sums + swap(sums)
    d_ctx_other, sb.one, sums = tie(d_ctx_other, sb.one, sums)
    sb.second()
    d_qkv, bias = attention_backward(qkv, ctx, lse, d_ctx, d_ctx_other, seg_col, seg_row, block)
    d_qkv, sb.two, *sc.three = tie(d_qkv, sb.two, *sc.three)
    sb.third()
    bias = bias.reshape(2, nx, part)
    bias = jnp.concatenate([bias[0], bias[1], jnp.zeros((nx, model - 2 * part), F32)], axis=1)
    tail = jnp.concatenate(
        [bias[:, None], d_bias_up.reshape(nx, 1, model), jnp.broadcast_to(sums[None], (nx, 6, model))], axis=1
    ).astype(BF16)
    attention_parts = [((0, 1), 2, (j * width, j * width + part), part, j * part) for j in range(3)]
    attention_parts.append(((3, 4), 5, (0, part), part, 3 * part))
    sa = Scatter(summed([tokens, x_other, d_qkv, d_attn, da_other, ctx], attention_parts, tail))
    d_qkv, sa.send = tie(d_qkv, sa.send)
    sa.first()
    send = dot_nt(d_qkv[rows:], w_all).astype(BF16)
    keep = d_first + dot_nt(d_qkv[:rows], w_all)
    sa.one, keep, send, *sb.three = tie(sa.one, keep, send, *sb.three)
    sa.second()
    input_grad = keep + swap(send).astype(F32)
    sa.two, input_grad = tie(sa.two, input_grad)
    sa.third()
    input_grad = input_grad.astype(BF16)
    gc = sc.result()
    gb = sb.result()
    ga = sa.result()
    g_qkv = jnp.stack([ga[:piece, j * part : (j + 1) * part] for j in range(3)])
    tail = ga[piece:]
    g_bqv = lax.dynamic_slice_in_dim(tail[0, : 2 * part].reshape(2, part), place_dp * qv, qv, axis=1)
    g_bup = lax.dynamic_slice_in_dim(tail[1], place_dp * piece, piece)
    six = lax.dynamic_slice_in_dim(tail[2:], ((place_dp * nx + which) * 2 + parity) * slim, slim, axis=1)
    return (
        layer_out,
        input_grad,
        g_qkv,
        g_bqv,
        ga[:piece, 3 * part :].T,
        gb,
        g_bup,
        gc.T,
        *[six[i] for i in range(6)],
    )


def solution(mesh):
    ndp, nt = mesh.devices.shape
    fine = Mesh(mesh.devices.reshape(ndp, nt // 2, 2), ("dp", "x", "c"))
    tensor = ("x", "c")
    every = ("dp", "x", "c")
    row = P(every, None)
    vec = P(every)
    return jax.shard_map(
        local,
        mesh=fine,
        in_specs=(
            row,
            row,
            P("dp", None),
            P(None, "dp", tensor),
            P(None, ("x", "c", "dp")),
            P(tensor, "dp"),
            P("dp", tensor),
            P(("x", "c", "dp")),
            P(tensor, "dp"),
            vec,
            vec,
            vec,
            vec,
            vec,
            vec,
        ),
        out_specs=(
            row,
            row,
            P(None, "dp", tensor),
            P(None, ("x", "c", "dp")),
            P(tensor, "dp"),
            P("dp", tensor),
            P(("x", "c", "dp")),
            P(tensor, "dp"),
            vec,
            vec,
            vec,
            vec,
            vec,
            vec,
        ),
        check_vma=False,
    )
```

```python
import functools

import jax
import jax.numpy as jnp
from jax import lax
from jax.experimental import pallas as pl
from jax.experimental.pallas import tpu as pltpu
from jax.sharding import Mesh, PartitionSpec as P

HD = 64
LANES = 128
EPSILON = 1e-05
ROOT_HALF = 0.7071067811865476
INV_ROOT_TWO_PI = 0.3989422804014327
F32 = jnp.float32
BF16 = jnp.bfloat16


def dot(a, b, dims):
    return lax.dot_general(a, b, (dims, ((), ())), preferred_element_type=F32)


def dot_nn(a, b):
    return dot(a, b, ((1,), (0,)))


def dot_nt(a, b):
    return dot(a, b, ((1,), (1,)))


def dot_tn(a, b):
    return dot(a, b, ((0,), (0,)))


CHEAP = pl.CostEstimate(flops=1000, bytes_accessed=1000, transcendentals=0)


def attention_forward_kernel(width, seg_q_ref, seg_k_ref, q_ref, k_ref, v_ref, *refs):
    ctx_ref, lse_ref = refs[-2:]
    lane = lax.broadcasted_iota(jnp.int32, (1, LANES), 1)
    bias = jnp.where(seg_q_ref[...] == seg_k_ref[...], 0.0, -1000000000.0)
    block = q_ref.shape[0]

    stats = jnp.zeros((block, LANES), F32)
    for tile in range(width // LANES):
        cols = slice(tile * LANES, (tile + 1) * LANES)
        q2 = q_ref[:, cols] * jnp.asarray(0.125, BF16)
        k2 = k_ref[:, cols]
        v2 = v_ref[:, cols]
        outs = []
        for half in range(2):
            qm = jnp.where((lane // HD) == half, q2, jnp.zeros_like(q2))
            s = dot_nt(qm, k2) + bias
            top = jnp.max(s, axis=-1, keepdims=True)
            e = jnp.exp(s - top)
            total = jnp.sum(e, axis=-1, keepdims=True)
            outs.append(dot_nn(e.astype(BF16), v2) * (1.0 / total))
            stats = jnp.where(lane == 2 * tile + half, top + jnp.log(total), stats)
        ctx_ref[:, cols] = jnp.where(lane < HD, outs[0], outs[1]).astype(BF16)
    lse_ref[...] = stats.T[: lse_ref.shape[0], :]


def attention_forward(qkv, seg_col, seg_row, block, first, count, made):
    rows, triple = qkv.shape
    width = triple // 3
    return pl.pallas_call(
        functools.partial(attention_forward_kernel, width),
        grid=(count,),
        in_specs=[
            pl.BlockSpec((block, 1), lambda i: (first + i, 0)),
            pl.BlockSpec((1, rows), lambda i: (0, 0)),
            pl.BlockSpec((block, width), lambda i: (first + i, 0)),
            pl.BlockSpec((rows, width), lambda i: (0, 1)),
            pl.BlockSpec((rows, width), lambda i: (0, 2)),
        ]
        + [pl.BlockSpec(memory_space=pl.ANY)] * len(made),
        out_specs=[
            pl.BlockSpec((block, width), lambda i: (first + i, 0)),
            pl.BlockSpec((8, block), lambda i: (0, first + i)),
        ],
        out_shape=[
            jax.ShapeDtypeStruct((rows, width), BF16),
            jax.ShapeDtypeStruct((8, rows), F32),
        ],
        input_output_aliases={5 + i: i for i in range(len(made))},
        cost_estimate=CHEAP,
        name="attention_forward",
    )(seg_col, seg_row, qkv, qkv, qkv, *made)


def split_specs(block, columns, halves):
    return [
        pl.BlockSpec((block, columns), lambda i, *_: (jnp.minimum(i, halves - 1), 0)),
        pl.BlockSpec((block, columns), lambda i, *_: (jnp.maximum(i - halves, 0), 0)),
    ]


def either(step, halves, own_ref, other_ref):
    return jnp.where(step < halves, own_ref[...], other_ref[...])


def attention_backward_kernel(
    width, halves, seg_k_ref, seg_q_ref, q_ref, k_ref, v_ref, ctx_ref, lse_ref, own_ref, other_ref, out_ref, sum_ref, dk_ref, dv_ref
):
    step = pl.program_id(0)
    block = q_ref.shape[0]
    lane = lax.broadcasted_iota(jnp.int32, (1, LANES), 1)

    @pl.when(step == 0)
    def _():
        dk_ref[...] = jnp.zeros_like(dk_ref)
        dv_ref[...] = jnp.zeros_like(dv_ref)
        sum_ref[...] = jnp.zeros_like(sum_ref)

    bias = jnp.where(seg_k_ref[...] == seg_q_ref[...], 0.0, -1000000000.0)
    for pair in range(width // LANES):
        cols = slice(pair * LANES, (pair + 1) * LANES)
        q2 = q_ref[:, cols] * jnp.asarray(0.125, BF16)
        k2 = k_ref[:, cols]
        v2 = v_ref[:, cols]
        d2 = jnp.where(step < halves, own_ref[:, cols], other_ref[:, cols])
        prod = (d2.astype(F32) * ctx_ref[:, cols].astype(F32)).T
        kt = (k2 * jnp.asarray(0.125, BF16)).T
        row = lax.broadcasted_iota(jnp.int32, (LANES, 1), 0)
        dq = None
        dk = None
        dv = None
        for half in range(2):
            mine = (lane // HD) == half
            qm = jnp.where(mine, q2, jnp.zeros_like(q2))
            dm = jnp.where(mine, d2, jnp.zeros_like(d2))
            ktm = jnp.where((row // HD) == half, kt, jnp.zeros_like(kt))
            inner = jnp.sum(prod[half * HD : (half + 1) * HD, :], axis=0, keepdims=True)
            lse = lse_ref[2 * pair + half : 2 * pair + half + 1, :]
            p = jnp.exp(dot_nt(k2, qm) + bias - lse)
            dp = dot_nt(v2, dm)
            ds = (p * (dp - inner)).astype(BF16)
            dv_h = dot_nn(p.astype(BF16), dm)
            dk_h = dot_nn(ds, qm)
            dq_h = dot_nn(ktm, ds)
            dv = dv_h if dv is None else dv + dv_h
            dk = dk_h if dk is None else dk + dk_h
            dq = dq_h if dq is None else dq + dq_h
        dk_ref[:, cols] += dk
        dv_ref[:, cols] += dv
        dq = dq.T.astype(BF16)
        out_ref[pl.ds(pl.multiple_of(step * block, block), block), cols] = dq
        sum_ref[:, cols] += jnp.sum(dq.astype(F32), axis=0, keepdims=True)

    @pl.when(step == pl.num_programs(0) - 1)
    def _():
        out_ref[:, width : 2 * width] = dk_ref[...].astype(BF16)
        dv = dv_ref[...].astype(BF16)
        out_ref[:, 2 * width : 3 * width] = dv
        sum_ref[:, width : 2 * width] = jnp.sum(dv.astype(F32), axis=0, keepdims=True)


def attention_backward(qkv, ctx, lse, d_own, d_other, seg_col, seg_row, block):
    rows, triple = qkv.shape
    width = triple // 3
    halves = rows // block // 2
    return pl.pallas_call(
        functools.partial(attention_backward_kernel, width, halves),
        grid=(rows // block,),
        in_specs=[
            pl.BlockSpec((rows, 1), lambda i: (0, 0)),
            pl.BlockSpec((1, block), lambda i: (0, i)),
            pl.BlockSpec((block, width), lambda i: (i, 0)),
            pl.BlockSpec((rows, width), lambda i: (0, 1)),
            pl.BlockSpec((rows, width), lambda i: (0, 2)),
            pl.BlockSpec((block, width), lambda i: (i, 0)),
            pl.BlockSpec((8, block), lambda i: (0, i)),
            *split_specs(block, width, halves),
        ],
        out_specs=[pl.BlockSpec((rows, triple), lambda i: (0, 0)), pl.BlockSpec((1, 2 * width), lambda i: (0, 0))],
        out_shape=[jax.ShapeDtypeStruct((rows, triple), BF16), jax.ShapeDtypeStruct((1, 2 * width), F32)],
        scratch_shapes=[pltpu.VMEM((rows, width), F32), pltpu.VMEM((rows, width), F32)],
        cost_estimate=CHEAP,
        name="attention_backward",
    )(seg_col, seg_row, qkv, qkv, qkv, ctx, lse, d_own, d_other)


def input_kernel(halves, d_ref, first_ref, w_ref, keep_ref, send_ref):
    step = pl.program_id(0)
    part = dot_nt(d_ref[...], w_ref[...])

    @pl.when(step < halves)
    def _():
        keep_ref[...] = first_ref[...] + part

    @pl.when(step >= halves)
    def _():
        send_ref[...] = part.astype(BF16)


def input_gradient(d_qkv, d_first, w_all, block):
    rows, model = d_first.shape
    width = d_qkv.shape[1]
    halves = rows // block
    by_row = pl.BlockSpec((block, width), lambda i: (i, 0))
    own = pl.BlockSpec((block, model), lambda i: (jnp.minimum(i, halves - 1), 0))
    return pl.pallas_call(
        functools.partial(input_kernel, halves),
        grid=(2 * halves,),
        in_specs=[by_row, own, pl.BlockSpec(w_all.shape, lambda i: (0, 0))],
        out_specs=split_specs(block, model, halves),
        out_shape=[jax.ShapeDtypeStruct((rows, model), F32), jax.ShapeDtypeStruct((rows, model), BF16)],
        cost_estimate=CHEAP,
        name="input_gradient",
    )(d_qkv, d_first, w_all)


def normalize(r):
    mean = jnp.mean(r, axis=-1, keepdims=True)
    cent = r - mean
    var = jnp.mean(cent * cent, axis=-1, keepdims=True)
    inv = lax.rsqrt(var + EPSILON)
    return cent * inv, inv


def normalize_back(hat, inv, gain, d_out):
    d_hat = d_out * gain
    first = jnp.mean(d_hat, axis=-1, keepdims=True)
    second = jnp.mean(d_hat * hat, axis=-1, keepdims=True)
    return inv * (d_hat - first - hat * second)


def swap(a):
    return lax.ppermute(a, "c", [(0, 1), (1, 0)])


def flip(a, axis, bit):
    n = lax.axis_size(axis)
    return lax.ppermute(a, axis, [(i, i ^ bit) for i in range(n)])


def turn(a, level):
    n, nx = lax.axis_size("dp"), lax.axis_size("x")
    pairs = []
    for d in range(n):
        for x in range(nx):
            for c in range(2):
                other = (d * nx + (x ^ 1)) if (c + level) % 2 == 0 else ((d ^ 1) * nx + x)
                pairs.append(((d * nx + x) * 2 + c, other * 2 + c))
    return lax.ppermute(a, ("dp", "x", "c"), pairs)


def tie(*values):
    return lax.optimization_barrier(values)


def add(*terms):
    return sum(t.astype(F32) for t in terms).astype(BF16)


def outer_bits():
    return lax.axis_size("dp").bit_length() - 2


def gather_far(near):
    parts = [near]
    for k in range(1, outer_bits()):
        held = jnp.concatenate(parts) if len(parts) > 1 else near
        parts.append(flip(held, "dp", 2 << k))
    return jnp.concatenate(parts[1:]) if len(parts) > 2 else parts[1]


OPT = {'bc': None, 'bn1': 'qkv', 'bz2': 'qkv', 'bf1': 'ctx', 'bn2': 'ctx', 'bf2': 'attn', 'c1': 'P3', 'c2': 'P4', 'b1': 'P3', 'b2': 'P4', 'c3': 'P5', 'b3': 'P6', 'an2': 'f1', 'bz1': 'f1'}


def stage(name, *values, **items):
    keys = [k for k in items if OPT.get(k) == name]
    extra, spans = [], []
    for k in keys:
        v = getattr(*items[k])
        many = isinstance(v, list)
        spans.append((k, len(v) if many else 1, many))
        extra += v if many else [v]
    if len(values) + len(extra) > 1:
        out = list(tie(*values, *extra))
    else:
        out = [*values, *extra]
    res, at = out[: len(values)], len(values)
    for k, n, many in spans:
        setattr(*items[k], out[at : at + n] if many else out[at])
        at += n
    return res if len(res) > 1 else (res[0] if res else None)


class Spread:
    def __init__(self, units, outer):
        self.units, self.outer = units, outer

    def first(self):
        self.one = turn(self.units, 0)

    def second(self):
        self.two = turn(jnp.concatenate([self.units, self.one]), 1)

    def pieces(self):
        n = self.units.shape[0]
        index = [(0, u, self.outer + u, 0, 0) for u in range(n)]
        index += [(1, u, self.outer + u, 1, 0) for u in range(n)]
        index += [(2, a * n + u, self.outer + u, a, 1) for a in range(2) for u in range(n)]
        return [self.units, self.one, self.two], index


def joined(spreads):
    arrays, index = [], []
    for s in spreads:
        more, at = s.pieces()
        index += [(i + len(arrays), *rest) for i, *rest in at]
        arrays += more
    return arrays, index


def put_units(index, moves, where_ref, ins, outs, each=None):
    dp = where_ref[0]
    for parity in range(2):

        @pl.when(where_ref[1] == parity)
        def _():
            for array, unit, outer, first, second in index:
                rx, ry = (second, first) if parity else (first, second)
                to = jnp.bitwise_xor(dp, 2 * outer + ry)
                for lead, rows, col, cols, target, at in moves:
                    value = ins[array][(unit, *lead, slice(0, rows), slice(col, col + cols))]
                    outs[target][pl.ds(pl.multiple_of(to * rows, 16), rows), at[rx] : at[rx] + cols] = value
                if each is not None:
                    each(ins[array], unit, to, rx)


def prepare_kernel(piece, dp_ref, qkv_ref, out_ref, up_ref, down_ref, qv_ref, *refs):
    vectors, (a_ref, bc_ref, row_ref) = refs[:-3], refs[-3:]
    part = qkv_ref.shape[2]
    for j in range(3):
        a_ref[:piece, j * part : (j + 1) * part] = qkv_ref[j]
    a_ref[:piece, 3 * part :] = out_ref[...].T
    row_ref[...] = jnp.zeros_like(row_ref)
    at = 0
    for v in vectors:
        n = v.shape[1]
        row_ref[0:1, at : at + n] = v[...].astype(F32)
        at += n
    n = qv_ref.shape[1]
    lane = lax.broadcasted_iota(jnp.int32, (n, part), 1)
    spot = (lane == lax.broadcasted_iota(jnp.int32, (n, part), 0) + n * dp_ref[0]).astype(BF16)
    both = dot_nn(qv_ref[...], spot)
    row_ref[1:2, :part] = both[0:1]
    row_ref[1:2, part : 2 * part] = both[1:2]
    exact = row_ref[0:1, :]
    high = exact.astype(BF16).astype(F32)
    middle = (exact - high).astype(BF16).astype(F32)
    low = exact - high - middle
    line = lax.broadcasted_iota(jnp.int32, (8, 1), 0)
    rows = jnp.where(line == 0, high, 0.0) + jnp.where(line == 1, middle, 0.0)
    rows += jnp.where(line == 2, low, 0.0) + jnp.where(line == 3, row_ref[1:2, :], 0.0)
    a_ref[piece:, :] = rows.astype(BF16)
    bc_ref[0] = up_ref[...]
    bc_ref[1] = down_ref[...].T


def prepare(w_qkv, w_out, w_up, w_down, b_qv, vectors):
    piece, part = w_qkv.shape[1:]
    model = w_up.shape[1]
    dp = lax.axis_index("dp").astype(jnp.int32)
    if piece % 16 == 0:

        def whole(s):
            return pl.BlockSpec(s, lambda i, d: (0,) * len(s))

        given = [w_qkv, w_out, w_up, w_down, b_qv, *[v[None] for v in vectors]]
        shapes = [(piece + 8, model), (2, piece, model)]
        return pl.pallas_call(
            functools.partial(prepare_kernel, piece),
            grid_spec=pltpu.PrefetchScalarGridSpec(
                num_scalar_prefetch=1,
                grid=(1,),
                in_specs=[whole(v.shape) for v in given],
                out_specs=[whole(s) for s in shapes],
                scratch_shapes=[pltpu.VMEM((8, model), F32)],
            ),
            out_shape=[jax.ShapeDtypeStruct(s, BF16) for s in shapes],
            cost_estimate=CHEAP,
            name="prepare_units",
        )(dp[None], *given)
    row = jnp.concatenate([v.astype(F32) for v in vectors])
    row = jnp.pad(row, (0, model - row.shape[0]))
    high = row.astype(BF16)
    middle = (row - high.astype(F32)).astype(BF16)
    low = (row - high.astype(F32) - middle.astype(F32)).astype(BF16)
    keep = lax.broadcasted_iota(jnp.int32, (1, part // b_qv.shape[1], 1), 1) == dp
    spot = jnp.where(keep, b_qv[:, None, :], jnp.zeros((), BF16)).reshape(-1)
    spot = jnp.pad(spot, (0, model - spot.shape[0]))
    tail = jnp.pad(jnp.stack([high, middle, low, spot]), ((0, 4), (0, 0)))
    unit = jnp.concatenate([w_qkv[0], w_qkv[1], w_qkv[2], w_out.T], axis=1)
    return jnp.concatenate([unit, tail], axis=0), jnp.stack([w_up, w_down.T])


def project_kernel(index, moves, piece, part, halves, where_ref, own_ref, other_ref, *refs):
    ins, (out_ref, w_ref, o_ref, ext_ref, bias_ref) = refs[:-5], refs[-5:]
    width = 2 * part

    @pl.when(pl.program_id(0) == 0)
    def _():
        bias_ref[...] = jnp.zeros_like(bias_ref)

        def each(source, unit, to, rx):
            value = source[unit, piece:, : 2 * part]
            ext_ref[to, :, 2 * part * rx : 2 * part * (rx + 1)] = value
            value = value.astype(F32)[3:4]
            bias_ref[0:1, rx * part : (rx + 1) * part] += value[:, :part]
            at = 2 * width + rx * part
            bias_ref[0:1, at : at + part] += value[:, part:]

        put_units(index, moves, where_ref, ins, (w_ref, o_ref), each)

    x = either(pl.program_id(0), halves, own_ref, other_ref)
    out_ref[...] = (dot_nn(x, w_ref[...]) + bias_ref[0:1, :]).astype(BF16)


def feed_kernel(index, moves, halves, where_ref, own_ref, other_ref, bias_ref, *refs):
    ins, (hidden_ref, slope_ref, keep_ref, send_ref, b_ref, c_ref) = refs[:-6], refs[-6:]
    step = pl.program_id(0)

    @pl.when(step == 0)
    def _():
        put_units(index, moves, where_ref, ins, (b_ref, c_ref))

    x = either(step, halves, own_ref, other_ref)
    hidden, slope = gelu_both(dot_nn(x, b_ref[...]) + bias_ref[...])
    hidden_ref[...] = hidden
    slope_ref[...] = slope
    part = dot_nt(hidden, c_ref[...])

    @pl.when(step < halves)
    def _():
        keep_ref[...] = part

    @pl.when(step >= halves)
    def _():
        send_ref[...] = part.astype(BF16)


def chunks(n, size=512):
    return [slice(at, min(at + size, n)) for at in range(0, n, size)]


def gelu_both(up):
    cdf = 0.5 * (1.0 + lax.erf(up * ROOT_HALF))
    slope = cdf + up * (jnp.exp(-0.5 * up * up) * INV_ROOT_TWO_PI)
    return (up * cdf).astype(BF16), slope.astype(BF16)


def feed_back_kernel(size, piece, where_ref, *refs):
    own_ref, other_ref, n_own_ref, n_other_ref, slope_ref, hidden_ref, c_ref, b_ref = refs[:8]
    keep_ref, send_ref, sum_ref, c_keep, c_send, b_keep, b_send = refs[8:15]
    d_ref, d_turned, n_turned, acc_ref, c_grad, b_grad = refs[15:]
    step, dp = pl.program_id(0), where_ref[0]
    half, model = own_ref.shape
    outer = c_keep.shape[0] // 2

    @pl.when(step == 0)
    def _():
        for at, d, n in ((0, own_ref, n_own_ref), (half, other_ref, n_other_ref)):
            d_ref[at : at + half, :] = d[...]
            d_turned[:, at : at + half] = d[...].T
            n_turned[:, at : at + half] = n[...].T

    d_up = (dot_nn(d_ref[...], c_ref[...]) * slope_ref[...].astype(F32)).astype(BF16)
    sum_ref[...] = jnp.sum(d_up.astype(F32), axis=0, keepdims=True)
    part = dot_nt(d_up, b_ref[...])

    @pl.when(step == 0)
    def _():
        acc_ref[...] = part

    @pl.when(step > 0)
    def _():
        acc_ref[...] += part

    c_grad[...] = dot_nn(d_turned[...], hidden_ref[...]).astype(BF16)
    b_grad[...] = dot_nn(n_turned[...], d_up).astype(BF16)
    width = c_ref.shape[1]
    for s in range(2 * model // width):
        for at in range(0, width, size):
            rx, to = divmod(s * width + at, model)
            for parity in range(2):

                @pl.when((step == s) & (where_ref[1] == parity))
                def _():
                    for ry in range(2):
                        first, second = (ry, rx) if parity else (rx, ry)
                        outs = ((c_send, b_send) if first else (c_keep, b_keep))

                        def move(z, carry):
                            rows = pl.ds(pl.multiple_of(jnp.bitwise_xor(dp, 2 * z + ry) * piece, 16), piece)
                            for out, grad in zip(outs, (c_grad, b_grad)):
                                out[second * outer + z, :, to : to + size] = grad[rows, at : at + size]
                            return carry

                        lax.fori_loop(0, outer, move, 0)

    @pl.when(step == pl.num_programs(0) - 1)
    def _():
        keep_ref[...] = acc_ref[:half, :]
        send_ref[...] = acc_ref[half:, :].astype(BF16)


def feed_back(d_own, d_other, n_own, n_other, slope, hidden, c, b, piece):
    rows, model = d_own.shape
    wide = b.shape[1]
    ndp = model // piece
    if piece % 16:
        d, n = jnp.concatenate([d_own, d_other]), jnp.concatenate([n_own, n_other])
        d_up = (dot_nn(d, c) * slope.astype(F32)).astype(BF16)
        part = dot_nt(d_up, b)
        sums = jnp.sum(d_up.astype(F32), axis=0, keepdims=True)
        wide_part = [((0, 1), 2, model, 0, True)]
        c_pair = summed([d_own, d_other, hidden], wide_part)
        b_pair = summed([n_own, n_other, d_up], wide_part)
        return part[:rows], part[rows:].astype(BF16), sums, *c_pair, *b_pair

    def whole(s):
        return pl.BlockSpec(s, lambda i, w: (0,) * len(s))

    def columns(n):
        return pl.BlockSpec((n, 512), lambda i, w: (0, i))

    units = (ndp, piece, model)
    return pl.pallas_call(
        functools.partial(feed_back_kernel, 256, piece),
        grid_spec=pltpu.PrefetchScalarGridSpec(
            num_scalar_prefetch=1,
            grid=(wide // 512,),
            in_specs=[whole((rows, model))] * 4 + [columns(2 * rows)] * 2 + [columns(model)] * 2,
            out_specs=[whole((rows, model))] * 2 + [columns(1)] + [whole(units)] * 4,
            scratch_shapes=[
                pltpu.VMEM((2 * rows, model), BF16),
                pltpu.VMEM((model, 2 * rows), BF16),
                pltpu.VMEM((model, 2 * rows), BF16),
                pltpu.VMEM((2 * rows, model), F32),
                pltpu.VMEM((model, 512), BF16),
                pltpu.VMEM((model, 512), BF16),
            ],
        ),
        out_shape=[
            jax.ShapeDtypeStruct((rows, model), F32),
            jax.ShapeDtypeStruct((rows, model), BF16),
            jax.ShapeDtypeStruct((1, wide), F32),
        ]
        + [jax.ShapeDtypeStruct(units, BF16)] * 4,
        cost_estimate=CHEAP,
        name="feed_back",
    )(where(), d_own, d_other, n_own, n_other, slope, hidden, c, b)


def ordered(spreads, moves):
    arrays, index = joined(spreads)
    order = jnp.bitwise_xor(jnp.arange(lax.axis_size("dp")), lax.axis_index("dp"))
    made = {}
    for lead, rows, col, cols, target, at in moves:
        for rx in range(2):
            both = []
            for swapped in range(2):
                units = {}
                for array, unit, outer, first, second in index:
                    x, y = (second, first) if swapped else (first, second)
                    if x == rx:
                        units[2 * outer + y] = arrays[array][(unit, *lead)][rows, col : col + cols]
                both.append(jnp.stack([units[k] for k in sorted(units)]))
            stack = jnp.take(jnp.where(lax.axis_index("c") == 0, both[0], both[1]), order, axis=0)
            made.setdefault(target, []).append((at[rx], stack))
    return [jnp.concatenate([m for _, m in sorted(made[t], key=lambda p: p[0])], axis=-1) for t in sorted(made)]


def project(spreads, own, other, piece, part, block):
    width = 2 * part
    rows, model = own.shape
    halves = rows // block
    moves = [((), piece, j * part, part, 0, (j * width, j * width + part)) for j in range(3)]
    moves.append(((), piece, 3 * part, part, 1, (0, part)))
    if piece % 16 == 0:
        arrays, index = joined(spreads)

        def whole(s):
            return pl.BlockSpec(s, lambda i, d: (0,) * len(s))

        shapes = [(model, 3 * width), (model, width), (model // piece, 8, 2 * width)]
        return pl.pallas_call(
            functools.partial(project_kernel, index, moves, piece, part, halves),
            grid_spec=pltpu.PrefetchScalarGridSpec(
                num_scalar_prefetch=1,
                grid=(2 * halves,),
                in_specs=split_specs(block, model, halves) + [whole(a.shape) for a in arrays],
                out_specs=[pl.BlockSpec((block, 3 * width), lambda i, d: (i, 0))] + [whole(s) for s in shapes],
                scratch_shapes=[pltpu.VMEM((8, 3 * width), F32)],
            ),
            out_shape=[jax.ShapeDtypeStruct(s, BF16) for s in [(2 * rows, 3 * width), *shapes]],
            cost_estimate=CHEAP,
            name="project_kernel",
        )(where(), own, other, *arrays)
    slices = [(lead, slice(0, n), *rest) for lead, n, *rest in moves]
    slices.append(((), slice(piece, piece + 8), 0, 2 * part, 2, (0, 2 * part)))
    w, o, ext = ordered(spreads, slices)
    bias = jnp.sum(ext[:, 3].astype(F32), axis=0).reshape(2, 2, part)
    bias = jnp.concatenate([bias[:, 0].reshape(-1), jnp.zeros((width,), F32), bias[:, 1].reshape(-1)])
    w, o = w.reshape(model, -1), o.reshape(model, -1)
    return (dot_nn(jnp.concatenate([own, other]), w) + bias[None]).astype(BF16), w, o, ext


def feed(spreads, own, other, bias, piece, block):
    rows, model = own.shape
    halves = rows // block
    moves = [((k,), piece, 0, model, k, (0, model)) for k in range(2)]
    if piece % 16 == 0:
        arrays, index = joined(spreads)

        def whole(s):
            return pl.BlockSpec(s, lambda i, d: (0,) * len(s))

        wide = pl.BlockSpec((block, 2 * model), lambda i, d: (i, 0))
        return pl.pallas_call(
            functools.partial(feed_kernel, index, moves, halves),
            grid_spec=pltpu.PrefetchScalarGridSpec(
                num_scalar_prefetch=1,
                grid=(2 * halves,),
                in_specs=split_specs(block, model, halves) + [whole(a.shape) for a in [bias, *arrays]],
                out_specs=[wide, wide, *split_specs(block, model, halves)] + [whole((model, 2 * model))] * 2,
            ),
            out_shape=[jax.ShapeDtypeStruct((2 * rows, 2 * model), BF16)] * 2
            + [jax.ShapeDtypeStruct((rows, model), F32), jax.ShapeDtypeStruct((rows, model), BF16)]
            + [jax.ShapeDtypeStruct((model, 2 * model), BF16)] * 2,
            cost_estimate=CHEAP,
            name="feed_kernel",
        )(where(), own, other, bias, *arrays)
    b, c = ordered(spreads, [(lead, slice(0, n), *rest) for lead, n, *rest in moves])
    b, c = b.reshape(model, -1), c.reshape(model, -1)
    hidden, slope = gelu_both(dot_nn(jnp.concatenate([own, other]), b) + bias)
    part = dot_nt(hidden, c)
    return hidden, slope, part[:rows], part[rows:].astype(BF16), b, c


def pull(own, other, slope, c, b, block):
    rows, model = own.shape
    wide = b.shape[1]
    halves = rows // block

    def whole(s):
        return pl.BlockSpec(s, lambda i: (0, 0))

    by_row = pl.BlockSpec((block, wide), lambda i: (i, 0))
    return pl.pallas_call(
        functools.partial(pull_kernel, halves),
        grid=(2 * halves,),
        in_specs=[*split_specs(block, model, halves), by_row, whole(c.shape), whole(b.shape)],
        out_specs=[by_row, *split_specs(block, model, halves), whole((1, wide))],
        out_shape=[
            jax.ShapeDtypeStruct((2 * rows, wide), BF16),
            jax.ShapeDtypeStruct((rows, model), F32),
            jax.ShapeDtypeStruct((rows, model), BF16),
            jax.ShapeDtypeStruct((1, wide), F32),
        ],
        cost_estimate=CHEAP,
        name="pull_kernel",
    )(own, other, slope, c, b)


def where():
    return jnp.stack([lax.axis_index("dp"), lax.axis_index("c")]).astype(jnp.int32)


def sum_kernel(parts, piece, extra, part, where_ref, *refs):
    count = 1 + max(max(*p[0], p[1]) for p in parts)
    ins = refs[:count]
    scratch = refs[count + (2 if extra else 0) :]
    outs, left_ref, acc, ext_ref = scratch[:2], scratch[2], scratch[3], scratch[4]
    dp, step = where_ref[0], pl.program_id(0)
    outer = outs[0].shape[0] // 2
    blocked = parts[0][4]
    if extra:
        lines_ref, bias_ref = refs[count : count + 2]
        ext_ref[...] = lines_ref[...].astype(F32)
        for rx in range(2):
            for k in range(2):
                ext_ref[rx, extra - 1 : extra, k * part : (k + 1) * part] = bias_ref[
                    0:1, (2 * k + rx) * part : (2 * k + rx + 1) * part
                ]

    def turned(own, other):
        half = ins[own].shape[0]
        left_ref[:, :half] = ins[own][...].T
        left_ref[:, half:] = ins[other][...].T

    for k, ((own, other), right, width, at, by_block) in enumerate(parts):
        if by_block:

            @pl.when(step == 0)
            def _():
                turned(own, other)

            for lanes in chunks(width, 256):
                acc[:, lanes] = dot_nn(left_ref[...], ins[right][:, lanes]).astype(BF16)
        else:

            @pl.when(step == 0)
            def _():
                if k == 0 or parts[k - 1][0] != (own, other):
                    turned(own, other)
                for j in range(ins[right].shape[1] // (2 * width)):
                    both = dot_nn(left_ref[...], ins[right][:, 2 * j * width : 2 * (j + 1) * width]).astype(BF16)
                    for rx in range(2):
                        lanes = slice(rx * acc.shape[1] // 2 + at + j * width, rx * acc.shape[1] // 2 + at + (j + 1) * width)
                        acc[:, lanes] = both[:, rx * width : (rx + 1) * width]

    span = outs[0].shape[2]

    def put(rx):
        lanes = slice(0, span) if blocked else slice(rx * span, (rx + 1) * span)
        for parity in range(2):

            @pl.when(where_ref[1] == parity)
            def _():
                for ry in range(2):
                    first, second = (ry, rx) if parity else (rx, ry)

                    def move(z, carry):
                        rows = pl.ds(pl.multiple_of(jnp.bitwise_xor(dp, 2 * z + ry) * piece, 16), piece)
                        outs[first][second * outer + z, :piece, :] = acc[rows, lanes]
                        if extra:
                            outs[first][second * outer + z, piece:, :] = ext_ref[rx].astype(BF16)
                        return carry

                    lax.fori_loop(0, outer, move, 0)

    for rx in range(2):
        if blocked:
            pl.when(step == rx)(functools.partial(put, rx))
        else:
            put(rx)


def summed(arrays, parts, ext=None, bias=None):
    ndp = lax.axis_size("dp")
    model = arrays[0].shape[1]
    piece = model // ndp
    blocked = parts[0][4]
    width = sum(p[2] if p[4] else arrays[p[1]].shape[1] // 2 for p in parts)
    extra = 0 if ext is None else ext.shape[1]
    if piece % 16 == 0:

        def whole(s):
            return pl.BlockSpec(s, lambda i, d: (0,) * len(s))

        given = list(arrays) + ([] if ext is None else [ext, bias])
        specs = [whole(a.shape) for a in given]
        if blocked:
            right = parts[0][1]
            specs[right] = pl.BlockSpec((arrays[right].shape[0], width), lambda i, d: (0, i))
        shape = (ndp, piece + extra, width)
        return pl.pallas_call(
            functools.partial(sum_kernel, parts, piece, extra, 0 if bias is None else bias.shape[1] // 4),
            grid_spec=pltpu.PrefetchScalarGridSpec(
                num_scalar_prefetch=1,
                grid=(2 if blocked else 1,),
                in_specs=specs,
                out_specs=[whole(shape)] * 2,
                scratch_shapes=[
                    pltpu.VMEM((model, 2 * arrays[0].shape[0]), BF16),
                    pltpu.VMEM((model, width if blocked else 2 * width), BF16),
                    pltpu.VMEM((2, max(extra, 8), width), F32),
                ],
            ),
            out_shape=[jax.ShapeDtypeStruct(shape, BF16)] * 2,
            cost_estimate=CHEAP,
            name="sum_units",
        )(where(), *given)
    order = jnp.bitwise_xor(jnp.arange(ndp), lax.axis_index("dp"))
    sides = []
    if extra:
        line = jnp.transpose(bias.reshape(2, 2, -1), (1, 0, 2)).reshape(2, -1)
        line = jnp.pad(line, ((0, 0), (0, width - line.shape[1]))).astype(BF16)
        ext = jnp.concatenate([ext[:, :-1], line[:, None]], axis=1)
    for rx in range(2):
        g = []
        for (own, other), right, cols, _, by_block in parts:
            left = jnp.concatenate([arrays[own], arrays[other]])
            for j in range(1 if by_block else arrays[right].shape[1] // (2 * cols)):
                at = (2 * j + rx) * cols
                g.append(dot_tn(left, arrays[right][:, at : at + cols]).astype(BF16))
        g = jnp.concatenate(g, axis=1).reshape(ndp, piece, width)
        if extra:
            g = jnp.concatenate([g, jnp.broadcast_to(ext[rx][None], (ndp, extra, width))], axis=1)
        g = jnp.take(g, order, axis=0).reshape(ndp // 2, 2, piece + extra, width)
        sides.append(jnp.moveaxis(g, 1, 0))
    g = jnp.stack(sides)
    g = jnp.where(lax.axis_index("c") == 0, g, jnp.swapaxes(g, 0, 1))
    return g[0].reshape(ndp, piece + extra, width), g[1].reshape(ndp, piece + extra, width)


class Scatter:
    def __init__(self, pair):
        self.keep, self.send = pair

    def first(self):
        self.one = turn(self.send, 0)

    def second(self):
        half = self.keep.shape[0] // 2
        self.kept = add(self.keep[:half], self.one[:half])
        self.two = turn(add(self.keep[half:], self.one[half:]), 1)

    def third(self):
        total = add(self.kept, self.two)
        outer = total.shape[0]
        if outer <= 4:
            self.last = [total[0]]
            self.three = [flip(total[k], "dp", 2 * k) for k in range(1, outer)]
            return
        for k in reversed(range(outer_bits())):
            half = total.shape[0] // 2
            total = add(total[:half], flip(total[half:], "dp", 2 << k))
        self.last, self.three = [total[0]], []

    def result(self):
        return sum(t.astype(F32) for t in self.last + self.three)


def local(
    tokens, grad_out, seg_ids, w_qkv, b_qv, w_out, w_up, b_up, w_down, b_out, b_down, g_one, s_one, g_two, s_two
):
    ndp = lax.axis_size("dp")
    nx = lax.axis_size("x")
    parity = lax.axis_index("c")
    which = lax.axis_index("x")
    place_dp = lax.axis_index("dp")
    rows, model = tokens.shape
    piece = model // ndp
    part = w_qkv.shape[2]
    width = nx * part
    slim = model // (ndp * nx * 2)
    qv = part // ndp
    extra = 8
    block = 256
    tall = 512

    unit_a, unit_bc = prepare(
        w_qkv, w_out, w_up, w_down, b_qv, [b_out, b_down, g_one, s_one, g_two, s_two, b_up]
    )
    a_near = Spread(jnp.stack([unit_a, flip(unit_a, "dp", 2)]), 0)

    class Box:
        pass

    box = Box()
    box.bc = unit_bc
    a_near.units = stage("z1", a_near.units, bc=(box, "bc"))
    a_far = Spread(gather_far(a_near.units), 2)
    a_near.first()
    a_near.one = stage("n1", a_near.one, bc=(box, "bc"), az=(a_far, "units"))
    a_near.second()
    a_far.units = stage("z2", a_far.units, bc=(box, "bc"), an2=(a_near, "two"))
    a_far.first()
    bc_near = Spread(jnp.stack([box.bc, flip(box.bc, "dp", 2)]), 0)
    a_far.one = stage("f1", a_far.one, bz1=(bc_near, "units"), an2=(a_near, "two"))
    a_far.second()
    bc_far = Spread(gather_far(bc_near.units), 2)
    bc_items = lambda: dict(bn1=(bc_near, "one"), bz2=(bc_far, "units"), bn2=(bc_near, "two"), bf1=(bc_far, "one"), bf2=(bc_far, "two"))
    done = set()

    def advance(name, *values):
        res = stage(name, *values, **{k: v for k, v in bc_items().items() if hasattr(*v)})
        order = ["z2", "f1", "f2", "qkv", "ctx", "attn", "normed", "feed"]
        at = order.index(name)
        ready = lambda k: k is None or order.index(OPT.get(k, "feed")) <= at
        if "n1" not in done and order.index(OPT.get("rn1", "z2")) <= at:
            bc_near.first()
            done.add("n1")
        if "n2" not in done and "n1" in done and (ready("bn1") or name == "feed"):
            bc_near.second()
            done.add("n2")
        if "f1" not in done and (ready("bz2") or name == "feed"):
            bc_far.first()
            done.add("f1")
        if "f2" not in done and "f1" in done and (ready("bf1") or name == "feed"):
            bc_far.second()
            done.add("f2")
        return res

    advance("z2")
    a_far.two = advance("f2", a_far.two)

    seg = lax.dynamic_index_in_dim(seg_ids, which, 0, keepdims=False).reshape(2, rows)
    seg_rel = jnp.concatenate(
        [
            lax.dynamic_index_in_dim(seg, parity, 0, keepdims=False),
            lax.dynamic_index_in_dim(seg, 1 - parity, 0, keepdims=False),
        ]
    )
    seg_col = seg_rel[:, None]
    seg_row = seg_rel[None, :]
    x_other = swap(tokens)

    qkv, w_all, o_t, ext = project([a_near, a_far], tokens, x_other, piece, part, block)
    ext = ext[:, :3].astype(F32)
    ext = (ext[:, 0] + ext[:, 1] + ext[:, 2]).reshape(ndp, nx, 2 * part)
    bias_up = jnp.transpose(ext[:, :, 6 * slim : 6 * slim + piece], (1, 0, 2)).reshape(1, nx * model)
    six = ext[:, :, : 6 * slim]
    six = jnp.stack([six, swap(six)], axis=2)
    six = jnp.where(lax.broadcasted_iota(jnp.int32, (1, 1, 2, 1), 2) == parity, six[:, :, :1], six[:, :, 1:])
    six = jnp.where(which == 0, six, six[:, ::-1]).reshape(ndp * nx * 2, 6, slim)
    vectors = jnp.transpose(six, (1, 0, 2)).reshape(6, model)
    bout_f, bdown_f, gone_f, sone_f, gtwo_f, stwo_f = [vectors[i : i + 1] for i in range(6)]

    qkv = advance("qkv", qkv)
    ctx, lse = attention_forward(qkv, seg_col, seg_row, tall, 0, 2 * rows // tall, ())
    ctx = advance("ctx", ctx)
    attn_send = dot_nt(ctx[rows:], o_t).astype(BF16)
    attn = dot_nt(ctx[:rows], o_t) + swap(attn_send).astype(F32)
    attn = advance("attn", attn)
    first = tokens.astype(F32) + attn + bout_f
    hat_one, inv_one = normalize(first)
    normed = hat_one * gone_f + sone_f
    normed_low = advance("normed", normed.astype(BF16))
    normed_other = swap(normed_low)
    normed_other = advance("feed", normed_other)
    hidden, slope, keep, send, b_all, c_all = feed([bc_near, bc_far], normed_low, normed_other, bias_up, piece, block)
    branch = keep + swap(send).astype(F32)
    second = normed + branch + bdown_f
    hat_two, inv_two = normalize(second)
    layer_out = (hat_two * gtwo_f + stwo_f).astype(BF16)

    g_in = grad_out.astype(F32)
    d_gain_two = jnp.sum(g_in * hat_two, axis=0)
    d_shift_two = jnp.sum(g_in, axis=0)
    d_second = normalize_back(hat_two, inv_two, gtwo_f, g_in)
    d_branch = d_second.astype(BF16)
    d_bias_down = jnp.sum(d_branch.astype(F32), axis=0)
    db_other = swap(d_branch)

    sc = sb = sa = None
    order = ["P0", "P1", "P2", "P3", "P4", "P5", "P6", "P7"]
    sent = set()

    def go(name, *values):
        items = {}
        for k, s in (("c", sc), ("b", sb)):
            if s is not None:
                for n, f in (("1", "one"), ("2", "two"), ("3", "three")):
                    if hasattr(s, f):
                        items[k + n] = (s, f)
        res = stage(name, *values, **items)
        at = order.index(name)
        for k, s in (("c", sc), ("b", sb)):
            if s is None:
                continue
            for n, need, f in ((1, None, "first"), (2, "1", "second"), (3, "2", "third")):
                if k + str(n) in sent or (n > 1 and k + str(n - 1) not in sent):
                    continue
                if n == 1 or order.index(OPT.get(k + need, "P7")) <= at:
                    getattr(s, f)()
                    sent.add(k + str(n))
        return res

    keep, send, d_bias_up, *pairs = feed_back(
        d_branch, db_other, normed_low, normed_other, slope, hidden, c_all, b_all, piece
    )
    sc, sb = Scatter(pairs[:2]), Scatter(pairs[2:])
    go("P0")
    d_normed = d_second + keep + swap(send).astype(F32)
    d_normed = go("P1", d_normed)
    d_gain_one = jnp.sum(d_normed * hat_one, axis=0)
    d_shift_one = jnp.sum(d_normed, axis=0)
    d_first = normalize_back(hat_one, inv_one, gone_f, d_normed)
    d_attn = d_first.astype(BF16)
    d_bias_out = jnp.sum(d_attn.astype(F32), axis=0)
    da_other = swap(d_attn)
    d_ctx = dot_nn(d_attn, o_t).astype(BF16)
    sums = jnp.stack([d_bias_out, d_bias_down, d_gain_one, d_shift_one, d_gain_two, d_shift_two])
    sums = sums + swap(sums)
    d_ctx_other = dot_nn(da_other, o_t).astype(BF16)
    spread = jnp.concatenate([d_bias_up.reshape(nx, model), jnp.broadcast_to(sums.reshape(1, -1), (nx, 6 * model))], axis=1)
    spread = jnp.pad(spread.reshape(nx, 7, model), ((0, 0), (0, 1), (0, 0))).astype(BF16)
    d_ctx_other, spread = go("P2", d_ctx_other, spread)
    d_qkv, bias = attention_backward(qkv, ctx, lse, d_ctx, d_ctx_other, seg_col, seg_row, block)
    d_qkv = go("P3", d_qkv)
    attention_parts = [((0, 1), 2, part, 0, False), ((3, 4), 5, part, 3 * part, False)]
    given = [tokens, x_other, d_qkv, d_attn, da_other, ctx]
    sa = Scatter(summed(given, attention_parts, spread, bias))
    d_qkv, sa.send = go("P4", d_qkv, sa.send)
    sa.first()
    keep, send = input_gradient(d_qkv, d_first, w_all, block)
    sa.one, keep, send = go("P5", sa.one, keep, send)
    sa.second()
    input_grad = keep + swap(send).astype(F32)
    sa.two, input_grad = go("P6", sa.two, input_grad)
    sa.third()
    go("P7")
    input_grad = input_grad.astype(BF16)
    gc = sc.result()
    gb = sb.result()
    ga = sa.result()
    g_qkv = jnp.stack([ga[:piece, j * part : (j + 1) * part] for j in range(3)])
    tail = ga[piece:]
    g_bqv = lax.dynamic_slice_in_dim(tail[7, : 2 * part].reshape(2, part), place_dp * qv, qv, axis=1)
    g_bup = lax.dynamic_slice_in_dim(tail[0], place_dp * piece, piece)
    six = lax.dynamic_slice_in_dim(tail[1:7], ((place_dp * nx + which) * 2 + parity) * slim, slim, axis=1)
    return (
        layer_out,
        input_grad,
        g_qkv,
        g_bqv,
        ga[:piece, 3 * part :].T,
        gb,
        g_bup,
        gc.T,
        *[six[i] for i in range(6)],
    )


def solution(mesh):
    ndp, nt = mesh.devices.shape
    fine = Mesh(mesh.devices.reshape(ndp, nt // 2, 2), ("dp", "x", "c"))
    tensor = ("x", "c")
    every = ("dp", "x", "c")
    row = P(every, None)
    vec = P(every)
    return jax.shard_map(
        local,
        mesh=fine,
        in_specs=(
            row,
            row,
            P("dp", None),
            P(None, "dp", tensor),
            P(None, ("x", "c", "dp")),
            P(tensor, "dp"),
            P("dp", tensor),
            P(("x", "c", "dp")),
            P(tensor, "dp"),
            vec,
            vec,
            vec,
            vec,
            vec,
            vec,
        ),
        out_specs=(
            row,
            row,
            P(None, "dp", tensor),
            P(None, ("x", "c", "dp")),
            P(tensor, "dp"),
            P("dp", tensor),
            P(("x", "c", "dp")),
            P(tensor, "dp"),
            vec,
            vec,
            vec,
            vec,
            vec,
            vec,
        ),
        check_vma=False,
    )
```

```python
import functools

import jax
import jax.numpy as jnp
from jax import lax
from jax.experimental import pallas as pl
from jax.experimental.pallas import tpu as pltpu
from jax.sharding import Mesh, PartitionSpec as P

HD = 64
LANES = 128
EPSILON = 1e-05
ROOT_HALF = 0.7071067811865476
INV_ROOT_TWO_PI = 0.3989422804014327
F32 = jnp.float32
BF16 = jnp.bfloat16


def dot(a, b, dims):
    return lax.dot_general(a, b, (dims, ((), ())), preferred_element_type=F32)


def dot_nn(a, b):
    return dot(a, b, ((1,), (0,)))


def dot_nt(a, b):
    return dot(a, b, ((1,), (1,)))


def dot_tn(a, b):
    return dot(a, b, ((0,), (0,)))


CHEAP = pl.CostEstimate(flops=1000, bytes_accessed=1000, transcendentals=0)


def attention_forward_kernel(width, seg_q_ref, seg_k_ref, q_ref, k_ref, v_ref, *refs):
    ctx_ref, lse_ref = refs[-2:]
    lane = lax.broadcasted_iota(jnp.int32, (1, LANES), 1)
    bias = jnp.where(seg_q_ref[...] == seg_k_ref[...], 0.0, -1000000000.0)
    block = q_ref.shape[0]

    stats = jnp.zeros((block, LANES), F32)
    for tile in range(width // LANES):
        cols = slice(tile * LANES, (tile + 1) * LANES)
        q2 = q_ref[:, cols] * jnp.asarray(0.125, BF16)
        k2 = k_ref[:, cols]
        v2 = v_ref[:, cols]
        outs = []
        for half in range(2):
            qm = jnp.where((lane // HD) == half, q2, jnp.zeros_like(q2))
            s = dot_nt(qm, k2) + bias
            top = jnp.max(s, axis=-1, keepdims=True)
            e = jnp.exp(s - top)
            total = jnp.sum(e, axis=-1, keepdims=True)
            outs.append(dot_nn(e.astype(BF16), v2) * (1.0 / total))
            stats = jnp.where(lane == 2 * tile + half, top + jnp.log(total), stats)
        ctx_ref[:, cols] = jnp.where(lane < HD, outs[0], outs[1]).astype(BF16)
    lse_ref[...] = stats.T[: lse_ref.shape[0], :]


def attention_forward(qkv, seg_col, seg_row, block, first, count, made):
    rows, triple = qkv.shape
    width = triple // 3
    return pl.pallas_call(
        functools.partial(attention_forward_kernel, width),
        grid=(count,),
        in_specs=[
            pl.BlockSpec((block, 1), lambda i: (first + i, 0)),
            pl.BlockSpec((1, rows), lambda i: (0, 0)),
            pl.BlockSpec((block, width), lambda i: (first + i, 0)),
            pl.BlockSpec((rows, width), lambda i: (0, 1)),
            pl.BlockSpec((rows, width), lambda i: (0, 2)),
        ]
        + [pl.BlockSpec(memory_space=pl.ANY)] * len(made),
        out_specs=[
            pl.BlockSpec((block, width), lambda i: (first + i, 0)),
            pl.BlockSpec((8, block), lambda i: (0, first + i)),
        ],
        out_shape=[
            jax.ShapeDtypeStruct((rows, width), BF16),
            jax.ShapeDtypeStruct((8, rows), F32),
        ],
        input_output_aliases={5 + i: i for i in range(len(made))},
        cost_estimate=CHEAP,
        name="attention_forward",
    )(seg_col, seg_row, qkv, qkv, qkv, *made)


def split_specs(block, columns, halves):
    return [
        pl.BlockSpec((block, columns), lambda i, *_: (jnp.minimum(i, halves - 1), 0)),
        pl.BlockSpec((block, columns), lambda i, *_: (jnp.maximum(i - halves, 0), 0)),
    ]


def either(step, halves, own_ref, other_ref):
    return jnp.where(step < halves, own_ref[...], other_ref[...])


def attention_backward_kernel(
    width, halves, seg_k_ref, seg_q_ref, q_ref, k_ref, v_ref, ctx_ref, lse_ref, own_ref, other_ref, out_ref, sum_ref, dk_ref, dv_ref
):
    step = pl.program_id(0)
    block = q_ref.shape[0]
    lane = lax.broadcasted_iota(jnp.int32, (1, LANES), 1)

    @pl.when(step == 0)
    def _():
        dk_ref[...] = jnp.zeros_like(dk_ref)
        dv_ref[...] = jnp.zeros_like(dv_ref)
        sum_ref[...] = jnp.zeros_like(sum_ref)

    bias = jnp.where(seg_k_ref[...] == seg_q_ref[...], 0.0, -1000000000.0)
    for pair in range(width // LANES):
        cols = slice(pair * LANES, (pair + 1) * LANES)
        q2 = q_ref[:, cols] * jnp.asarray(0.125, BF16)
        k2 = k_ref[:, cols]
        v2 = v_ref[:, cols]
        d2 = jnp.where(step < halves, own_ref[:, cols], other_ref[:, cols])
        prod = (d2.astype(F32) * ctx_ref[:, cols].astype(F32)).T
        kt = (k2 * jnp.asarray(0.125, BF16)).T
        row = lax.broadcasted_iota(jnp.int32, (LANES, 1), 0)
        dq = None
        dk = None
        dv = None
        for half in range(2):
            mine = (lane // HD) == half
            qm = jnp.where(mine, q2, jnp.zeros_like(q2))
            dm = jnp.where(mine, d2, jnp.zeros_like(d2))
            ktm = jnp.where((row // HD) == half, kt, jnp.zeros_like(kt))
            inner = jnp.sum(prod[half * HD : (half + 1) * HD, :], axis=0, keepdims=True)
            lse = lse_ref[2 * pair + half : 2 * pair + half + 1, :]
            p = jnp.exp(dot_nt(k2, qm) + bias - lse)
            dp = dot_nt(v2, dm)
            ds = (p * (dp - inner)).astype(BF16)
            dv_h = dot_nn(p.astype(BF16), dm)
            dk_h = dot_nn(ds, qm)
            dq_h = dot_nn(ktm, ds)
            dv = dv_h if dv is None else dv + dv_h
            dk = dk_h if dk is None else dk + dk_h
            dq = dq_h if dq is None else dq + dq_h
        dk_ref[:, cols] += dk
        dv_ref[:, cols] += dv
        dq = dq.T.astype(BF16)
        out_ref[pl.ds(pl.multiple_of(step * block, block), block), cols] = dq
        sum_ref[:, cols] += jnp.sum(dq.astype(F32), axis=0, keepdims=True)

    @pl.when(step == pl.num_programs(0) - 1)
    def _():
        out_ref[:, width : 2 * width] = dk_ref[...].astype(BF16)
        dv = dv_ref[...].astype(BF16)
        out_ref[:, 2 * width : 3 * width] = dv
        sum_ref[:, width : 2 * width] = jnp.sum(dv.astype(F32), axis=0, keepdims=True)


def attention_backward(qkv, ctx, lse, d_own, d_other, seg_col, seg_row, block):
    rows, triple = qkv.shape
    width = triple // 3
    halves = rows // block // 2
    return pl.pallas_call(
        functools.partial(attention_backward_kernel, width, halves),
        grid=(rows // block,),
        in_specs=[
            pl.BlockSpec((rows, 1), lambda i: (0, 0)),
            pl.BlockSpec((1, block), lambda i: (0, i)),
            pl.BlockSpec((block, width), lambda i: (i, 0)),
            pl.BlockSpec((rows, width), lambda i: (0, 1)),
            pl.BlockSpec((rows, width), lambda i: (0, 2)),
            pl.BlockSpec((block, width), lambda i: (i, 0)),
            pl.BlockSpec((8, block), lambda i: (0, i)),
            *split_specs(block, width, halves),
        ],
        out_specs=[pl.BlockSpec((rows, triple), lambda i: (0, 0)), pl.BlockSpec((1, 2 * width), lambda i: (0, 0))],
        out_shape=[jax.ShapeDtypeStruct((rows, triple), BF16), jax.ShapeDtypeStruct((1, 2 * width), F32)],
        scratch_shapes=[pltpu.VMEM((rows, width), F32), pltpu.VMEM((rows, width), F32)],
        cost_estimate=CHEAP,
        name="attention_backward",
    )(seg_col, seg_row, qkv, qkv, qkv, ctx, lse, d_own, d_other)


def input_kernel(halves, d_ref, first_ref, w_ref, keep_ref, send_ref):
    step = pl.program_id(0)
    part = dot_nt(d_ref[...], w_ref[...])

    @pl.when(step < halves)
    def _():
        keep_ref[...] = first_ref[...] + part

    @pl.when(step >= halves)
    def _():
        send_ref[...] = part.astype(BF16)


def input_gradient(d_qkv, d_first, w_all, block):
    rows, model = d_first.shape
    width = d_qkv.shape[1]
    halves = rows // block
    by_row = pl.BlockSpec((block, width), lambda i: (i, 0))
    own = pl.BlockSpec((block, model), lambda i: (jnp.minimum(i, halves - 1), 0))
    return pl.pallas_call(
        functools.partial(input_kernel, halves),
        grid=(2 * halves,),
        in_specs=[by_row, own, pl.BlockSpec(w_all.shape, lambda i: (0, 0))],
        out_specs=split_specs(block, model, halves),
        out_shape=[jax.ShapeDtypeStruct((rows, model), F32), jax.ShapeDtypeStruct((rows, model), BF16)],
        cost_estimate=CHEAP,
        name="input_gradient",
    )(d_qkv, d_first, w_all)


def normalize(r):
    mean = jnp.mean(r, axis=-1, keepdims=True)
    cent = r - mean
    var = jnp.mean(cent * cent, axis=-1, keepdims=True)
    inv = lax.rsqrt(var + EPSILON)
    return cent * inv, inv


def normalize_back(hat, inv, gain, d_out):
    d_hat = d_out * gain
    first = jnp.mean(d_hat, axis=-1, keepdims=True)
    second = jnp.mean(d_hat * hat, axis=-1, keepdims=True)
    return inv * (d_hat - first - hat * second)


def swap(a):
    return lax.ppermute(a, "c", [(0, 1), (1, 0)])


def flip(a, axis, bit):
    n = lax.axis_size(axis)
    return lax.ppermute(a, axis, [(i, i ^ bit) for i in range(n)])


def turn(a, level):
    n, nx = lax.axis_size("dp"), lax.axis_size("x")
    pairs = []
    for d in range(n):
        for x in range(nx):
            for c in range(2):
                other = (d * nx + (x ^ 1)) if (c + level) % 2 == 0 else ((d ^ 1) * nx + x)
                pairs.append(((d * nx + x) * 2 + c, other * 2 + c))
    return lax.ppermute(a, ("dp", "x", "c"), pairs)


def tie(*values):
    return lax.optimization_barrier(values)


def add(*terms):
    return sum(t.astype(F32) for t in terms).astype(BF16)


def outer_bits():
    return lax.axis_size("dp").bit_length() - 2


def gather_far(near):
    parts = [near]
    for k in range(1, outer_bits()):
        held = jnp.concatenate(parts) if len(parts) > 1 else near
        parts.append(flip(held, "dp", 2 << k))
    return jnp.concatenate(parts[1:]) if len(parts) > 2 else parts[1]


OPT = {'bc': None, 'bn1': 'f2', 'bz2': 'qkv', 'bf1': 'ctx', 'bn2': 'ctx', 'bf2': 'attn', 'c1': 'P3', 'c2': 'P4', 'c3': 'P5', 'b1': 'P3', 'b2': 'P5', 'b3': 'P6', 'an2': 'f1', 'bz1': 'f1'}


def stage(name, *values, **items):
    keys = [k for k in items if OPT.get(k) == name]
    extra, spans = [], []
    for k in keys:
        v = getattr(*items[k])
        many = isinstance(v, list)
        spans.append((k, len(v) if many else 1, many))
        extra += v if many else [v]
    if len(values) + len(extra) > 1:
        out = list(tie(*values, *extra))
    else:
        out = [*values, *extra]
    res, at = out[: len(values)], len(values)
    for k, n, many in spans:
        setattr(*items[k], out[at : at + n] if many else out[at])
        at += n
    return res if len(res) > 1 else (res[0] if res else None)


class Spread:
    def __init__(self, units, outer):
        self.units, self.outer = units, outer

    def first(self):
        self.one = turn(self.units, 0)

    def second(self):
        self.two = turn(jnp.concatenate([self.units, self.one]), 1)

    def pieces(self):
        n = self.units.shape[0]
        index = [(0, u, self.outer + u, 0, 0) for u in range(n)]
        index += [(1, u, self.outer + u, 1, 0) for u in range(n)]
        index += [(2, a * n + u, self.outer + u, a, 1) for a in range(2) for u in range(n)]
        return [self.units, self.one, self.two], index


def joined(spreads):
    arrays, index = [], []
    for s in spreads:
        more, at = s.pieces()
        index += [(i + len(arrays), *rest) for i, *rest in at]
        arrays += more
    return arrays, index


def put_units(index, moves, where_ref, ins, outs, each=None):
    dp = where_ref[0]
    for parity in range(2):

        @pl.when(where_ref[1] == parity)
        def _():
            for array, unit, outer, first, second in index:
                rx, ry = (second, first) if parity else (first, second)
                to = jnp.bitwise_xor(dp, 2 * outer + ry)
                for lead, rows, col, cols, target, at in moves:
                    value = ins[array][(unit, *lead, slice(0, rows), slice(col, col + cols))]
                    outs[target][pl.ds(pl.multiple_of(to * rows, 16), rows), at[rx] : at[rx] + cols] = value
                if each is not None:
                    each(ins[array], unit, to, rx)


def prepare_kernel(piece, dp_ref, qkv_ref, out_ref, up_ref, down_ref, qv_ref, *refs):
    vectors, (a_ref, bc_ref, row_ref) = refs[:-3], refs[-3:]
    part = qkv_ref.shape[2]
    for j in range(3):
        a_ref[:piece, j * part : (j + 1) * part] = qkv_ref[j]
    a_ref[:piece, 3 * part :] = out_ref[...].T
    row_ref[...] = jnp.zeros_like(row_ref)
    at = 0
    for v in vectors:
        n = v.shape[1]
        row_ref[0:1, at : at + n] = v[...].astype(F32)
        at += n
    n = qv_ref.shape[1]
    lane = lax.broadcasted_iota(jnp.int32, (n, part), 1)
    spot = (lane == lax.broadcasted_iota(jnp.int32, (n, part), 0) + n * dp_ref[0]).astype(BF16)
    both = dot_nn(qv_ref[...], spot)
    row_ref[1:2, :part] = both[0:1]
    row_ref[1:2, part : 2 * part] = both[1:2]
    exact = row_ref[0:1, :]
    high = exact.astype(BF16).astype(F32)
    middle = (exact - high).astype(BF16).astype(F32)
    low = exact - high - middle
    line = lax.broadcasted_iota(jnp.int32, (8, 1), 0)
    rows = jnp.where(line == 0, high, 0.0) + jnp.where(line == 1, middle, 0.0)
    rows += jnp.where(line == 2, low, 0.0) + jnp.where(line == 3, row_ref[1:2, :], 0.0)
    a_ref[piece:, :] = rows.astype(BF16)
    bc_ref[0] = up_ref[...]
    bc_ref[1] = down_ref[...].T


def prepare(w_qkv, w_out, w_up, w_down, b_qv, vectors):
    piece, part = w_qkv.shape[1:]
    model = w_up.shape[1]
    dp = lax.axis_index("dp").astype(jnp.int32)
    if piece % 16 == 0:

        def whole(s):
            return pl.BlockSpec(s, lambda i, d: (0,) * len(s))

        given = [w_qkv, w_out, w_up, w_down, b_qv, *[v[None] for v in vectors]]
        shapes = [(piece + 8, model), (2, piece, model)]
        return pl.pallas_call(
            functools.partial(prepare_kernel, piece),
            grid_spec=pltpu.PrefetchScalarGridSpec(
                num_scalar_prefetch=1,
                grid=(1,),
                in_specs=[whole(v.shape) for v in given],
                out_specs=[whole(s) for s in shapes],
                scratch_shapes=[pltpu.VMEM((8, model), F32)],
            ),
            out_shape=[jax.ShapeDtypeStruct(s, BF16) for s in shapes],
            cost_estimate=CHEAP,
            name="prepare_units",
        )(dp[None], *given)
    row = jnp.concatenate([v.astype(F32) for v in vectors])
    row = jnp.pad(row, (0, model - row.shape[0]))
    high = row.astype(BF16)
    middle = (row - high.astype(F32)).astype(BF16)
    low = (row - high.astype(F32) - middle.astype(F32)).astype(BF16)
    keep = lax.broadcasted_iota(jnp.int32, (1, part // b_qv.shape[1], 1), 1) == dp
    spot = jnp.where(keep, b_qv[:, None, :], jnp.zeros((), BF16)).reshape(-1)
    spot = jnp.pad(spot, (0, model - spot.shape[0]))
    tail = jnp.pad(jnp.stack([high, middle, low, spot]), ((0, 4), (0, 0)))
    unit = jnp.concatenate([w_qkv[0], w_qkv[1], w_qkv[2], w_out.T], axis=1)
    return jnp.concatenate([unit, tail], axis=0), jnp.stack([w_up, w_down.T])


def project_kernel(index, moves, piece, part, halves, where_ref, own_ref, other_ref, *refs):
    ins, (out_ref, w_ref, o_ref, ext_ref, bias_ref) = refs[:-5], refs[-5:]
    width = 2 * part

    @pl.when(pl.program_id(0) == 0)
    def _():
        bias_ref[...] = jnp.zeros_like(bias_ref)

        def each(source, unit, to, rx):
            value = source[unit, piece:, : 2 * part]
            ext_ref[to, :, 2 * part * rx : 2 * part * (rx + 1)] = value
            value = value.astype(F32)[3:4]
            bias_ref[0:1, rx * part : (rx + 1) * part] += value[:, :part]
            at = 2 * width + rx * part
            bias_ref[0:1, at : at + part] += value[:, part:]

        put_units(index, moves, where_ref, ins, (w_ref, o_ref), each)

    x = either(pl.program_id(0), halves, own_ref, other_ref)
    out_ref[...] = (dot_nn(x, w_ref[...]) + bias_ref[0:1, :]).astype(BF16)


def feed_kernel(index, moves, halves, where_ref, own_ref, other_ref, bias_ref, *refs):
    ins, (hidden_ref, slope_ref, keep_ref, send_ref, b_ref, c_ref) = refs[:-6], refs[-6:]
    step = pl.program_id(0)

    @pl.when(step == 0)
    def _():
        put_units(index, moves, where_ref, ins, (b_ref, c_ref))

    x = either(step, halves, own_ref, other_ref)
    hidden, slope = gelu_both(dot_nn(x, b_ref[...]) + bias_ref[...])
    hidden_ref[...] = hidden
    slope_ref[...] = slope
    part = dot_nt(hidden, c_ref[...])

    @pl.when(step < halves)
    def _():
        keep_ref[...] = part

    @pl.when(step >= halves)
    def _():
        send_ref[...] = part.astype(BF16)


def chunks(n, size=512):
    return [slice(at, min(at + size, n)) for at in range(0, n, size)]


def gelu_both(up):
    cdf = 0.5 * (1.0 + lax.erf(up * ROOT_HALF))
    slope = cdf + up * (jnp.exp(-0.5 * up * up) * INV_ROOT_TWO_PI)
    return (up * cdf).astype(BF16), slope.astype(BF16)


def feed_back_kernel(size, piece, where_ref, *refs):
    own_ref, other_ref, n_own_ref, n_other_ref, slope_ref, hidden_ref, c_ref, b_ref = refs[:8]
    keep_ref, send_ref, sum_ref, c_keep, c_send, b_keep, b_send = refs[8:15]
    d_ref, d_turned, n_turned, acc_ref, c_grad, b_grad = refs[15:]
    step, dp = pl.program_id(0), where_ref[0]
    half, model = own_ref.shape
    outer = c_keep.shape[0] // 2

    @pl.when(step == 0)
    def _():
        for at, d, n in ((0, own_ref, n_own_ref), (half, other_ref, n_other_ref)):
            d_ref[at : at + half, :] = d[...]
            d_turned[:, at : at + half] = d[...].T
            n_turned[:, at : at + half] = n[...].T

    d_up = (dot_nn(d_ref[...], c_ref[...]) * slope_ref[...].astype(F32)).astype(BF16)
    sum_ref[...] = jnp.sum(d_up.astype(F32), axis=0, keepdims=True)
    part = dot_nt(d_up, b_ref[...])

    @pl.when(step == 0)
    def _():
        acc_ref[...] = part

    @pl.when(step > 0)
    def _():
        acc_ref[...] += part

    c_grad[...] = dot_nn(d_turned[...], hidden_ref[...]).astype(BF16)
    b_grad[...] = dot_nn(n_turned[...], d_up).astype(BF16)
    width = c_ref.shape[1]
    for s in range(2 * model // width):
        for at in range(0, width, size):
            rx, to = divmod(s * width + at, model)
            for parity in range(2):

                @pl.when((step == s) & (where_ref[1] == parity))
                def _():
                    for ry in range(2):
                        first, second = (ry, rx) if parity else (rx, ry)
                        outs = ((c_send, b_send) if first else (c_keep, b_keep))

                        def move(z, carry):
                            rows = pl.ds(pl.multiple_of(jnp.bitwise_xor(dp, 2 * z + ry) * piece, 16), piece)
                            for out, grad in zip(outs, (c_grad, b_grad)):
                                out[second * outer + z, :, to : to + size] = grad[rows, at : at + size]
                            return carry

                        lax.fori_loop(0, outer, move, 0)

    @pl.when(step == pl.num_programs(0) - 1)
    def _():
        keep_ref[...] = acc_ref[:half, :]
        send_ref[...] = acc_ref[half:, :].astype(BF16)


def feed_back(d_own, d_other, n_own, n_other, slope, hidden, c, b, piece):
    rows, model = d_own.shape
    wide = b.shape[1]
    ndp = model // piece
    if piece % 16:
        d, n = jnp.concatenate([d_own, d_other]), jnp.concatenate([n_own, n_other])
        d_up = (dot_nn(d, c) * slope.astype(F32)).astype(BF16)
        part = dot_nt(d_up, b)
        sums = jnp.sum(d_up.astype(F32), axis=0, keepdims=True)
        wide_part = [((0, 1), 2, model, 0, True)]
        c_pair = summed([d_own, d_other, hidden], wide_part)
        b_pair = summed([n_own, n_other, d_up], wide_part)
        return part[:rows], part[rows:].astype(BF16), sums, *c_pair, *b_pair

    def whole(s):
        return pl.BlockSpec(s, lambda i, w: (0,) * len(s))

    def columns(n):
        return pl.BlockSpec((n, 512), lambda i, w: (0, i))

    units = (ndp, piece, model)
    return pl.pallas_call(
        functools.partial(feed_back_kernel, 256, piece),
        grid_spec=pltpu.PrefetchScalarGridSpec(
            num_scalar_prefetch=1,
            grid=(wide // 512,),
            in_specs=[whole((rows, model))] * 4 + [columns(2 * rows)] * 2 + [columns(model)] * 2,
            out_specs=[whole((rows, model))] * 2 + [columns(1)] + [whole(units)] * 4,
            scratch_shapes=[
                pltpu.VMEM((2 * rows, model), BF16),
                pltpu.VMEM((model, 2 * rows), BF16),
                pltpu.VMEM((model, 2 * rows), BF16),
                pltpu.VMEM((2 * rows, model), F32),
                pltpu.VMEM((model, 512), BF16),
                pltpu.VMEM((model, 512), BF16),
            ],
        ),
        out_shape=[
            jax.ShapeDtypeStruct((rows, model), F32),
            jax.ShapeDtypeStruct((rows, model), BF16),
            jax.ShapeDtypeStruct((1, wide), F32),
        ]
        + [jax.ShapeDtypeStruct(units, BF16)] * 4,
        cost_estimate=CHEAP,
        name="feed_back",
    )(where(), d_own, d_other, n_own, n_other, slope, hidden, c, b)


def ordered(spreads, moves):
    arrays, index = joined(spreads)
    order = jnp.bitwise_xor(jnp.arange(lax.axis_size("dp")), lax.axis_index("dp"))
    made = {}
    for lead, rows, col, cols, target, at in moves:
        for rx in range(2):
            both = []
            for swapped in range(2):
                units = {}
                for array, unit, outer, first, second in index:
                    x, y = (second, first) if swapped else (first, second)
                    if x == rx:
                        units[2 * outer + y] = arrays[array][(unit, *lead)][rows, col : col + cols]
                both.append(jnp.stack([units[k] for k in sorted(units)]))
            stack = jnp.take(jnp.where(lax.axis_index("c") == 0, both[0], both[1]), order, axis=0)
            made.setdefault(target, []).append((at[rx], stack))
    return [jnp.concatenate([m for _, m in sorted(made[t], key=lambda p: p[0])], axis=-1) for t in sorted(made)]


def project(spreads, own, other, piece, part, block):
    width = 2 * part
    rows, model = own.shape
    halves = rows // block
    moves = [((), piece, j * part, part, 0, (j * width, j * width + part)) for j in range(3)]
    moves.append(((), piece, 3 * part, part, 1, (0, part)))
    if piece % 16 == 0:
        arrays, index = joined(spreads)

        def whole(s):
            return pl.BlockSpec(s, lambda i, d: (0,) * len(s))

        shapes = [(model, 3 * width), (model, width), (model // piece, 8, 2 * width)]
        return pl.pallas_call(
            functools.partial(project_kernel, index, moves, piece, part, halves),
            grid_spec=pltpu.PrefetchScalarGridSpec(
                num_scalar_prefetch=1,
                grid=(2 * halves,),
                in_specs=split_specs(block, model, halves) + [whole(a.shape) for a in arrays],
                out_specs=[pl.BlockSpec((block, 3 * width), lambda i, d: (i, 0))] + [whole(s) for s in shapes],
                scratch_shapes=[pltpu.VMEM((8, 3 * width), F32)],
            ),
            out_shape=[jax.ShapeDtypeStruct(s, BF16) for s in [(2 * rows, 3 * width), *shapes]],
            cost_estimate=CHEAP,
            name="project_kernel",
        )(where(), own, other, *arrays)
    slices = [(lead, slice(0, n), *rest) for lead, n, *rest in moves]
    slices.append(((), slice(piece, piece + 8), 0, 2 * part, 2, (0, 2 * part)))
    w, o, ext = ordered(spreads, slices)
    bias = jnp.sum(ext[:, 3].astype(F32), axis=0).reshape(2, 2, part)
    bias = jnp.concatenate([bias[:, 0].reshape(-1), jnp.zeros((width,), F32), bias[:, 1].reshape(-1)])
    w, o = w.reshape(model, -1), o.reshape(model, -1)
    return (dot_nn(jnp.concatenate([own, other]), w) + bias[None]).astype(BF16), w, o, ext


def feed(spreads, own, other, bias, piece, block):
    rows, model = own.shape
    halves = rows // block
    moves = [((k,), piece, 0, model, k, (0, model)) for k in range(2)]
    if piece % 16 == 0:
        arrays, index = joined(spreads)

        def whole(s):
            return pl.BlockSpec(s, lambda i, d: (0,) * len(s))

        wide = pl.BlockSpec((block, 2 * model), lambda i, d: (i, 0))
        return pl.pallas_call(
            functools.partial(feed_kernel, index, moves, halves),
            grid_spec=pltpu.PrefetchScalarGridSpec(
                num_scalar_prefetch=1,
                grid=(2 * halves,),
                in_specs=split_specs(block, model, halves) + [whole(a.shape) for a in [bias, *arrays]],
                out_specs=[wide, wide, *split_specs(block, model, halves)] + [whole((model, 2 * model))] * 2,
            ),
            out_shape=[jax.ShapeDtypeStruct((2 * rows, 2 * model), BF16)] * 2
            + [jax.ShapeDtypeStruct((rows, model), F32), jax.ShapeDtypeStruct((rows, model), BF16)]
            + [jax.ShapeDtypeStruct((model, 2 * model), BF16)] * 2,
            cost_estimate=CHEAP,
            name="feed_kernel",
        )(where(), own, other, bias, *arrays)
    b, c = ordered(spreads, [(lead, slice(0, n), *rest) for lead, n, *rest in moves])
    b, c = b.reshape(model, -1), c.reshape(model, -1)
    hidden, slope = gelu_both(dot_nn(jnp.concatenate([own, other]), b) + bias)
    part = dot_nt(hidden, c)
    return hidden, slope, part[:rows], part[rows:].astype(BF16), b, c


def pull(own, other, slope, c, b, block):
    rows, model = own.shape
    wide = b.shape[1]
    halves = rows // block

    def whole(s):
        return pl.BlockSpec(s, lambda i: (0, 0))

    by_row = pl.BlockSpec((block, wide), lambda i: (i, 0))
    return pl.pallas_call(
        functools.partial(pull_kernel, halves),
        grid=(2 * halves,),
        in_specs=[*split_specs(block, model, halves), by_row, whole(c.shape), whole(b.shape)],
        out_specs=[by_row, *split_specs(block, model, halves), whole((1, wide))],
        out_shape=[
            jax.ShapeDtypeStruct((2 * rows, wide), BF16),
            jax.ShapeDtypeStruct((rows, model), F32),
            jax.ShapeDtypeStruct((rows, model), BF16),
            jax.ShapeDtypeStruct((1, wide), F32),
        ],
        cost_estimate=CHEAP,
        name="pull_kernel",
    )(own, other, slope, c, b)


def where():
    return jnp.stack([lax.axis_index("dp"), lax.axis_index("c")]).astype(jnp.int32)


def sum_kernel(parts, piece, extra, part, where_ref, *refs):
    count = 1 + max(max(*p[0], p[1]) for p in parts)
    ins = refs[:count]
    scratch = refs[count + (2 if extra else 0) :]
    outs, left_ref, acc, ext_ref = scratch[:2], scratch[2], scratch[3], scratch[4]
    dp, step = where_ref[0], pl.program_id(0)
    outer = outs[0].shape[0] // 2
    blocked = parts[0][4]
    if extra:
        lines_ref, bias_ref = refs[count : count + 2]
        ext_ref[...] = lines_ref[...].astype(F32)
        for rx in range(2):
            for k in range(2):
                ext_ref[rx, extra - 1 : extra, k * part : (k + 1) * part] = bias_ref[
                    0:1, (2 * k + rx) * part : (2 * k + rx + 1) * part
                ]

    def turned(own, other):
        half = ins[own].shape[0]
        left_ref[:, :half] = ins[own][...].T
        left_ref[:, half:] = ins[other][...].T

    for k, ((own, other), right, width, at, by_block) in enumerate(parts):
        if by_block:

            @pl.when(step == 0)
            def _():
                turned(own, other)

            for lanes in chunks(width, 256):
                acc[:, lanes] = dot_nn(left_ref[...], ins[right][:, lanes]).astype(BF16)
        else:

            @pl.when(step == 0)
            def _():
                if k == 0 or parts[k - 1][0] != (own, other):
                    turned(own, other)
                for j in range(ins[right].shape[1] // (2 * width)):
                    both = dot_nn(left_ref[...], ins[right][:, 2 * j * width : 2 * (j + 1) * width]).astype(BF16)
                    for rx in range(2):
                        lanes = slice(rx * acc.shape[1] // 2 + at + j * width, rx * acc.shape[1] // 2 + at + (j + 1) * width)
                        acc[:, lanes] = both[:, rx * width : (rx + 1) * width]

    span = outs[0].shape[2]

    def put(rx):
        lanes = slice(0, span) if blocked else slice(rx * span, (rx + 1) * span)
        for parity in range(2):

            @pl.when(where_ref[1] == parity)
            def _():
                for ry in range(2):
                    first, second = (ry, rx) if parity else (rx, ry)

                    def move(z, carry):
                        rows = pl.ds(pl.multiple_of(jnp.bitwise_xor(dp, 2 * z + ry) * piece, 16), piece)
                        outs[first][second * outer + z, :piece, :] = acc[rows, lanes]
                        if extra:
                            outs[first][second * outer + z, piece:, :] = ext_ref[rx].astype(BF16)
                        return carry

                    lax.fori_loop(0, outer, move, 0)

    for rx in range(2):
        if blocked:
            pl.when(step == rx)(functools.partial(put, rx))
        else:
            put(rx)


def summed(arrays, parts, ext=None, bias=None):
    ndp = lax.axis_size("dp")
    model = arrays[0].shape[1]
    piece = model // ndp
    blocked = parts[0][4]
    width = sum(p[2] if p[4] else arrays[p[1]].shape[1] // 2 for p in parts)
    extra = 0 if ext is None else ext.shape[1]
    if piece % 16 == 0:

        def whole(s):
            return pl.BlockSpec(s, lambda i, d: (0,) * len(s))

        given = list(arrays) + ([] if ext is None else [ext, bias])
        specs = [whole(a.shape) for a in given]
        if blocked:
            right = parts[0][1]
            specs[right] = pl.BlockSpec((arrays[right].shape[0], width), lambda i, d: (0, i))
        shape = (ndp, piece + extra, width)
        return pl.pallas_call(
            functools.partial(sum_kernel, parts, piece, extra, 0 if bias is None else bias.shape[1] // 4),
            grid_spec=pltpu.PrefetchScalarGridSpec(
                num_scalar_prefetch=1,
                grid=(2 if blocked else 1,),
                in_specs=specs,
                out_specs=[whole(shape)] * 2,
                scratch_shapes=[
                    pltpu.VMEM((model, 2 * arrays[0].shape[0]), BF16),
                    pltpu.VMEM((model, width if blocked else 2 * width), BF16),
                    pltpu.VMEM((2, max(extra, 8), width), F32),
                ],
            ),
            out_shape=[jax.ShapeDtypeStruct(shape, BF16)] * 2,
            cost_estimate=CHEAP,
            name="sum_units",
        )(where(), *given)
    order = jnp.bitwise_xor(jnp.arange(ndp), lax.axis_index("dp"))
    sides = []
    if extra:
        line = jnp.transpose(bias.reshape(2, 2, -1), (1, 0, 2)).reshape(2, -1)
        line = jnp.pad(line, ((0, 0), (0, width - line.shape[1]))).astype(BF16)
        ext = jnp.concatenate([ext[:, :-1], line[:, None]], axis=1)
    for rx in range(2):
        g = []
        for (own, other), right, cols, _, by_block in parts:
            left = jnp.concatenate([arrays[own], arrays[other]])
            for j in range(1 if by_block else arrays[right].shape[1] // (2 * cols)):
                at = (2 * j + rx) * cols
                g.append(dot_tn(left, arrays[right][:, at : at + cols]).astype(BF16))
        g = jnp.concatenate(g, axis=1).reshape(ndp, piece, width)
        if extra:
            g = jnp.concatenate([g, jnp.broadcast_to(ext[rx][None], (ndp, extra, width))], axis=1)
        g = jnp.take(g, order, axis=0).reshape(ndp // 2, 2, piece + extra, width)
        sides.append(jnp.moveaxis(g, 1, 0))
    g = jnp.stack(sides)
    g = jnp.where(lax.axis_index("c") == 0, g, jnp.swapaxes(g, 0, 1))
    return g[0].reshape(ndp, piece + extra, width), g[1].reshape(ndp, piece + extra, width)


class Scatter:
    def __init__(self, pair):
        self.keep, self.send = pair

    def first(self):
        self.one = turn(self.send, 0)

    def second(self):
        half = self.keep.shape[0] // 2
        self.kept = add(self.keep[:half], self.one[:half])
        self.two = turn(add(self.keep[half:], self.one[half:]), 1)

    def third(self):
        total = add(self.kept, self.two)
        outer = total.shape[0]
        if outer <= 4:
            self.last = [total[0]]
            self.three = [flip(total[k], "dp", 2 * k) for k in range(1, outer)]
            return
        for k in reversed(range(outer_bits())):
            half = total.shape[0] // 2
            total = add(total[:half], flip(total[half:], "dp", 2 << k))
        self.last, self.three = [total[0]], []

    def result(self):
        return sum(t.astype(F32) for t in self.last + self.three)


def local(
    tokens, grad_out, seg_ids, w_qkv, b_qv, w_out, w_up, b_up, w_down, b_out, b_down, g_one, s_one, g_two, s_two
):
    ndp = lax.axis_size("dp")
    nx = lax.axis_size("x")
    parity = lax.axis_index("c")
    which = lax.axis_index("x")
    place_dp = lax.axis_index("dp")
    rows, model = tokens.shape
    piece = model // ndp
    part = w_qkv.shape[2]
    width = nx * part
    slim = model // (ndp * nx * 2)
    qv = part // ndp
    extra = 8
    block = 256
    tall = 512

    unit_a, unit_bc = prepare(
        w_qkv, w_out, w_up, w_down, b_qv, [b_out, b_down, g_one, s_one, g_two, s_two, b_up]
    )
    a_near = Spread(jnp.stack([unit_a, flip(unit_a, "dp", 2)]), 0)

    class Box:
        pass

    box = Box()
    box.bc = unit_bc
    a_near.units = stage("z1", a_near.units, bc=(box, "bc"))
    a_far = Spread(gather_far(a_near.units), 2)
    a_near.first()
    a_near.one = stage("n1", a_near.one, bc=(box, "bc"), az=(a_far, "units"))
    a_near.second()
    a_far.units = stage("z2", a_far.units, bc=(box, "bc"), an2=(a_near, "two"))
    a_far.first()
    bc_near = Spread(jnp.stack([box.bc, flip(box.bc, "dp", 2)]), 0)
    a_far.one = stage("f1", a_far.one, bz1=(bc_near, "units"), an2=(a_near, "two"))
    a_far.second()
    bc_far = Spread(gather_far(bc_near.units), 2)
    bc_items = lambda: dict(bn1=(bc_near, "one"), bz2=(bc_far, "units"), bn2=(bc_near, "two"), bf1=(bc_far, "one"), bf2=(bc_far, "two"))
    done = set()

    def advance(name, *values):
        res = stage(name, *values, **{k: v for k, v in bc_items().items() if hasattr(*v)})
        order = ["z2", "f1", "f2", "qkv", "ctx", "attn", "normed", "feed"]
        at = order.index(name)
        ready = lambda k: k is None or order.index(OPT.get(k, "feed")) <= at
        if "n1" not in done and order.index(OPT.get("rn1", "z2")) <= at:
            bc_near.first()
            done.add("n1")
        if "n2" not in done and "n1" in done and (ready("bn1") or name == "feed"):
            bc_near.second()
            done.add("n2")
        if "f1" not in done and (ready("bz2") or name == "feed"):
            bc_far.first()
            done.add("f1")
        if "f2" not in done and "f1" in done and (ready("bf1") or name == "feed"):
            bc_far.second()
            done.add("f2")
        return res

    advance("z2")
    a_far.two = advance("f2", a_far.two)

    seg = lax.dynamic_index_in_dim(seg_ids, which, 0, keepdims=False).reshape(2, rows)
    seg_rel = jnp.concatenate(
        [
            lax.dynamic_index_in_dim(seg, parity, 0, keepdims=False),
            lax.dynamic_index_in_dim(seg, 1 - parity, 0, keepdims=False),
        ]
    )
    seg_col = seg_rel[:, None]
    seg_row = seg_rel[None, :]
    x_other = swap(tokens)

    qkv, w_all, o_t, ext = project([a_near, a_far], tokens, x_other, piece, part, block)
    ext = ext[:, :3].astype(F32)
    ext = (ext[:, 0] + ext[:, 1] + ext[:, 2]).reshape(ndp, nx, 2 * part)
    bias_up = jnp.transpose(ext[:, :, 6 * slim : 6 * slim + piece], (1, 0, 2)).reshape(1, nx * model)
    six = ext[:, :, : 6 * slim]
    six = jnp.stack([six, swap(six)], axis=2)
    six = jnp.where(lax.broadcasted_iota(jnp.int32, (1, 1, 2, 1), 2) == parity, six[:, :, :1], six[:, :, 1:])
    six = jnp.where(which == 0, six, six[:, ::-1]).reshape(ndp * nx * 2, 6, slim)
    vectors = jnp.transpose(six, (1, 0, 2)).reshape(6, model)
    bout_f, bdown_f, gone_f, sone_f, gtwo_f, stwo_f = [vectors[i : i + 1] for i in range(6)]

    qkv = advance("qkv", qkv)
    ctx, lse = attention_forward(qkv, seg_col, seg_row, tall, 0, 2 * rows // tall, ())
    ctx = advance("ctx", ctx)
    attn_send = dot_nt(ctx[rows:], o_t).astype(BF16)
    attn = dot_nt(ctx[:rows], o_t) + swap(attn_send).astype(F32)
    attn = advance("attn", attn)
    first = tokens.astype(F32) + attn + bout_f
    hat_one, inv_one = normalize(first)
    normed = hat_one * gone_f + sone_f
    normed_low = advance("normed", normed.astype(BF16))
    normed_other = swap(normed_low)
    normed_other = advance("feed", normed_other)
    hidden, slope, keep, send, b_all, c_all = feed([bc_near, bc_far], normed_low, normed_other, bias_up, piece, block)
    branch = keep + swap(send).astype(F32)
    second = normed + branch + bdown_f
    hat_two, inv_two = normalize(second)
    layer_out = (hat_two * gtwo_f + stwo_f).astype(BF16)

    g_in = grad_out.astype(F32)
    d_gain_two = jnp.sum(g_in * hat_two, axis=0)
    d_shift_two = jnp.sum(g_in, axis=0)
    d_second = normalize_back(hat_two, inv_two, gtwo_f, g_in)
    d_branch = d_second.astype(BF16)
    d_bias_down = jnp.sum(d_branch.astype(F32), axis=0)
    db_other = swap(d_branch)

    sc = sb = sa = None
    order = ["P0", "P1", "P2", "P3", "P4", "P5", "P6", "P7"]
    sent = set()

    def go(name, *values):
        items = {}
        for k, s in (("c", sc), ("b", sb)):
            if s is not None:
                for n, f in (("1", "one"), ("2", "two"), ("3", "three")):
                    if hasattr(s, f):
                        items[k + n] = (s, f)
        res = stage(name, *values, **items)
        at = order.index(name)
        for k, s in (("c", sc), ("b", sb)):
            if s is None:
                continue
            for n, need, f in ((1, None, "first"), (2, "1", "second"), (3, "2", "third")):
                if k + str(n) in sent or (n > 1 and k + str(n - 1) not in sent):
                    continue
                if n == 1 or order.index(OPT.get(k + need, "P7")) <= at:
                    getattr(s, f)()
                    sent.add(k + str(n))
        return res

    keep, send, d_bias_up, *pairs = feed_back(
        d_branch, db_other, normed_low, normed_other, slope, hidden, c_all, b_all, piece
    )
    sc, sb = Scatter(pairs[:2]), Scatter(pairs[2:])
    go("P0")
    d_normed = d_second + keep + swap(send).astype(F32)
    d_normed = go("P1", d_normed)
    d_gain_one = jnp.sum(d_normed * hat_one, axis=0)
    d_shift_one = jnp.sum(d_normed, axis=0)
    d_first = normalize_back(hat_one, inv_one, gone_f, d_normed)
    d_attn = d_first.astype(BF16)
    d_bias_out = jnp.sum(d_attn.astype(F32), axis=0)
    da_other = swap(d_attn)
    d_ctx = dot_nn(d_attn, o_t).astype(BF16)
    sums = jnp.stack([d_bias_out, d_bias_down, d_gain_one, d_shift_one, d_gain_two, d_shift_two])
    sums = sums + swap(sums)
    d_ctx_other = dot_nn(da_other, o_t).astype(BF16)
    spread = jnp.concatenate([d_bias_up.reshape(nx, model), jnp.broadcast_to(sums.reshape(1, -1), (nx, 6 * model))], axis=1)
    spread = jnp.pad(spread.reshape(nx, 7, model), ((0, 0), (0, 1), (0, 0))).astype(BF16)
    d_ctx_other, spread = go("P2", d_ctx_other, spread)
    d_qkv, bias = attention_backward(qkv, ctx, lse, d_ctx, d_ctx_other, seg_col, seg_row, block)
    d_qkv = go("P3", d_qkv)
    attention_parts = [((0, 1), 2, part, 0, False), ((3, 4), 5, part, 3 * part, False)]
    given = [tokens, x_other, d_qkv, d_attn, da_other, ctx]
    sa = Scatter(summed(given, attention_parts, spread, bias))
    d_qkv, sa.send = go("P4", d_qkv, sa.send)
    sa.first()
    keep, send = input_gradient(d_qkv, d_first, w_all, block)
    sa.one, keep, send = go("P5", sa.one, keep, send)
    sa.second()
    input_grad = keep + swap(send).astype(F32)
    sa.two, input_grad = go("P6", sa.two, input_grad)
    sa.third()
    go("P7")
    input_grad = input_grad.astype(BF16)
    gc = sc.result()
    gb = sb.result()
    ga = sa.result()
    g_qkv = jnp.stack([ga[:piece, j * part : (j + 1) * part] for j in range(3)])
    tail = ga[piece:]
    g_bqv = lax.dynamic_slice_in_dim(tail[7, : 2 * part].reshape(2, part), place_dp * qv, qv, axis=1)
    g_bup = lax.dynamic_slice_in_dim(tail[0], place_dp * piece, piece)
    six = lax.dynamic_slice_in_dim(tail[1:7], ((place_dp * nx + which) * 2 + parity) * slim, slim, axis=1)
    return (
        layer_out,
        input_grad,
        g_qkv,
        g_bqv,
        ga[:piece, 3 * part :].T,
        gb,
        g_bup,
        gc.T,
        *[six[i] for i in range(6)],
    )


def solution(mesh):
    ndp, nt = mesh.devices.shape
    fine = Mesh(mesh.devices.reshape(ndp, nt // 2, 2), ("dp", "x", "c"))
    tensor = ("x", "c")
    every = ("dp", "x", "c")
    row = P(every, None)
    vec = P(every)
    return jax.shard_map(
        local,
        mesh=fine,
        in_specs=(
            row,
            row,
            P("dp", None),
            P(None, "dp", tensor),
            P(None, ("x", "c", "dp")),
            P(tensor, "dp"),
            P("dp", tensor),
            P(("x", "c", "dp")),
            P(tensor, "dp"),
            vec,
            vec,
            vec,
            vec,
            vec,
            vec,
        ),
        out_specs=(
            row,
            row,
            P(None, "dp", tensor),
            P(None, ("x", "c", "dp")),
            P(tensor, "dp"),
            P("dp", tensor),
            P(("x", "c", "dp")),
            P(tensor, "dp"),
            vec,
            vec,
            vec,
            vec,
            vec,
            vec,
        ),
        check_vma=False,
    )
```

```python
import functools

import jax
import jax.numpy as jnp
from jax import lax
from jax.experimental import pallas as pl
from jax.experimental.pallas import tpu as pltpu
from jax.sharding import Mesh, PartitionSpec as P

HD = 64
LANES = 128
EPSILON = 1e-05
ROOT_HALF = 0.7071067811865476
INV_ROOT_TWO_PI = 0.3989422804014327
F32 = jnp.float32
BF16 = jnp.bfloat16


def dot(a, b, dims):
    return lax.dot_general(a, b, (dims, ((), ())), preferred_element_type=F32)


def dot_nn(a, b):
    return dot(a, b, ((1,), (0,)))


def dot_nt(a, b):
    return dot(a, b, ((1,), (1,)))


def dot_tn(a, b):
    return dot(a, b, ((0,), (0,)))


CHEAP = pl.CostEstimate(flops=1000, bytes_accessed=1000, transcendentals=0)


def attention_forward_kernel(width, seg_q_ref, seg_k_ref, q_ref, k_ref, v_ref, *refs):
    ctx_ref, lse_ref = refs[-2:]
    lane = lax.broadcasted_iota(jnp.int32, (1, LANES), 1)
    bias = jnp.where(seg_q_ref[...] == seg_k_ref[...], 0.0, -1000000000.0)
    block = q_ref.shape[0]

    stats = jnp.zeros((block, LANES), F32)
    for tile in range(width // LANES):
        cols = slice(tile * LANES, (tile + 1) * LANES)
        q2 = q_ref[:, cols] * jnp.asarray(0.125, BF16)
        k2 = k_ref[:, cols]
        v2 = v_ref[:, cols]
        outs = []
        for half in range(2):
            qm = jnp.where((lane // HD) == half, q2, jnp.zeros_like(q2))
            s = dot_nt(qm, k2) + bias
            top = jnp.max(s, axis=-1, keepdims=True)
            e = jnp.exp(s - top)
            total = jnp.sum(e, axis=-1, keepdims=True)
            outs.append(dot_nn(e.astype(BF16), v2) * (1.0 / total))
            stats = jnp.where(lane == 2 * tile + half, top + jnp.log(total), stats)
        ctx_ref[:, cols] = jnp.where(lane < HD, outs[0], outs[1]).astype(BF16)
    lse_ref[...] = stats.T[: lse_ref.shape[0], :]


def attention_forward(qkv, seg_col, seg_row, block, first, count, made):
    rows, triple = qkv.shape
    width = triple // 3
    return pl.pallas_call(
        functools.partial(attention_forward_kernel, width),
        grid=(count,),
        in_specs=[
            pl.BlockSpec((block, 1), lambda i: (first + i, 0)),
            pl.BlockSpec((1, rows), lambda i: (0, 0)),
            pl.BlockSpec((block, width), lambda i: (first + i, 0)),
            pl.BlockSpec((rows, width), lambda i: (0, 1)),
            pl.BlockSpec((rows, width), lambda i: (0, 2)),
        ]
        + [pl.BlockSpec(memory_space=pl.ANY)] * len(made),
        out_specs=[
            pl.BlockSpec((block, width), lambda i: (first + i, 0)),
            pl.BlockSpec((8, block), lambda i: (0, first + i)),
        ],
        out_shape=[
            jax.ShapeDtypeStruct((rows, width), BF16),
            jax.ShapeDtypeStruct((8, rows), F32),
        ],
        input_output_aliases={5 + i: i for i in range(len(made))},
        cost_estimate=CHEAP,
        compiler_params=pltpu.CompilerParams(vmem_limit_bytes=30 * 1024 * 1024),
        name="attention_forward",
    )(seg_col, seg_row, qkv, qkv, qkv, *made)


def split_specs(block, columns, halves):
    return [
        pl.BlockSpec((block, columns), lambda i, *_: (jnp.minimum(i, halves - 1), 0)),
        pl.BlockSpec((block, columns), lambda i, *_: (jnp.maximum(i - halves, 0), 0)),
    ]


def either(step, halves, own_ref, other_ref):
    return jnp.where(step < halves, own_ref[...], other_ref[...])


def attention_backward_kernel(
    width, halves, seg_k_ref, seg_q_ref, q_ref, k_ref, v_ref, ctx_ref, lse_ref, own_ref, other_ref, out_ref, sum_ref, dk_ref, dv_ref
):
    step = pl.program_id(0)
    block = q_ref.shape[0]
    lane = lax.broadcasted_iota(jnp.int32, (1, LANES), 1)

    @pl.when(step == 0)
    def _():
        dk_ref[...] = jnp.zeros_like(dk_ref)
        dv_ref[...] = jnp.zeros_like(dv_ref)
        sum_ref[...] = jnp.zeros_like(sum_ref)

    bias = jnp.where(seg_k_ref[...] == seg_q_ref[...], 0.0, -1000000000.0)
    for pair in range(width // LANES):
        cols = slice(pair * LANES, (pair + 1) * LANES)
        q2 = q_ref[:, cols] * jnp.asarray(0.125, BF16)
        k2 = k_ref[:, cols]
        v2 = v_ref[:, cols]
        d2 = jnp.where(step < halves, own_ref[:, cols], other_ref[:, cols])
        prod = (d2.astype(F32) * ctx_ref[:, cols].astype(F32)).T
        kt = (k2 * jnp.asarray(0.125, BF16)).T
        row = lax.broadcasted_iota(jnp.int32, (LANES, 1), 0)
        dq = None
        dk = None
        dv = None
        for half in range(2):
            mine = (lane // HD) == half
            qm = jnp.where(mine, q2, jnp.zeros_like(q2))
            dm = jnp.where(mine, d2, jnp.zeros_like(d2))
            ktm = jnp.where((row // HD) == half, kt, jnp.zeros_like(kt))
            inner = jnp.sum(prod[half * HD : (half + 1) * HD, :], axis=0, keepdims=True)
            lse = lse_ref[2 * pair + half : 2 * pair + half + 1, :]
            p = jnp.exp(dot_nt(k2, qm) + bias - lse)
            dp = dot_nt(v2, dm)
            ds = (p * (dp - inner)).astype(BF16)
            dv_h = dot_nn(p.astype(BF16), dm)
            dk_h = dot_nn(ds, qm)
            dq_h = dot_nn(ktm, ds)
            dv = dv_h if dv is None else dv + dv_h
            dk = dk_h if dk is None else dk + dk_h
            dq = dq_h if dq is None else dq + dq_h
        dk_ref[:, cols] += dk
        dv_ref[:, cols] += dv
        dq = dq.T.astype(BF16)
        out_ref[pl.ds(pl.multiple_of(step * block, block), block), cols] = dq
        sum_ref[:, cols] += jnp.sum(dq.astype(F32), axis=0, keepdims=True)

    @pl.when(step == pl.num_programs(0) - 1)
    def _():
        out_ref[:, width : 2 * width] = dk_ref[...].astype(BF16)
        dv = dv_ref[...].astype(BF16)
        out_ref[:, 2 * width : 3 * width] = dv
        sum_ref[:, width : 2 * width] = jnp.sum(dv.astype(F32), axis=0, keepdims=True)


def attention_backward(qkv, ctx, lse, d_own, d_other, seg_col, seg_row, block):
    rows, triple = qkv.shape
    width = triple // 3
    halves = rows // block // 2
    return pl.pallas_call(
        functools.partial(attention_backward_kernel, width, halves),
        grid=(rows // block,),
        in_specs=[
            pl.BlockSpec((rows, 1), lambda i: (0, 0)),
            pl.BlockSpec((1, block), lambda i: (0, i)),
            pl.BlockSpec((block, width), lambda i: (i, 0)),
            pl.BlockSpec((rows, width), lambda i: (0, 1)),
            pl.BlockSpec((rows, width), lambda i: (0, 2)),
            pl.BlockSpec((block, width), lambda i: (i, 0)),
            pl.BlockSpec((8, block), lambda i: (0, i)),
            *split_specs(block, width, halves),
        ],
        out_specs=[pl.BlockSpec((rows, triple), lambda i: (0, 0)), pl.BlockSpec((1, 2 * width), lambda i: (0, 0))],
        out_shape=[jax.ShapeDtypeStruct((rows, triple), BF16), jax.ShapeDtypeStruct((1, 2 * width), F32)],
        scratch_shapes=[pltpu.VMEM((rows, width), F32), pltpu.VMEM((rows, width), F32)],
        cost_estimate=CHEAP,
        compiler_params=pltpu.CompilerParams(vmem_limit_bytes=30 * 1024 * 1024),
        name="attention_backward",
    )(seg_col, seg_row, qkv, qkv, qkv, ctx, lse, d_own, d_other)


def input_kernel(halves, d_ref, first_ref, w_ref, keep_ref, send_ref):
    step = pl.program_id(0)
    part = dot_nt(d_ref[...], w_ref[...])

    @pl.when(step < halves)
    def _():
        keep_ref[...] = first_ref[...] + part

    @pl.when(step >= halves)
    def _():
        send_ref[...] = part.astype(BF16)


def input_gradient(d_qkv, d_first, w_all, block):
    rows, model = d_first.shape
    width = d_qkv.shape[1]
    halves = rows // block
    by_row = pl.BlockSpec((block, width), lambda i: (i, 0))
    own = pl.BlockSpec((block, model), lambda i: (jnp.minimum(i, halves - 1), 0))
    return pl.pallas_call(
        functools.partial(input_kernel, halves),
        grid=(2 * halves,),
        in_specs=[by_row, own, pl.BlockSpec(w_all.shape, lambda i: (0, 0))],
        out_specs=split_specs(block, model, halves),
        out_shape=[jax.ShapeDtypeStruct((rows, model), F32), jax.ShapeDtypeStruct((rows, model), BF16)],
        cost_estimate=CHEAP,
        name="input_gradient",
    )(d_qkv, d_first, w_all)


def normalize(r):
    mean = jnp.mean(r, axis=-1, keepdims=True)
    cent = r - mean
    var = jnp.mean(cent * cent, axis=-1, keepdims=True)
    inv = lax.rsqrt(var + EPSILON)
    return cent * inv, inv


def normalize_back(hat, inv, gain, d_out):
    d_hat = d_out * gain
    first = jnp.mean(d_hat, axis=-1, keepdims=True)
    second = jnp.mean(d_hat * hat, axis=-1, keepdims=True)
    return inv * (d_hat - first - hat * second)


def swap(a):
    return lax.ppermute(a, "c", [(0, 1), (1, 0)])


def flip(a, axis, bit):
    n = lax.axis_size(axis)
    return lax.ppermute(a, axis, [(i, i ^ bit) for i in range(n)])


def turn(a, level):
    n, nx = lax.axis_size("dp"), lax.axis_size("x")
    pairs = []
    for d in range(n):
        for x in range(nx):
            for c in range(2):
                other = (d * nx + (x ^ 1)) if (c + level) % 2 == 0 else ((d ^ 1) * nx + x)
                pairs.append(((d * nx + x) * 2 + c, other * 2 + c))
    return lax.ppermute(a, ("dp", "x", "c"), pairs)


def tie(*values):
    return lax.optimization_barrier(values)


def add(*terms):
    return sum(t.astype(F32) for t in terms).astype(BF16)


def outer_bits():
    return lax.axis_size("dp").bit_length() - 2


def gather_far(near):
    parts = [near]
    for k in range(1, outer_bits()):
        held = jnp.concatenate(parts) if len(parts) > 1 else near
        parts.append(flip(held, "dp", 2 << k))
    return jnp.concatenate(parts[1:]) if len(parts) > 2 else parts[1]


OPT = {'bc': None, 'bn1': 'f2', 'bz2': 'qkv', 'bf1': 'ctx', 'bn2': 'ctx', 'bf2': 'attn', 'c1': 'P3', 'c2': 'P4', 'c3': 'P5', 'b1': 'P3', 'b2': 'P4', 'b3': 'P6', 'an2': 'f1', 'bz1': 'f1'}


def stage(name, *values, **items):
    keys = [k for k in items if OPT.get(k) == name]
    extra, spans = [], []
    for k in keys:
        v = getattr(*items[k])
        many = isinstance(v, list)
        spans.append((k, len(v) if many else 1, many))
        extra += v if many else [v]
    if len(values) + len(extra) > 1:
        out = list(tie(*values, *extra))
    else:
        out = [*values, *extra]
    res, at = out[: len(values)], len(values)
    for k, n, many in spans:
        setattr(*items[k], out[at : at + n] if many else out[at])
        at += n
    return res if len(res) > 1 else (res[0] if res else None)


class Spread:
    def __init__(self, units, outer):
        self.units, self.outer = units, outer

    def first(self):
        self.one = turn(self.units, 0)

    def second(self):
        self.two = turn(jnp.concatenate([self.units, self.one]), 1)

    def pieces(self):
        n = self.units.shape[0]
        index = [(0, u, self.outer + u, 0, 0) for u in range(n)]
        index += [(1, u, self.outer + u, 1, 0) for u in range(n)]
        index += [(2, a * n + u, self.outer + u, a, 1) for a in range(2) for u in range(n)]
        return [self.units, self.one, self.two], index


def joined(spreads):
    arrays, index = [], []
    for s in spreads:
        more, at = s.pieces()
        index += [(i + len(arrays), *rest) for i, *rest in at]
        arrays += more
    return arrays, index


def put_units(index, moves, where_ref, ins, outs, each=None):
    dp = where_ref[0]
    for parity in range(2):

        @pl.when(where_ref[1] == parity)
        def _():
            for array, unit, outer, first, second in index:
                rx, ry = (second, first) if parity else (first, second)
                to = jnp.bitwise_xor(dp, 2 * outer + ry)
                for lead, rows, col, cols, target, at in moves:
                    value = ins[array][(unit, *lead, slice(0, rows), slice(col, col + cols))]
                    outs[target][pl.ds(pl.multiple_of(to * rows, 16), rows), at[rx] : at[rx] + cols] = value
                if each is not None:
                    each(ins[array], unit, to, rx)


def prepare_kernel(piece, dp_ref, qkv_ref, out_ref, up_ref, down_ref, qv_ref, *refs):
    vectors, (a_ref, bc_ref, row_ref) = refs[:-3], refs[-3:]
    part = qkv_ref.shape[2]
    for j in range(3):
        a_ref[:piece, j * part : (j + 1) * part] = qkv_ref[j]
    a_ref[:piece, 3 * part :] = out_ref[...].T
    row_ref[...] = jnp.zeros_like(row_ref)
    at = 0
    for v in vectors:
        n = v.shape[1]
        row_ref[0:1, at : at + n] = v[...].astype(F32)
        at += n
    n = qv_ref.shape[1]
    lane = lax.broadcasted_iota(jnp.int32, (n, part), 1)
    spot = (lane == lax.broadcasted_iota(jnp.int32, (n, part), 0) + n * dp_ref[0]).astype(BF16)
    both = dot_nn(qv_ref[...], spot)
    row_ref[1:2, :part] = both[0:1]
    row_ref[1:2, part : 2 * part] = both[1:2]
    exact = row_ref[0:1, :]
    high = exact.astype(BF16).astype(F32)
    middle = (exact - high).astype(BF16).astype(F32)
    low = exact - high - middle
    line = lax.broadcasted_iota(jnp.int32, (8, 1), 0)
    rows = jnp.where(line == 0, high, 0.0) + jnp.where(line == 1, middle, 0.0)
    rows += jnp.where(line == 2, low, 0.0) + jnp.where(line == 3, row_ref[1:2, :], 0.0)
    a_ref[piece:, :] = rows.astype(BF16)
    bc_ref[0] = up_ref[...]
    bc_ref[1] = down_ref[...]


def prepare(w_qkv, w_out, w_up, w_down, b_qv, vectors):
    piece, part = w_qkv.shape[1:]
    model = w_up.shape[1]
    dp = lax.axis_index("dp").astype(jnp.int32)
    if piece % 16 == 0:

        def whole(s):
            return pl.BlockSpec(s, lambda i, d: (0,) * len(s))

        given = [w_qkv, w_out, w_up, w_down.T, b_qv, *[v[None] for v in vectors]]
        shapes = [(piece + 8, model), (2, piece, model)]
        return pl.pallas_call(
            functools.partial(prepare_kernel, piece),
            grid_spec=pltpu.PrefetchScalarGridSpec(
                num_scalar_prefetch=1,
                grid=(1,),
                in_specs=[whole(v.shape) for v in given],
                out_specs=[whole(s) for s in shapes],
                scratch_shapes=[pltpu.VMEM((8, model), F32)],
            ),
            out_shape=[jax.ShapeDtypeStruct(s, BF16) for s in shapes],
            cost_estimate=CHEAP,
            name="prepare_units",
        )(dp[None], *given)
    row = jnp.concatenate([v.astype(F32) for v in vectors])
    row = jnp.pad(row, (0, model - row.shape[0]))
    high = row.astype(BF16)
    middle = (row - high.astype(F32)).astype(BF16)
    low = (row - high.astype(F32) - middle.astype(F32)).astype(BF16)
    keep = lax.broadcasted_iota(jnp.int32, (1, part // b_qv.shape[1], 1), 1) == dp
    spot = jnp.where(keep, b_qv[:, None, :], jnp.zeros((), BF16)).reshape(-1)
    spot = jnp.pad(spot, (0, model - spot.shape[0]))
    tail = jnp.pad(jnp.stack([high, middle, low, spot]), ((0, 4), (0, 0)))
    unit = jnp.concatenate([w_qkv[0], w_qkv[1], w_qkv[2], w_out.T], axis=1)
    return jnp.concatenate([unit, tail], axis=0), jnp.stack([w_up, w_down.T])


def project_kernel(index, moves, piece, part, halves, where_ref, own_ref, other_ref, *refs):
    ins, (out_ref, w_ref, o_ref, ext_ref, bias_ref) = refs[:-5], refs[-5:]
    width = 2 * part

    @pl.when(pl.program_id(0) == 0)
    def _():
        bias_ref[...] = jnp.zeros_like(bias_ref)

        def each(source, unit, to, rx):
            value = source[unit, piece:, : 2 * part]
            ext_ref[to, :, 2 * part * rx : 2 * part * (rx + 1)] = value
            value = value.astype(F32)[3:4]
            bias_ref[0:1, rx * part : (rx + 1) * part] += value[:, :part]
            at = 2 * width + rx * part
            bias_ref[0:1, at : at + part] += value[:, part:]

        put_units(index, moves, where_ref, ins, (w_ref, o_ref), each)

    x = either(pl.program_id(0), halves, own_ref, other_ref)
    out_ref[...] = (dot_nn(x, w_ref[...]) + bias_ref[0:1, :]).astype(BF16)


def feed_kernel(index, moves, halves, where_ref, own_ref, other_ref, bias_ref, *refs):
    ins, (hidden_ref, slope_ref, keep_ref, send_ref, b_ref, c_ref) = refs[:-6], refs[-6:]
    step = pl.program_id(0)

    @pl.when(step == 0)
    def _():
        put_units(index, moves, where_ref, ins, (b_ref, c_ref))

    x = either(step, halves, own_ref, other_ref)
    hidden, slope = gelu_both(dot_nn(x, b_ref[...]) + bias_ref[...])
    hidden_ref[...] = hidden
    slope_ref[...] = slope
    part = dot_nt(hidden, c_ref[...])

    @pl.when(step < halves)
    def _():
        keep_ref[...] = part

    @pl.when(step >= halves)
    def _():
        send_ref[...] = part.astype(BF16)


def chunks(n, size=512):
    return [slice(at, min(at + size, n)) for at in range(0, n, size)]


def gelu_both(up):
    cdf = 0.5 * (1.0 + lax.erf(up * ROOT_HALF))
    slope = cdf + up * (jnp.exp(-0.5 * up * up) * INV_ROOT_TWO_PI)
    return (up * cdf).astype(BF16), slope.astype(BF16)


def feed_back_kernel(size, piece, where_ref, *refs):
    own_ref, other_ref, n_own_ref, n_other_ref, slope_ref, hidden_ref, c_ref, b_ref = refs[:8]
    keep_ref, send_ref, sum_ref, c_keep, c_send, b_keep, b_send = refs[8:15]
    d_ref, d_turned, n_turned, acc_ref, c_grad, b_grad = refs[15:]
    step, dp = pl.program_id(0), where_ref[0]
    half, model = own_ref.shape
    outer = c_keep.shape[0] // 2

    @pl.when(step == 0)
    def _():
        for at, d, n in ((0, own_ref, n_own_ref), (half, other_ref, n_other_ref)):
            d_ref[at : at + half, :] = d[...]
            d_turned[:, at : at + half] = d[...].T
            n_turned[:, at : at + half] = n[...].T

    d_up = (dot_nn(d_ref[...], c_ref[...]) * slope_ref[...].astype(F32)).astype(BF16)
    sum_ref[...] = jnp.sum(d_up.astype(F32), axis=0, keepdims=True)
    part = dot_nt(d_up, b_ref[...])

    @pl.when(step == 0)
    def _():
        acc_ref[...] = part

    @pl.when(step > 0)
    def _():
        acc_ref[...] += part

    c_grad[...] = dot_nn(d_turned[...], hidden_ref[...]).astype(BF16)
    b_grad[...] = dot_nn(n_turned[...], d_up).astype(BF16)
    width = c_ref.shape[1]
    for s in range(2 * model // width):
        for at in range(0, width, size):
            rx, to = divmod(s * width + at, model)
            for parity in range(2):

                @pl.when((step == s) & (where_ref[1] == parity))
                def _():
                    for ry in range(2):
                        first, second = (ry, rx) if parity else (rx, ry)
                        outs = ((c_send, b_send) if first else (c_keep, b_keep))

                        def move(z, carry):
                            rows = pl.ds(pl.multiple_of(jnp.bitwise_xor(dp, 2 * z + ry) * piece, 16), piece)
                            for out, grad in zip(outs, (c_grad, b_grad)):
                                out[second * outer + z, :, to : to + size] = grad[rows, at : at + size]
                            return carry

                        lax.fori_loop(0, outer, move, 0)

    @pl.when(step == pl.num_programs(0) - 1)
    def _():
        keep_ref[...] = acc_ref[:half, :]
        send_ref[...] = acc_ref[half:, :].astype(BF16)


def feed_back(d_own, d_other, n_own, n_other, slope, hidden, c, b, piece):
    rows, model = d_own.shape
    wide = b.shape[1]
    ndp = model // piece
    if piece % 16:
        d, n = jnp.concatenate([d_own, d_other]), jnp.concatenate([n_own, n_other])
        d_up = (dot_nn(d, c) * slope.astype(F32)).astype(BF16)
        part = dot_nt(d_up, b)
        sums = jnp.sum(d_up.astype(F32), axis=0, keepdims=True)
        wide_part = [((0, 1), 2, model, 0, True)]
        c_pair = summed([d_own, d_other, hidden], wide_part)
        b_pair = summed([n_own, n_other, d_up], wide_part)
        return part[:rows], part[rows:].astype(BF16), sums, *c_pair, *b_pair

    def whole(s):
        return pl.BlockSpec(s, lambda i, w: (0,) * len(s))

    def columns(n):
        return pl.BlockSpec((n, 512), lambda i, w: (0, i))

    units = (ndp, piece, model)
    return pl.pallas_call(
        functools.partial(feed_back_kernel, 256, piece),
        grid_spec=pltpu.PrefetchScalarGridSpec(
            num_scalar_prefetch=1,
            grid=(wide // 512,),
            in_specs=[whole((rows, model))] * 4 + [columns(2 * rows)] * 2 + [columns(model)] * 2,
            out_specs=[whole((rows, model))] * 2 + [columns(1)] + [whole(units)] * 4,
            scratch_shapes=[
                pltpu.VMEM((2 * rows, model), BF16),
                pltpu.VMEM((model, 2 * rows), BF16),
                pltpu.VMEM((model, 2 * rows), BF16),
                pltpu.VMEM((2 * rows, model), F32),
                pltpu.VMEM((model, 512), BF16),
                pltpu.VMEM((model, 512), BF16),
            ],
        ),
        out_shape=[
            jax.ShapeDtypeStruct((rows, model), F32),
            jax.ShapeDtypeStruct((rows, model), BF16),
            jax.ShapeDtypeStruct((1, wide), F32),
        ]
        + [jax.ShapeDtypeStruct(units, BF16)] * 4,
        cost_estimate=CHEAP,
        name="feed_back",
    )(where(), d_own, d_other, n_own, n_other, slope, hidden, c, b)


def ordered(spreads, moves):
    arrays, index = joined(spreads)
    order = jnp.bitwise_xor(jnp.arange(lax.axis_size("dp")), lax.axis_index("dp"))
    made = {}
    for lead, rows, col, cols, target, at in moves:
        for rx in range(2):
            both = []
            for swapped in range(2):
                units = {}
                for array, unit, outer, first, second in index:
                    x, y = (second, first) if swapped else (first, second)
                    if x == rx:
                        units[2 * outer + y] = arrays[array][(unit, *lead)][rows, col : col + cols]
                both.append(jnp.stack([units[k] for k in sorted(units)]))
            stack = jnp.take(jnp.where(lax.axis_index("c") == 0, both[0], both[1]), order, axis=0)
            made.setdefault(target, []).append((at[rx], stack))
    return [jnp.concatenate([m for _, m in sorted(made[t], key=lambda p: p[0])], axis=-1) for t in sorted(made)]


def project(spreads, own, other, piece, part, block):
    width = 2 * part
    rows, model = own.shape
    halves = rows // block
    moves = [((), piece, j * part, part, 0, (j * width, j * width + part)) for j in range(3)]
    moves.append(((), piece, 3 * part, part, 1, (0, part)))
    if piece % 16 == 0:
        arrays, index = joined(spreads)

        def whole(s):
            return pl.BlockSpec(s, lambda i, d: (0,) * len(s))

        shapes = [(model, 3 * width), (model, width), (model // piece, 8, 2 * width)]
        return pl.pallas_call(
            functools.partial(project_kernel, index, moves, piece, part, halves),
            grid_spec=pltpu.PrefetchScalarGridSpec(
                num_scalar_prefetch=1,
                grid=(2 * halves,),
                in_specs=split_specs(block, model, halves) + [whole(a.shape) for a in arrays],
                out_specs=[pl.BlockSpec((block, 3 * width), lambda i, d: (i, 0))] + [whole(s) for s in shapes],
                scratch_shapes=[pltpu.VMEM((8, 3 * width), F32)],
            ),
            out_shape=[jax.ShapeDtypeStruct(s, BF16) for s in [(2 * rows, 3 * width), *shapes]],
            cost_estimate=CHEAP,
            name="project_kernel",
        )(where(), own, other, *arrays)
    slices = [(lead, slice(0, n), *rest) for lead, n, *rest in moves]
    slices.append(((), slice(piece, piece + 8), 0, 2 * part, 2, (0, 2 * part)))
    w, o, ext = ordered(spreads, slices)
    bias = jnp.sum(ext[:, 3].astype(F32), axis=0).reshape(2, 2, part)
    bias = jnp.concatenate([bias[:, 0].reshape(-1), jnp.zeros((width,), F32), bias[:, 1].reshape(-1)])
    w, o = w.reshape(model, -1), o.reshape(model, -1)
    return (dot_nn(jnp.concatenate([own, other]), w) + bias[None]).astype(BF16), w, o, ext


def feed(spreads, own, other, bias, piece, block):
    rows, model = own.shape
    halves = rows // block
    moves = [((k,), piece, 0, model, k, (0, model)) for k in range(2)]
    if piece % 16 == 0:
        arrays, index = joined(spreads)

        def whole(s):
            return pl.BlockSpec(s, lambda i, d: (0,) * len(s))

        wide = pl.BlockSpec((block, 2 * model), lambda i, d: (i, 0))
        return pl.pallas_call(
            functools.partial(feed_kernel, index, moves, halves),
            grid_spec=pltpu.PrefetchScalarGridSpec(
                num_scalar_prefetch=1,
                grid=(2 * halves,),
                in_specs=split_specs(block, model, halves) + [whole(a.shape) for a in [bias, *arrays]],
                out_specs=[wide, wide, *split_specs(block, model, halves)] + [whole((model, 2 * model))] * 2,
            ),
            out_shape=[jax.ShapeDtypeStruct((2 * rows, 2 * model), BF16)] * 2
            + [jax.ShapeDtypeStruct((rows, model), F32), jax.ShapeDtypeStruct((rows, model), BF16)]
            + [jax.ShapeDtypeStruct((model, 2 * model), BF16)] * 2,
            cost_estimate=CHEAP,
            name="feed_kernel",
        )(where(), own, other, bias, *arrays)
    b, c = ordered(spreads, [(lead, slice(0, n), *rest) for lead, n, *rest in moves])
    b, c = b.reshape(model, -1), c.reshape(model, -1)
    hidden, slope = gelu_both(dot_nn(jnp.concatenate([own, other]), b) + bias)
    part = dot_nt(hidden, c)
    return hidden, slope, part[:rows], part[rows:].astype(BF16), b, c


def where():
    return jnp.stack([lax.axis_index("dp"), lax.axis_index("c")]).astype(jnp.int32)


def sum_kernel(parts, piece, extra, part, where_ref, *refs):
    count = 1 + max(max(*p[0], p[1]) for p in parts)
    ins = refs[:count]
    scratch = refs[count + (3 if extra else 0) :]
    outs, left_ref, acc, ext_ref = scratch[:2], scratch[2], scratch[3], scratch[4]
    dp, step = where_ref[0], pl.program_id(0)
    outer = outs[0].shape[0] // 2
    blocked = parts[0][4]
    if extra:
        lines_ref, up_ref, bias_ref = refs[count : count + 3]
        model = lines_ref.shape[1]
        for rx in range(2):
            ext_ref[rx] = jnp.zeros(ext_ref.shape[1:], F32)
            ext_ref[rx, 0:1, :] = up_ref[0:1, rx * model : (rx + 1) * model]
            ext_ref[rx, 1:7, :] = lines_ref[0:6, :]
            for k in range(2):
                ext_ref[rx, extra - 1 : extra, k * part : (k + 1) * part] = bias_ref[
                    0:1, (2 * k + rx) * part : (2 * k + rx + 1) * part
                ]

    def turned(own, other):
        half = ins[own].shape[0]
        left_ref[:, :half] = ins[own][...].T
        left_ref[:, half:] = ins[other][...].T

    for k, ((own, other), right, width, at, by_block) in enumerate(parts):
        if by_block:

            @pl.when(step == 0)
            def _():
                turned(own, other)

            for lanes in chunks(width, 256):
                acc[:, lanes] = dot_nn(left_ref[...], ins[right][:, lanes]).astype(BF16)
        else:

            @pl.when(step == 0)
            def _():
                if k == 0 or parts[k - 1][0] != (own, other):
                    turned(own, other)
                for j in range(ins[right].shape[1] // (2 * width)):
                    both = dot_nn(left_ref[...], ins[right][:, 2 * j * width : 2 * (j + 1) * width]).astype(BF16)
                    for rx in range(2):
                        lanes = slice(rx * acc.shape[1] // 2 + at + j * width, rx * acc.shape[1] // 2 + at + (j + 1) * width)
                        acc[:, lanes] = both[:, rx * width : (rx + 1) * width]

    span = outs[0].shape[2]

    def put(rx):
        lanes = slice(0, span) if blocked else slice(rx * span, (rx + 1) * span)
        for parity in range(2):

            @pl.when(where_ref[1] == parity)
            def _():
                for ry in range(2):
                    first, second = (ry, rx) if parity else (rx, ry)

                    def move(z, carry):
                        rows = pl.ds(pl.multiple_of(jnp.bitwise_xor(dp, 2 * z + ry) * piece, 16), piece)
                        outs[first][second * outer + z, :piece, :] = acc[rows, lanes]
                        if extra:
                            outs[first][second * outer + z, piece:, :] = ext_ref[rx].astype(BF16)
                        return carry

                    lax.fori_loop(0, outer, move, 0)

    for rx in range(2):
        if blocked:
            pl.when(step == rx)(functools.partial(put, rx))
        else:
            put(rx)


def summed(arrays, parts, lines=None, bias_up=None, bias=None):
    ndp = lax.axis_size("dp")
    model = arrays[0].shape[1]
    piece = model // ndp
    blocked = parts[0][4]
    width = sum(p[2] if p[4] else arrays[p[1]].shape[1] // 2 for p in parts)
    extra = 0 if lines is None else 8
    if piece % 16 == 0:

        def whole(s):
            return pl.BlockSpec(s, lambda i, d: (0,) * len(s))

        given = list(arrays) + ([] if lines is None else [lines, bias_up, bias])
        specs = [whole(a.shape) for a in given]
        if blocked:
            right = parts[0][1]
            specs[right] = pl.BlockSpec((arrays[right].shape[0], width), lambda i, d: (0, i))
        shape = (ndp, piece + extra, width)
        return pl.pallas_call(
            functools.partial(sum_kernel, parts, piece, extra, 0 if bias is None else bias.shape[1] // 4),
            grid_spec=pltpu.PrefetchScalarGridSpec(
                num_scalar_prefetch=1,
                grid=(2 if blocked else 1,),
                in_specs=specs,
                out_specs=[whole(shape)] * 2,
                scratch_shapes=[
                    pltpu.VMEM((model, 2 * arrays[0].shape[0]), BF16),
                    pltpu.VMEM((model, width if blocked else 2 * width), BF16),
                    pltpu.VMEM((2, max(extra, 8), width), F32),
                ],
            ),
            out_shape=[jax.ShapeDtypeStruct(shape, BF16)] * 2,
            cost_estimate=CHEAP,
        compiler_params=pltpu.CompilerParams(vmem_limit_bytes=40 * 1024 * 1024),
        name="sum_units",
        )(where(), *given)
    order = jnp.bitwise_xor(jnp.arange(ndp), lax.axis_index("dp"))
    sides = []
    if extra:
        line = jnp.transpose(bias.reshape(2, 2, -1), (1, 0, 2)).reshape(2, -1)
        line = jnp.pad(line, ((0, 0), (0, width - line.shape[1]))).astype(BF16)
        both = jnp.broadcast_to(lines.astype(BF16)[None], (2, *lines.shape))
        ext = jnp.concatenate([bias_up.astype(BF16).reshape(2, 1, -1), both, line[:, None]], axis=1)
    for rx in range(2):
        g = []
        for (own, other), right, cols, _, by_block in parts:
            left = jnp.concatenate([arrays[own], arrays[other]])
            for j in range(1 if by_block else arrays[right].shape[1] // (2 * cols)):
                at = (2 * j + rx) * cols
                g.append(dot_tn(left, arrays[right][:, at : at + cols]).astype(BF16))
        g = jnp.concatenate(g, axis=1).reshape(ndp, piece, width)
        if extra:
            g = jnp.concatenate([g, jnp.broadcast_to(ext[rx][None], (ndp, extra, width))], axis=1)
        g = jnp.take(g, order, axis=0).reshape(ndp // 2, 2, piece + extra, width)
        sides.append(jnp.moveaxis(g, 1, 0))
    g = jnp.stack(sides)
    g = jnp.where(lax.axis_index("c") == 0, g, jnp.swapaxes(g, 0, 1))
    return g[0].reshape(ndp, piece + extra, width), g[1].reshape(ndp, piece + extra, width)


class Scatter:
    def __init__(self, pair):
        self.keep, self.send = pair

    def first(self):
        self.one = turn(self.send, 0)

    def second(self):
        half = self.keep.shape[0] // 2
        self.kept = add(self.keep[:half], self.one[:half])
        self.two = turn(add(self.keep[half:], self.one[half:]), 1)

    def third(self):
        total = add(self.kept, self.two)
        outer = total.shape[0]
        if outer <= 4:
            self.last = [total[0]]
            self.three = [flip(total[k], "dp", 2 * k) for k in range(1, outer)]
            return
        for k in reversed(range(outer_bits())):
            half = total.shape[0] // 2
            total = add(total[:half], flip(total[half:], "dp", 2 << k))
        self.last, self.three = [total[0]], []

    def result(self):
        return sum(t.astype(F32) for t in self.last + self.three)


def local(
    tokens, grad_out, seg_ids, w_qkv, b_qv, w_out, w_up, b_up, w_down, b_out, b_down, g_one, s_one, g_two, s_two
):
    ndp = lax.axis_size("dp")
    nx = lax.axis_size("x")
    parity = lax.axis_index("c")
    which = lax.axis_index("x")
    place_dp = lax.axis_index("dp")
    rows, model = tokens.shape
    piece = model // ndp
    part = w_qkv.shape[2]
    width = nx * part
    slim = model // (ndp * nx * 2)
    qv = part // ndp
    extra = 8
    block = 256
    tall = 512

    unit_a, unit_bc = prepare(
        w_qkv, w_out, w_up, w_down, b_qv, [b_out, b_down, g_one, s_one, g_two, s_two, b_up]
    )
    a_near = Spread(jnp.stack([unit_a, flip(unit_a, "dp", 2)]), 0)

    class Box:
        pass

    box = Box()
    box.bc = unit_bc
    a_near.units = stage("z1", a_near.units, bc=(box, "bc"))
    a_far = Spread(gather_far(a_near.units), 2)
    a_near.first()
    a_near.one = stage("n1", a_near.one, bc=(box, "bc"), az=(a_far, "units"))
    a_near.second()
    a_far.units = stage("z2", a_far.units, bc=(box, "bc"), an2=(a_near, "two"))
    a_far.first()
    bc_near = Spread(jnp.stack([box.bc, flip(box.bc, "dp", 2)]), 0)
    a_far.one = stage("f1", a_far.one, bz1=(bc_near, "units"), an2=(a_near, "two"))
    a_far.second()
    bc_far = Spread(gather_far(bc_near.units), 2)
    bc_items = lambda: dict(bn1=(bc_near, "one"), bz2=(bc_far, "units"), bn2=(bc_near, "two"), bf1=(bc_far, "one"), bf2=(bc_far, "two"))
    done = set()

    def advance(name, *values):
        res = stage(name, *values, **{k: v for k, v in bc_items().items() if hasattr(*v)})
        order = ["z2", "f1", "f2", "qkv", "ctx", "attn", "normed", "feed"]
        at = order.index(name)
        ready = lambda k: k is None or order.index(OPT.get(k, "feed")) <= at
        if "n1" not in done and order.index(OPT.get("rn1", "z2")) <= at:
            bc_near.first()
            done.add("n1")
        if "n2" not in done and "n1" in done and (ready("bn1") or name == "feed"):
            bc_near.second()
            done.add("n2")
        if "f1" not in done and (ready("bz2") or name == "feed"):
            bc_far.first()
            done.add("f1")
        if "f2" not in done and "f1" in done and (ready("bf1") or name == "feed"):
            bc_far.second()
            done.add("f2")
        return res

    advance("z2")
    a_far.two = advance("f2", a_far.two)

    seg = lax.dynamic_index_in_dim(seg_ids, which, 0, keepdims=False).reshape(2, rows)
    seg_rel = jnp.concatenate(
        [
            lax.dynamic_index_in_dim(seg, parity, 0, keepdims=False),
            lax.dynamic_index_in_dim(seg, 1 - parity, 0, keepdims=False),
        ]
    )
    seg_col = seg_rel[:, None]
    seg_row = seg_rel[None, :]
    x_other = swap(tokens)

    qkv, w_all, o_t, ext = project([a_near, a_far], tokens, x_other, piece, part, block)
    ext = ext[:, :3].astype(F32)
    ext = (ext[:, 0] + ext[:, 1] + ext[:, 2]).reshape(ndp, nx, 2 * part)
    bias_up = jnp.transpose(ext[:, :, 6 * slim : 6 * slim + piece], (1, 0, 2)).reshape(1, nx * model)
    six = ext[:, :, : 6 * slim]
    six = jnp.stack([six, swap(six)], axis=2)
    six = jnp.where(lax.broadcasted_iota(jnp.int32, (1, 1, 2, 1), 2) == parity, six[:, :, :1], six[:, :, 1:])
    six = jnp.where(which == 0, six, six[:, ::-1]).reshape(ndp * nx * 2, 6, slim)
    vectors = jnp.transpose(six, (1, 0, 2)).reshape(6, model)
    bout_f, bdown_f, gone_f, sone_f, gtwo_f, stwo_f = [vectors[i : i + 1] for i in range(6)]

    qkv = advance("qkv", qkv)
    ctx, lse = attention_forward(qkv, seg_col, seg_row, tall, 0, 2 * rows // tall, ())
    ctx = advance("ctx", ctx)
    attn_send = dot_nt(ctx[rows:], o_t).astype(BF16)
    attn = dot_nt(ctx[:rows], o_t) + swap(attn_send).astype(F32)
    attn = advance("attn", attn)
    first = tokens.astype(F32) + attn + bout_f
    hat_one, inv_one = normalize(first)
    normed = hat_one * gone_f + sone_f
    normed_low = advance("normed", normed.astype(BF16))
    normed_other = swap(normed_low)
    normed_other = advance("feed", normed_other)
    hidden, slope, keep, send, b_all, c_all = feed([bc_near, bc_far], normed_low, normed_other, bias_up, piece, block)
    branch = keep + swap(send).astype(F32)
    second = normed + branch + bdown_f
    hat_two, inv_two = normalize(second)
    layer_out = (hat_two * gtwo_f + stwo_f).astype(BF16)

    g_in = grad_out.astype(F32)
    d_gain_two = jnp.sum(g_in * hat_two, axis=0)
    d_shift_two = jnp.sum(g_in, axis=0)
    d_second = normalize_back(hat_two, inv_two, gtwo_f, g_in)
    d_branch = d_second.astype(BF16)
    d_bias_down = jnp.sum(d_branch.astype(F32), axis=0)
    db_other = swap(d_branch)

    sc = sb = sa = None
    order = ["P0", "P1", "P2", "P3", "P4", "P5", "P6", "P7"]
    sent = set()

    def go(name, *values):
        items = {}
        for k, s in (("c", sc), ("b", sb)):
            if s is not None:
                for n, f in (("1", "one"), ("2", "two"), ("3", "three")):
                    if hasattr(s, f):
                        items[k + n] = (s, f)
        res = stage(name, *values, **items)
        at = order.index(name)
        for k, s in (("c", sc), ("b", sb)):
            if s is None:
                continue
            for n, need, f in ((1, None, "first"), (2, "1", "second"), (3, "2", "third")):
                if k + str(n) in sent or (n > 1 and k + str(n - 1) not in sent):
                    continue
                if n == 1 or order.index(OPT.get(k + need, "P7")) <= at:
                    getattr(s, f)()
                    sent.add(k + str(n))
        return res

    keep, send, d_bias_up, *pairs = feed_back(
        d_branch, db_other, normed_low, normed_other, slope, hidden, c_all, b_all, piece
    )
    sc, sb = Scatter(pairs[:2]), Scatter(pairs[2:])
    go("P0")
    d_normed = d_second + keep + swap(send).astype(F32)
    d_normed = go("P1", d_normed)
    d_gain_one = jnp.sum(d_normed * hat_one, axis=0)
    d_shift_one = jnp.sum(d_normed, axis=0)
    d_first = normalize_back(hat_one, inv_one, gone_f, d_normed)
    d_attn = d_first.astype(BF16)
    d_bias_out = jnp.sum(d_attn.astype(F32), axis=0)
    da_other = swap(d_attn)
    d_ctx = dot_nn(d_attn, o_t).astype(BF16)
    sums = jnp.stack([d_bias_out, d_bias_down, d_gain_one, d_shift_one, d_gain_two, d_shift_two])
    sums = sums + swap(sums)
    d_ctx_other = dot_nn(da_other, o_t).astype(BF16)
    d_ctx_other = go("P2", d_ctx_other)
    d_qkv, bias = attention_backward(qkv, ctx, lse, d_ctx, d_ctx_other, seg_col, seg_row, block)
    d_qkv = go("P3", d_qkv)
    attention_parts = [((0, 1), 2, part, 0, False), ((3, 4), 5, part, 3 * part, False)]
    given = [tokens, x_other, d_qkv, d_attn, da_other, ctx]
    sa = Scatter(summed(given, attention_parts, sums, d_bias_up, bias))
    d_qkv, sa.send = go("P4", d_qkv, sa.send)
    sa.first()
    keep, send = input_gradient(d_qkv, d_first, w_all, block)
    sa.one, keep, send = go("P5", sa.one, keep, send)
    sa.second()
    input_grad = keep + swap(send).astype(F32)
    sa.two, input_grad = go("P6", sa.two, input_grad)
    sa.third()
    go("P7")
    input_grad = input_grad.astype(BF16)
    gc = sc.result()
    gb = sb.result()
    ga = sa.result()
    g_qkv = jnp.stack([ga[:piece, j * part : (j + 1) * part] for j in range(3)])
    tail = ga[piece:]
    g_bqv = lax.dynamic_slice_in_dim(tail[7, : 2 * part].reshape(2, part), place_dp * qv, qv, axis=1)
    g_bup = lax.dynamic_slice_in_dim(tail[0], place_dp * piece, piece)
    six = lax.dynamic_slice_in_dim(tail[1:7], ((place_dp * nx + which) * 2 + parity) * slim, slim, axis=1)
    return (
        layer_out,
        input_grad,
        g_qkv,
        g_bqv,
        ga[:piece, 3 * part :].T,
        gb,
        g_bup,
        gc.T,
        *[six[i] for i in range(6)],
    )


def solution(mesh):
    ndp, nt = mesh.devices.shape
    fine = Mesh(mesh.devices.reshape(ndp, nt // 2, 2), ("dp", "x", "c"))
    tensor = ("x", "c")
    every = ("dp", "x", "c")
    row = P(every, None)
    vec = P(every)
    return jax.shard_map(
        local,
        mesh=fine,
        in_specs=(
            row,
            row,
            P("dp", None),
            P(None, "dp", tensor),
            P(None, ("x", "c", "dp")),
            P(tensor, "dp"),
            P("dp", tensor),
            P(("x", "c", "dp")),
            P(tensor, "dp"),
            vec,
            vec,
            vec,
            vec,
            vec,
            vec,
        ),
        out_specs=(
            row,
            row,
            P(None, "dp", tensor),
            P(None, ("x", "c", "dp")),
            P(tensor, "dp"),
            P("dp", tensor),
            P(("x", "c", "dp")),
            P(tensor, "dp"),
            vec,
            vec,
            vec,
            vec,
            vec,
            vec,
        ),
        check_vma=False,
    )
```

```python
import functools

import jax
import jax.numpy as jnp
from jax import lax
from jax.experimental import pallas as pl
from jax.experimental.pallas import tpu as pltpu
from jax.sharding import Mesh, PartitionSpec as P

HD = 64
LANES = 128
EPSILON = 1e-05
ROOT_HALF = 0.7071067811865476
INV_ROOT_TWO_PI = 0.3989422804014327
F32 = jnp.float32
BF16 = jnp.bfloat16


def dot(a, b, dims):
    return lax.dot_general(a, b, (dims, ((), ())), preferred_element_type=F32)


def dot_nn(a, b):
    return dot(a, b, ((1,), (0,)))


def dot_nt(a, b):
    return dot(a, b, ((1,), (1,)))


def dot_tn(a, b):
    return dot(a, b, ((0,), (0,)))


CHEAP = pl.CostEstimate(flops=1000, bytes_accessed=1000, transcendentals=0)


def attention_forward_kernel(width, seg_q_ref, seg_k_ref, q_ref, k_ref, v_ref, *refs):
    ctx_ref, lse_ref = refs[-2:]
    lane = lax.broadcasted_iota(jnp.int32, (1, LANES), 1)
    bias = jnp.where(seg_q_ref[...] == seg_k_ref[...], 0.0, -1000000000.0)
    block = q_ref.shape[0]

    stats = jnp.zeros((block, LANES), F32)
    for tile in range(width // LANES):
        cols = slice(tile * LANES, (tile + 1) * LANES)
        q2 = q_ref[:, cols] * jnp.asarray(0.125, BF16)
        k2 = k_ref[:, cols]
        v2 = v_ref[:, cols]
        outs = []
        for half in range(2):
            qm = jnp.where((lane // HD) == half, q2, jnp.zeros_like(q2))
            s = dot_nt(qm, k2) + bias
            top = jnp.max(s, axis=-1, keepdims=True)
            e = jnp.exp(s - top)
            total = jnp.sum(e, axis=-1, keepdims=True)
            outs.append(dot_nn(e.astype(BF16), v2) * (1.0 / total))
            stats = jnp.where(lane == 2 * tile + half, top + jnp.log(total), stats)
        ctx_ref[:, cols] = jnp.where(lane < HD, outs[0], outs[1]).astype(BF16)
    lse_ref[...] = stats.T[: lse_ref.shape[0], :]


def attention_forward(qkv, seg_col, seg_row, block, first, count, made):
    rows, triple = qkv.shape
    width = triple // 3
    return pl.pallas_call(
        functools.partial(attention_forward_kernel, width),
        grid=(count,),
        in_specs=[
            pl.BlockSpec((block, 1), lambda i: (first + i, 0)),
            pl.BlockSpec((1, rows), lambda i: (0, 0)),
            pl.BlockSpec((block, width), lambda i: (first + i, 0)),
            pl.BlockSpec((rows, width), lambda i: (0, 1)),
            pl.BlockSpec((rows, width), lambda i: (0, 2)),
        ]
        + [pl.BlockSpec(memory_space=pl.ANY)] * len(made),
        out_specs=[
            pl.BlockSpec((block, width), lambda i: (first + i, 0)),
            pl.BlockSpec((8, block), lambda i: (0, first + i)),
        ],
        out_shape=[
            jax.ShapeDtypeStruct((rows, width), BF16),
            jax.ShapeDtypeStruct((8, rows), F32),
        ],
        input_output_aliases={5 + i: i for i in range(len(made))},
        cost_estimate=CHEAP,
        compiler_params=pltpu.CompilerParams(vmem_limit_bytes=30 * 1024 * 1024),
        name="attention_forward",
    )(seg_col, seg_row, qkv, qkv, qkv, *made)


def split_specs(block, columns, halves):
    return [
        pl.BlockSpec((block, columns), lambda i, *_: (jnp.minimum(i, halves - 1), 0)),
        pl.BlockSpec((block, columns), lambda i, *_: (jnp.maximum(i - halves, 0), 0)),
    ]


def either(step, halves, own_ref, other_ref):
    return jnp.where(step < halves, own_ref[...], other_ref[...])


def attention_backward_kernel(
    width, halves, seg_k_ref, seg_q_ref, q_ref, k_ref, v_ref, ctx_ref, lse_ref, own_ref, other_ref, out_ref, sum_ref, dk_ref, dv_ref
):
    step = pl.program_id(0)
    block = q_ref.shape[0]
    lane = lax.broadcasted_iota(jnp.int32, (1, LANES), 1)

    @pl.when(step == 0)
    def _():
        dk_ref[...] = jnp.zeros_like(dk_ref)
        dv_ref[...] = jnp.zeros_like(dv_ref)
        sum_ref[...] = jnp.zeros_like(sum_ref)

    bias = jnp.where(seg_k_ref[...] == seg_q_ref[...], 0.0, -1000000000.0)
    for pair in range(width // LANES):
        cols = slice(pair * LANES, (pair + 1) * LANES)
        q2 = q_ref[:, cols] * jnp.asarray(0.125, BF16)
        k2 = k_ref[:, cols]
        v2 = v_ref[:, cols]
        d2 = jnp.where(step < halves, own_ref[:, cols], other_ref[:, cols])
        prod = (d2.astype(F32) * ctx_ref[:, cols].astype(F32)).T
        kt = (k2 * jnp.asarray(0.125, BF16)).T
        row = lax.broadcasted_iota(jnp.int32, (LANES, 1), 0)
        dq = None
        dk = None
        dv = None
        for half in range(2):
            mine = (lane // HD) == half
            qm = jnp.where(mine, q2, jnp.zeros_like(q2))
            dm = jnp.where(mine, d2, jnp.zeros_like(d2))
            ktm = jnp.where((row // HD) == half, kt, jnp.zeros_like(kt))
            inner = jnp.sum(prod[half * HD : (half + 1) * HD, :], axis=0, keepdims=True)
            lse = lse_ref[2 * pair + half : 2 * pair + half + 1, :]
            p = jnp.exp(dot_nt(k2, qm) + bias - lse)
            dp = dot_nt(v2, dm)
            ds = (p * (dp - inner)).astype(BF16)
            dv_h = dot_nn(p.astype(BF16), dm)
            dk_h = dot_nn(ds, qm)
            dq_h = dot_nn(ktm, ds)
            dv = dv_h if dv is None else dv + dv_h
            dk = dk_h if dk is None else dk + dk_h
            dq = dq_h if dq is None else dq + dq_h
        dk_ref[:, cols] += dk
        dv_ref[:, cols] += dv
        dq = dq.T.astype(BF16)
        out_ref[pl.ds(pl.multiple_of(step * block, block), block), cols] = dq
        sum_ref[:, cols] += jnp.sum(dq.astype(F32), axis=0, keepdims=True)

    @pl.when(step == pl.num_programs(0) - 1)
    def _():
        out_ref[:, width : 2 * width] = dk_ref[...].astype(BF16)
        dv = dv_ref[...].astype(BF16)
        out_ref[:, 2 * width : 3 * width] = dv
        sum_ref[:, width : 2 * width] = jnp.sum(dv.astype(F32), axis=0, keepdims=True)


def attention_backward(qkv, ctx, lse, d_own, d_other, seg_col, seg_row, block):
    rows, triple = qkv.shape
    width = triple // 3
    halves = rows // block // 2
    return pl.pallas_call(
        functools.partial(attention_backward_kernel, width, halves),
        grid=(rows // block,),
        in_specs=[
            pl.BlockSpec((rows, 1), lambda i: (0, 0)),
            pl.BlockSpec((1, block), lambda i: (0, i)),
            pl.BlockSpec((block, width), lambda i: (i, 0)),
            pl.BlockSpec((rows, width), lambda i: (0, 1)),
            pl.BlockSpec((rows, width), lambda i: (0, 2)),
            pl.BlockSpec((block, width), lambda i: (i, 0)),
            pl.BlockSpec((8, block), lambda i: (0, i)),
            *split_specs(block, width, halves),
        ],
        out_specs=[pl.BlockSpec((rows, triple), lambda i: (0, 0)), pl.BlockSpec((1, 2 * width), lambda i: (0, 0))],
        out_shape=[jax.ShapeDtypeStruct((rows, triple), BF16), jax.ShapeDtypeStruct((1, 2 * width), F32)],
        scratch_shapes=[pltpu.VMEM((rows, width), F32), pltpu.VMEM((rows, width), F32)],
        cost_estimate=CHEAP,
        compiler_params=pltpu.CompilerParams(vmem_limit_bytes=30 * 1024 * 1024),
        name="attention_backward",
    )(seg_col, seg_row, qkv, qkv, qkv, ctx, lse, d_own, d_other)


def input_kernel(halves, d_ref, first_ref, w_ref, keep_ref, send_ref):
    step = pl.program_id(0)
    part = dot_nt(d_ref[...], w_ref[...])

    @pl.when(step < halves)
    def _():
        keep_ref[...] = first_ref[...] + part

    @pl.when(step >= halves)
    def _():
        send_ref[...] = part.astype(BF16)


def input_gradient(d_qkv, d_first, w_all, block):
    rows, model = d_first.shape
    width = d_qkv.shape[1]
    halves = rows // block
    by_row = pl.BlockSpec((block, width), lambda i: (i, 0))
    own = pl.BlockSpec((block, model), lambda i: (jnp.minimum(i, halves - 1), 0))
    return pl.pallas_call(
        functools.partial(input_kernel, halves),
        grid=(2 * halves,),
        in_specs=[by_row, own, pl.BlockSpec(w_all.shape, lambda i: (0, 0))],
        out_specs=split_specs(block, model, halves),
        out_shape=[jax.ShapeDtypeStruct((rows, model), F32), jax.ShapeDtypeStruct((rows, model), BF16)],
        cost_estimate=CHEAP,
        name="input_gradient",
    )(d_qkv, d_first, w_all)


def normalize(r):
    mean = jnp.mean(r, axis=-1, keepdims=True)
    cent = r - mean
    var = jnp.mean(cent * cent, axis=-1, keepdims=True)
    inv = lax.rsqrt(var + EPSILON)
    return cent * inv, inv


def normalize_back(hat, inv, gain, d_out):
    d_hat = d_out * gain
    first = jnp.mean(d_hat, axis=-1, keepdims=True)
    second = jnp.mean(d_hat * hat, axis=-1, keepdims=True)
    return inv * (d_hat - first - hat * second)


def swap(a):
    return lax.ppermute(a, "c", [(0, 1), (1, 0)])


def flip(a, axis, bit):
    n = lax.axis_size(axis)
    return lax.ppermute(a, axis, [(i, i ^ bit) for i in range(n)])


def turn(a, level):
    n, nx = lax.axis_size("dp"), lax.axis_size("x")
    pairs = []
    for d in range(n):
        for x in range(nx):
            for c in range(2):
                other = (d * nx + (x ^ 1)) if (c + level) % 2 == 0 else ((d ^ 1) * nx + x)
                pairs.append(((d * nx + x) * 2 + c, other * 2 + c))
    return lax.ppermute(a, ("dp", "x", "c"), pairs)


def tie(*values):
    return lax.optimization_barrier(values)


def add(*terms):
    return sum(t.astype(F32) for t in terms).astype(BF16)


def outer_bits():
    return lax.axis_size("dp").bit_length() - 2


def gather_far(near):
    parts = [near]
    for k in range(1, outer_bits()):
        held = jnp.concatenate(parts) if len(parts) > 1 else near
        parts.append(flip(held, "dp", 2 << k))
    return jnp.concatenate(parts[1:]) if len(parts) > 2 else parts[1]


OPT = {'bc': None, 'bn1': 'f2', 'bz2': 'qkv', 'bf1': 'ctx', 'bn2': 'ctx', 'bf2': 'attn', 'c1': 'P3', 'c2': 'P4', 'c3': 'P5', 'b1': 'P3', 'b2': 'P4', 'b3': 'P6', 'an2': 'f1', 'bz1': 'f1'}


def stage(name, *values, **items):
    keys = [k for k in items if OPT.get(k) == name]
    extra, spans = [], []
    for k in keys:
        v = getattr(*items[k])
        many = isinstance(v, list)
        spans.append((k, len(v) if many else 1, many))
        extra += v if many else [v]
    if len(values) + len(extra) > 1:
        out = list(tie(*values, *extra))
    else:
        out = [*values, *extra]
    res, at = out[: len(values)], len(values)
    for k, n, many in spans:
        setattr(*items[k], out[at : at + n] if many else out[at])
        at += n
    return res if len(res) > 1 else (res[0] if res else None)


class Spread:
    def __init__(self, units, outer):
        self.units, self.outer = units, outer

    def first(self):
        self.one = turn(self.units, 0)

    def second(self):
        self.two = turn(jnp.concatenate([self.units, self.one]), 1)

    def pieces(self):
        n = self.units.shape[0]
        index = [(0, u, self.outer + u, 0, 0) for u in range(n)]
        index += [(1, u, self.outer + u, 1, 0) for u in range(n)]
        index += [(2, a * n + u, self.outer + u, a, 1) for a in range(2) for u in range(n)]
        return [self.units, self.one, self.two], index


def joined(spreads):
    arrays, index = [], []
    for s in spreads:
        more, at = s.pieces()
        index += [(i + len(arrays), *rest) for i, *rest in at]
        arrays += more
    return arrays, index


def put_units(index, moves, where_ref, ins, outs, each=None):
    dp = where_ref[0]
    for parity in range(2):

        @pl.when(where_ref[1] == parity)
        def _():
            for array, unit, outer, first, second in index:
                rx, ry = (second, first) if parity else (first, second)
                to = jnp.bitwise_xor(dp, 2 * outer + ry)
                for lead, rows, col, cols, target, at in moves:
                    value = ins[array][(unit, *lead, slice(0, rows), slice(col, col + cols))]
                    outs[target][pl.ds(pl.multiple_of(to * rows, 16), rows), at[rx] : at[rx] + cols] = value
                if each is not None:
                    each(ins[array], unit, to, rx)


def prepare_kernel(piece, dp_ref, qkv_ref, out_ref, up_ref, down_ref, qv_ref, *refs):
    vectors, (a_ref, bc_ref, row_ref) = refs[:-3], refs[-3:]
    part = qkv_ref.shape[2]
    for j in range(3):
        a_ref[:piece, j * part : (j + 1) * part] = qkv_ref[j]
    a_ref[:piece, 3 * part :] = out_ref[...].T
    row_ref[...] = jnp.zeros_like(row_ref)
    at = 0
    for v in vectors:
        n = v.shape[1]
        row_ref[0:1, at : at + n] = v[...].astype(F32)
        at += n
    n = qv_ref.shape[1]
    lane = lax.broadcasted_iota(jnp.int32, (n, part), 1)
    spot = (lane == lax.broadcasted_iota(jnp.int32, (n, part), 0) + n * dp_ref[0]).astype(BF16)
    both = dot_nn(qv_ref[...], spot)
    row_ref[1:2, :part] = both[0:1]
    row_ref[1:2, part : 2 * part] = both[1:2]
    exact = row_ref[0:1, :]
    high = exact.astype(BF16).astype(F32)
    middle = (exact - high).astype(BF16).astype(F32)
    low = exact - high - middle
    line = lax.broadcasted_iota(jnp.int32, (8, 1), 0)
    rows = jnp.where(line == 0, high, 0.0) + jnp.where(line == 1, middle, 0.0)
    rows += jnp.where(line == 2, low, 0.0) + jnp.where(line == 3, row_ref[1:2, :], 0.0)
    a_ref[piece:, :] = rows.astype(BF16)
    bc_ref[0] = up_ref[...]
    bc_ref[1] = down_ref[...]


def prepare(w_qkv, w_out, w_up, w_down, b_qv, vectors):
    piece, part = w_qkv.shape[1:]
    model = w_up.shape[1]
    dp = lax.axis_index("dp").astype(jnp.int32)
    if piece % 16 == 0:

        def whole(s):
            return pl.BlockSpec(s, lambda i, d: (0,) * len(s))

        given = [w_qkv, w_out, w_up, w_down.T, b_qv, *[v[None] for v in vectors]]
        shapes = [(piece + 8, model), (2, piece, model)]
        return pl.pallas_call(
            functools.partial(prepare_kernel, piece),
            grid_spec=pltpu.PrefetchScalarGridSpec(
                num_scalar_prefetch=1,
                grid=(1,),
                in_specs=[whole(v.shape) for v in given],
                out_specs=[whole(s) for s in shapes],
                scratch_shapes=[pltpu.VMEM((8, model), F32)],
            ),
            out_shape=[jax.ShapeDtypeStruct(s, BF16) for s in shapes],
            cost_estimate=CHEAP,
            name="prepare_units",
        )(dp[None], *given)
    row = jnp.concatenate([v.astype(F32) for v in vectors])
    row = jnp.pad(row, (0, model - row.shape[0]))
    high = row.astype(BF16)
    middle = (row - high.astype(F32)).astype(BF16)
    low = (row - high.astype(F32) - middle.astype(F32)).astype(BF16)
    keep = lax.broadcasted_iota(jnp.int32, (1, part // b_qv.shape[1], 1), 1) == dp
    spot = jnp.where(keep, b_qv[:, None, :], jnp.zeros((), BF16)).reshape(-1)
    spot = jnp.pad(spot, (0, model - spot.shape[0]))
    tail = jnp.pad(jnp.stack([high, middle, low, spot]), ((0, 4), (0, 0)))
    unit = jnp.concatenate([w_qkv[0], w_qkv[1], w_qkv[2], w_out.T], axis=1)
    return jnp.concatenate([unit, tail], axis=0), jnp.stack([w_up, w_down.T])


def project_kernel(index, moves, piece, part, halves, where_ref, own_ref, other_ref, *refs):
    ins, (out_ref, w_ref, o_ref, ext_ref, bias_ref) = refs[:-5], refs[-5:]
    width = 2 * part

    @pl.when(pl.program_id(0) == 0)
    def _():
        bias_ref[...] = jnp.zeros_like(bias_ref)

        def each(source, unit, to, rx):
            value = source[unit, piece:, : 2 * part]
            ext_ref[to, :, 2 * part * rx : 2 * part * (rx + 1)] = value
            value = value.astype(F32)[3:4]
            bias_ref[0:1, rx * part : (rx + 1) * part] += value[:, :part]
            at = 2 * width + rx * part
            bias_ref[0:1, at : at + part] += value[:, part:]

        put_units(index, moves, where_ref, ins, (w_ref, o_ref), each)

    x = either(pl.program_id(0), halves, own_ref, other_ref)
    out_ref[...] = (dot_nn(x, w_ref[...]) + bias_ref[0:1, :]).astype(BF16)


def feed_kernel(index, moves, halves, where_ref, own_ref, other_ref, bias_ref, *refs):
    ins, (hidden_ref, slope_ref, keep_ref, send_ref, b_ref, c_ref) = refs[:-6], refs[-6:]
    step = pl.program_id(0)

    @pl.when(step == 0)
    def _():
        put_units(index, moves, where_ref, ins, (b_ref, c_ref))

    x = either(step, halves, own_ref, other_ref)
    hidden, slope = gelu_both(dot_nn(x, b_ref[...]) + bias_ref[...])
    hidden_ref[...] = hidden
    slope_ref[...] = slope
    part = dot_nt(hidden, c_ref[...])

    @pl.when(step < halves)
    def _():
        keep_ref[...] = part

    @pl.when(step >= halves)
    def _():
        send_ref[...] = part.astype(BF16)


def chunks(n, size=512):
    return [slice(at, min(at + size, n)) for at in range(0, n, size)]


def gelu_both(up):
    cdf = 0.5 * (1.0 + lax.erf(up * ROOT_HALF))
    slope = cdf + up * (jnp.exp(-0.5 * up * up) * INV_ROOT_TWO_PI)
    return (up * cdf).astype(BF16), slope.astype(BF16)


def feed_back_kernel(size, piece, where_ref, *refs):
    own_ref, other_ref, n_own_ref, n_other_ref, slope_ref, hidden_ref, c_ref, b_ref = refs[:8]
    keep_ref, send_ref, sum_ref, c_keep, c_send, b_keep, b_send = refs[8:15]
    d_ref, d_turned, n_turned, acc_ref, c_grad, b_grad = refs[15:]
    step, dp = pl.program_id(0), where_ref[0]
    half, model = own_ref.shape
    outer = c_keep.shape[0] // 2

    @pl.when(step == 0)
    def _():
        for at, d, n in ((0, own_ref, n_own_ref), (half, other_ref, n_other_ref)):
            d_ref[at : at + half, :] = d[...]
            d_turned[:, at : at + half] = d[...].T
            n_turned[:, at : at + half] = n[...].T

    d_up = (dot_nn(d_ref[...], c_ref[...]) * slope_ref[...].astype(F32)).astype(BF16)
    sum_ref[...] = jnp.sum(d_up.astype(F32), axis=0, keepdims=True)
    part = dot_nt(d_up, b_ref[...])

    @pl.when(step == 0)
    def _():
        acc_ref[...] = part

    @pl.when(step > 0)
    def _():
        acc_ref[...] += part

    c_grad[...] = dot_nn(d_turned[...], hidden_ref[...]).astype(BF16)
    b_grad[...] = dot_nn(n_turned[...], d_up).astype(BF16)
    width = c_ref.shape[1]
    for s in range(2 * model // width):
        for at in range(0, width, size):
            rx, to = divmod(s * width + at, model)
            for parity in range(2):

                @pl.when((step == s) & (where_ref[1] == parity))
                def _():
                    for ry in range(2):
                        first, second = (ry, rx) if parity else (rx, ry)
                        outs = ((c_send, b_send) if first else (c_keep, b_keep))

                        def move(z, carry):
                            rows = pl.ds(pl.multiple_of(jnp.bitwise_xor(dp, 2 * z + ry) * piece, 16), piece)
                            for out, grad in zip(outs, (c_grad, b_grad)):
                                out[second * outer + z, :, to : to + size] = grad[rows, at : at + size]
                            return carry

                        lax.fori_loop(0, outer, move, 0)

    @pl.when(step == pl.num_programs(0) - 1)
    def _():
        keep_ref[...] = acc_ref[:half, :]
        send_ref[...] = acc_ref[half:, :].astype(BF16)


def feed_back(d_own, d_other, n_own, n_other, slope, hidden, c, b, piece):
    rows, model = d_own.shape
    wide = b.shape[1]
    ndp = model // piece
    if piece % 16:
        d, n = jnp.concatenate([d_own, d_other]), jnp.concatenate([n_own, n_other])
        d_up = (dot_nn(d, c) * slope.astype(F32)).astype(BF16)
        part = dot_nt(d_up, b)
        sums = jnp.sum(d_up.astype(F32), axis=0, keepdims=True)
        wide_part = [((0, 1), 2, model, 0, True)]
        c_pair = summed([d_own, d_other, hidden], wide_part)
        b_pair = summed([n_own, n_other, d_up], wide_part)
        return part[:rows], part[rows:].astype(BF16), sums, *c_pair, *b_pair

    def whole(s):
        return pl.BlockSpec(s, lambda i, w: (0,) * len(s))

    def columns(n):
        return pl.BlockSpec((n, 512), lambda i, w: (0, i))

    units = (ndp, piece, model)
    return pl.pallas_call(
        functools.partial(feed_back_kernel, 256, piece),
        grid_spec=pltpu.PrefetchScalarGridSpec(
            num_scalar_prefetch=1,
            grid=(wide // 512,),
            in_specs=[whole((rows, model))] * 4 + [columns(2 * rows)] * 2 + [columns(model)] * 2,
            out_specs=[whole((rows, model))] * 2 + [columns(1)] + [whole(units)] * 4,
            scratch_shapes=[
                pltpu.VMEM((2 * rows, model), BF16),
                pltpu.VMEM((model, 2 * rows), BF16),
                pltpu.VMEM((model, 2 * rows), BF16),
                pltpu.VMEM((2 * rows, model), F32),
                pltpu.VMEM((model, 512), BF16),
                pltpu.VMEM((model, 512), BF16),
            ],
        ),
        out_shape=[
            jax.ShapeDtypeStruct((rows, model), F32),
            jax.ShapeDtypeStruct((rows, model), BF16),
            jax.ShapeDtypeStruct((1, wide), F32),
        ]
        + [jax.ShapeDtypeStruct(units, BF16)] * 4,
        cost_estimate=CHEAP,
        compiler_params=pltpu.CompilerParams(vmem_limit_bytes=52 * 1024 * 1024),
        name="feed_back",
    )(where(), d_own, d_other, n_own, n_other, slope, hidden, c, b)


def ordered(spreads, moves):
    arrays, index = joined(spreads)
    order = jnp.bitwise_xor(jnp.arange(lax.axis_size("dp")), lax.axis_index("dp"))
    made = {}
    for lead, rows, col, cols, target, at in moves:
        for rx in range(2):
            both = []
            for swapped in range(2):
                units = {}
                for array, unit, outer, first, second in index:
                    x, y = (second, first) if swapped else (first, second)
                    if x == rx:
                        units[2 * outer + y] = arrays[array][(unit, *lead)][rows, col : col + cols]
                both.append(jnp.stack([units[k] for k in sorted(units)]))
            stack = jnp.take(jnp.where(lax.axis_index("c") == 0, both[0], both[1]), order, axis=0)
            made.setdefault(target, []).append((at[rx], stack))
    return [jnp.concatenate([m for _, m in sorted(made[t], key=lambda p: p[0])], axis=-1) for t in sorted(made)]


def project(spreads, own, other, piece, part, block):
    width = 2 * part
    rows, model = own.shape
    halves = rows // block
    moves = [((), piece, j * part, part, 0, (j * width, j * width + part)) for j in range(3)]
    moves.append(((), piece, 3 * part, part, 1, (0, part)))
    if piece % 16 == 0:
        arrays, index = joined(spreads)

        def whole(s):
            return pl.BlockSpec(s, lambda i, d: (0,) * len(s))

        shapes = [(model, 3 * width), (model, width), (model // piece, 8, 2 * width)]
        return pl.pallas_call(
            functools.partial(project_kernel, index, moves, piece, part, halves),
            grid_spec=pltpu.PrefetchScalarGridSpec(
                num_scalar_prefetch=1,
                grid=(2 * halves,),
                in_specs=split_specs(block, model, halves) + [whole(a.shape) for a in arrays],
                out_specs=[pl.BlockSpec((block, 3 * width), lambda i, d: (i, 0))] + [whole(s) for s in shapes],
                scratch_shapes=[pltpu.VMEM((8, 3 * width), F32)],
            ),
            out_shape=[jax.ShapeDtypeStruct(s, BF16) for s in [(2 * rows, 3 * width), *shapes]],
            cost_estimate=CHEAP,
            name="project_kernel",
        )(where(), own, other, *arrays)
    slices = [(lead, slice(0, n), *rest) for lead, n, *rest in moves]
    slices.append(((), slice(piece, piece + 8), 0, 2 * part, 2, (0, 2 * part)))
    w, o, ext = ordered(spreads, slices)
    bias = jnp.sum(ext[:, 3].astype(F32), axis=0).reshape(2, 2, part)
    bias = jnp.concatenate([bias[:, 0].reshape(-1), jnp.zeros((width,), F32), bias[:, 1].reshape(-1)])
    w, o = w.reshape(model, -1), o.reshape(model, -1)
    return (dot_nn(jnp.concatenate([own, other]), w) + bias[None]).astype(BF16), w, o, ext


def feed(spreads, own, other, bias, piece, block):
    rows, model = own.shape
    halves = rows // block
    moves = [((k,), piece, 0, model, k, (0, model)) for k in range(2)]
    if piece % 16 == 0:
        arrays, index = joined(spreads)

        def whole(s):
            return pl.BlockSpec(s, lambda i, d: (0,) * len(s))

        wide = pl.BlockSpec((block, 2 * model), lambda i, d: (i, 0))
        return pl.pallas_call(
            functools.partial(feed_kernel, index, moves, halves),
            grid_spec=pltpu.PrefetchScalarGridSpec(
                num_scalar_prefetch=1,
                grid=(2 * halves,),
                in_specs=split_specs(block, model, halves) + [whole(a.shape) for a in [bias, *arrays]],
                out_specs=[wide, wide, *split_specs(block, model, halves)] + [whole((model, 2 * model))] * 2,
            ),
            out_shape=[jax.ShapeDtypeStruct((2 * rows, 2 * model), BF16)] * 2
            + [jax.ShapeDtypeStruct((rows, model), F32), jax.ShapeDtypeStruct((rows, model), BF16)]
            + [jax.ShapeDtypeStruct((model, 2 * model), BF16)] * 2,
            cost_estimate=CHEAP,
            name="feed_kernel",
        )(where(), own, other, bias, *arrays)
    b, c = ordered(spreads, [(lead, slice(0, n), *rest) for lead, n, *rest in moves])
    b, c = b.reshape(model, -1), c.reshape(model, -1)
    hidden, slope = gelu_both(dot_nn(jnp.concatenate([own, other]), b) + bias)
    part = dot_nt(hidden, c)
    return hidden, slope, part[:rows], part[rows:].astype(BF16), b, c


def where():
    return jnp.stack([lax.axis_index("dp"), lax.axis_index("c")]).astype(jnp.int32)


def sum_kernel(parts, piece, extra, part, where_ref, *refs):
    count = 1 + max(max(*p[0], p[1]) for p in parts)
    ins = refs[:count]
    scratch = refs[count + (3 if extra else 0) :]
    outs, left_ref, acc, ext_ref = scratch[:2], scratch[2], scratch[3], scratch[4]
    dp, step = where_ref[0], pl.program_id(0)
    outer = outs[0].shape[0] // 2
    blocked = parts[0][4]
    if extra:
        lines_ref, up_ref, bias_ref = refs[count : count + 3]
        model = lines_ref.shape[1]
        for rx in range(2):
            ext_ref[rx] = jnp.zeros(ext_ref.shape[1:], F32)
            ext_ref[rx, 0:1, :] = up_ref[0:1, rx * model : (rx + 1) * model]
            ext_ref[rx, 1:7, :] = lines_ref[0:6, :]
            for k in range(2):
                ext_ref[rx, extra - 1 : extra, k * part : (k + 1) * part] = bias_ref[
                    0:1, (2 * k + rx) * part : (2 * k + rx + 1) * part
                ]

    def turned(own, other):
        half = ins[own].shape[0]
        left_ref[:, :half] = ins[own][...].T
        left_ref[:, half:] = ins[other][...].T

    for k, ((own, other), right, width, at, by_block) in enumerate(parts):
        if by_block:

            @pl.when(step == 0)
            def _():
                turned(own, other)

            for lanes in chunks(width, 256):
                acc[:, lanes] = dot_nn(left_ref[...], ins[right][:, lanes]).astype(BF16)
        else:

            @pl.when(step == 0)
            def _():
                if k == 0 or parts[k - 1][0] != (own, other):
                    turned(own, other)
                for j in range(ins[right].shape[1] // (2 * width)):
                    both = dot_nn(left_ref[...], ins[right][:, 2 * j * width : 2 * (j + 1) * width]).astype(BF16)
                    for rx in range(2):
                        lanes = slice(rx * acc.shape[1] // 2 + at + j * width, rx * acc.shape[1] // 2 + at + (j + 1) * width)
                        acc[:, lanes] = both[:, rx * width : (rx + 1) * width]

    span = outs[0].shape[2]

    def put(rx):
        lanes = slice(0, span) if blocked else slice(rx * span, (rx + 1) * span)
        for parity in range(2):

            @pl.when(where_ref[1] == parity)
            def _():
                for ry in range(2):
                    first, second = (ry, rx) if parity else (rx, ry)

                    def move(z, carry):
                        rows = pl.ds(pl.multiple_of(jnp.bitwise_xor(dp, 2 * z + ry) * piece, 16), piece)
                        outs[first][second * outer + z, :piece, :] = acc[rows, lanes]
                        if extra:
                            outs[first][second * outer + z, piece:, :] = ext_ref[rx].astype(BF16)
                        return carry

                    lax.fori_loop(0, outer, move, 0)

    for rx in range(2):
        if blocked:
            pl.when(step == rx)(functools.partial(put, rx))
        else:
            put(rx)


def summed(arrays, parts, lines=None, bias_up=None, bias=None):
    ndp = lax.axis_size("dp")
    model = arrays[0].shape[1]
    piece = model // ndp
    blocked = parts[0][4]
    width = sum(p[2] if p[4] else arrays[p[1]].shape[1] // 2 for p in parts)
    extra = 0 if lines is None else 8
    if piece % 16 == 0:

        def whole(s):
            return pl.BlockSpec(s, lambda i, d: (0,) * len(s))

        given = list(arrays) + ([] if lines is None else [lines, bias_up, bias])
        specs = [whole(a.shape) for a in given]
        if blocked:
            right = parts[0][1]
            specs[right] = pl.BlockSpec((arrays[right].shape[0], width), lambda i, d: (0, i))
        shape = (ndp, piece + extra, width)
        return pl.pallas_call(
            functools.partial(sum_kernel, parts, piece, extra, 0 if bias is None else bias.shape[1] // 4),
            grid_spec=pltpu.PrefetchScalarGridSpec(
                num_scalar_prefetch=1,
                grid=(2 if blocked else 1,),
                in_specs=specs,
                out_specs=[whole(shape)] * 2,
                scratch_shapes=[
                    pltpu.VMEM((model, 2 * arrays[0].shape[0]), BF16),
                    pltpu.VMEM((model, width if blocked else 2 * width), BF16),
                    pltpu.VMEM((2, max(extra, 8), width), F32),
                ],
            ),
            out_shape=[jax.ShapeDtypeStruct(shape, BF16)] * 2,
            cost_estimate=CHEAP,
        compiler_params=pltpu.CompilerParams(vmem_limit_bytes=40 * 1024 * 1024),
        name="sum_units",
        )(where(), *given)
    order = jnp.bitwise_xor(jnp.arange(ndp), lax.axis_index("dp"))
    sides = []
    if extra:
        line = jnp.transpose(bias.reshape(2, 2, -1), (1, 0, 2)).reshape(2, -1)
        line = jnp.pad(line, ((0, 0), (0, width - line.shape[1]))).astype(BF16)
        both = jnp.broadcast_to(lines.astype(BF16)[None], (2, *lines.shape))
        ext = jnp.concatenate([bias_up.astype(BF16).reshape(2, 1, -1), both, line[:, None]], axis=1)
    for rx in range(2):
        g = []
        for (own, other), right, cols, _, by_block in parts:
            left = jnp.concatenate([arrays[own], arrays[other]])
            for j in range(1 if by_block else arrays[right].shape[1] // (2 * cols)):
                at = (2 * j + rx) * cols
                g.append(dot_tn(left, arrays[right][:, at : at + cols]).astype(BF16))
        g = jnp.concatenate(g, axis=1).reshape(ndp, piece, width)
        if extra:
            g = jnp.concatenate([g, jnp.broadcast_to(ext[rx][None], (ndp, extra, width))], axis=1)
        g = jnp.take(g, order, axis=0).reshape(ndp // 2, 2, piece + extra, width)
        sides.append(jnp.moveaxis(g, 1, 0))
    g = jnp.stack(sides)
    g = jnp.where(lax.axis_index("c") == 0, g, jnp.swapaxes(g, 0, 1))
    return g[0].reshape(ndp, piece + extra, width), g[1].reshape(ndp, piece + extra, width)


class Scatter:
    def __init__(self, pair):
        self.keep, self.send = pair

    def first(self):
        self.one = turn(self.send, 0)

    def second(self):
        half = self.keep.shape[0] // 2
        self.kept = add(self.keep[:half], self.one[:half])
        self.two = turn(add(self.keep[half:], self.one[half:]), 1)

    def third(self):
        total = add(self.kept, self.two)
        outer = total.shape[0]
        if outer <= 4:
            self.last = [total[0]]
            self.three = [flip(total[k], "dp", 2 * k) for k in range(1, outer)]
            return
        for k in reversed(range(outer_bits())):
            half = total.shape[0] // 2
            total = add(total[:half], flip(total[half:], "dp", 2 << k))
        self.last, self.three = [total[0]], []

    def result(self):
        return sum(t.astype(F32) for t in self.last + self.three)


def local(
    tokens, grad_out, seg_ids, w_qkv, b_qv, w_out, w_up, b_up, w_down, b_out, b_down, g_one, s_one, g_two, s_two
):
    ndp = lax.axis_size("dp")
    nx = lax.axis_size("x")
    parity = lax.axis_index("c")
    which = lax.axis_index("x")
    place_dp = lax.axis_index("dp")
    rows, model = tokens.shape
    piece = model // ndp
    part = w_qkv.shape[2]
    width = nx * part
    slim = model // (ndp * nx * 2)
    qv = part // ndp
    extra = 8
    block = 256
    tall = 512

    unit_a, unit_bc = prepare(
        w_qkv, w_out, w_up, w_down, b_qv, [b_out, b_down, g_one, s_one, g_two, s_two, b_up]
    )
    a_near = Spread(jnp.stack([unit_a, flip(unit_a, "dp", 2)]), 0)

    class Box:
        pass

    box = Box()
    box.bc = unit_bc
    a_near.units = stage("z1", a_near.units, bc=(box, "bc"))
    a_far = Spread(gather_far(a_near.units), 2)
    a_near.first()
    a_near.one = stage("n1", a_near.one, bc=(box, "bc"), az=(a_far, "units"))
    a_near.second()
    a_far.units = stage("z2", a_far.units, bc=(box, "bc"), an2=(a_near, "two"))
    a_far.first()
    bc_near = Spread(jnp.stack([box.bc, flip(box.bc, "dp", 2)]), 0)
    a_far.one = stage("f1", a_far.one, bz1=(bc_near, "units"), an2=(a_near, "two"))
    a_far.second()
    bc_far = Spread(gather_far(bc_near.units), 2)
    bc_items = lambda: dict(bn1=(bc_near, "one"), bz2=(bc_far, "units"), bn2=(bc_near, "two"), bf1=(bc_far, "one"), bf2=(bc_far, "two"))
    done = set()

    def advance(name, *values):
        res = stage(name, *values, **{k: v for k, v in bc_items().items() if hasattr(*v)})
        order = ["z2", "f1", "f2", "qkv", "ctx", "attn", "normed", "feed"]
        at = order.index(name)
        ready = lambda k: k is None or order.index(OPT.get(k, "feed")) <= at
        if "n1" not in done and order.index(OPT.get("rn1", "z2")) <= at:
            bc_near.first()
            done.add("n1")
        if "n2" not in done and "n1" in done and (ready("bn1") or name == "feed"):
            bc_near.second()
            done.add("n2")
        if "f1" not in done and (ready("bz2") or name == "feed"):
            bc_far.first()
            done.add("f1")
        if "f2" not in done and "f1" in done and (ready("bf1") or name == "feed"):
            bc_far.second()
            done.add("f2")
        return res

    advance("z2")
    a_far.two = advance("f2", a_far.two)

    seg = lax.dynamic_index_in_dim(seg_ids, which, 0, keepdims=False).reshape(2, rows)
    seg_rel = jnp.concatenate(
        [
            lax.dynamic_index_in_dim(seg, parity, 0, keepdims=False),
            lax.dynamic_index_in_dim(seg, 1 - parity, 0, keepdims=False),
        ]
    )
    seg_col = seg_rel[:, None]
    seg_row = seg_rel[None, :]
    x_other = swap(tokens)

    qkv, w_all, o_t, ext = project([a_near, a_far], tokens, x_other, piece, part, block)
    ext = ext[:, :3].astype(F32)
    ext = (ext[:, 0] + ext[:, 1] + ext[:, 2]).reshape(ndp, nx, 2 * part)
    bias_up = jnp.transpose(ext[:, :, 6 * slim : 6 * slim + piece], (1, 0, 2)).reshape(1, nx * model)
    six = ext[:, :, : 6 * slim]
    six = jnp.stack([six, swap(six)], axis=2)
    six = jnp.where(lax.broadcasted_iota(jnp.int32, (1, 1, 2, 1), 2) == parity, six[:, :, :1], six[:, :, 1:])
    six = jnp.where(which == 0, six, six[:, ::-1]).reshape(ndp * nx * 2, 6, slim)
    vectors = jnp.transpose(six, (1, 0, 2)).reshape(6, model)
    bout_f, bdown_f, gone_f, sone_f, gtwo_f, stwo_f = [vectors[i : i + 1] for i in range(6)]

    qkv = advance("qkv", qkv)
    ctx, lse = attention_forward(qkv, seg_col, seg_row, tall, 0, 2 * rows // tall, ())
    ctx = advance("ctx", ctx)
    attn_send = dot_nt(ctx[rows:], o_t).astype(BF16)
    attn = dot_nt(ctx[:rows], o_t) + swap(attn_send).astype(F32)
    attn = advance("attn", attn)
    first = tokens.astype(F32) + attn + bout_f
    hat_one, inv_one = normalize(first)
    normed = hat_one * gone_f + sone_f
    normed_low = advance("normed", normed.astype(BF16))
    normed_other = swap(normed_low)
    normed_other = advance("feed", normed_other)
    hidden, slope, keep, send, b_all, c_all = feed([bc_near, bc_far], normed_low, normed_other, bias_up, piece, block)
    branch = keep + swap(send).astype(F32)
    second = normed + branch + bdown_f
    hat_two, inv_two = normalize(second)
    layer_out = (hat_two * gtwo_f + stwo_f).astype(BF16)

    g_in = grad_out.astype(F32)
    d_gain_two = jnp.sum(g_in * hat_two, axis=0)
    d_shift_two = jnp.sum(g_in, axis=0)
    d_second = normalize_back(hat_two, inv_two, gtwo_f, g_in)
    d_branch = d_second.astype(BF16)
    d_bias_down = jnp.sum(d_branch.astype(F32), axis=0)
    db_other = swap(d_branch)

    sc = sb = sa = None
    order = ["P0", "P1", "P2", "P3", "P4", "P5", "P6", "P7"]
    sent = set()

    def go(name, *values):
        items = {}
        for k, s in (("c", sc), ("b", sb)):
            if s is not None:
                for n, f in (("1", "one"), ("2", "two"), ("3", "three")):
                    if hasattr(s, f):
                        items[k + n] = (s, f)
        res = stage(name, *values, **items)
        at = order.index(name)
        for k, s in (("c", sc), ("b", sb)):
            if s is None:
                continue
            for n, need, f in ((1, None, "first"), (2, "1", "second"), (3, "2", "third")):
                if k + str(n) in sent or (n > 1 and k + str(n - 1) not in sent):
                    continue
                if n == 1 or order.index(OPT.get(k + need, "P7")) <= at:
                    getattr(s, f)()
                    sent.add(k + str(n))
        return res

    keep, send, d_bias_up, *pairs = feed_back(
        d_branch, db_other, normed_low, normed_other, slope, hidden, c_all, b_all, piece
    )
    sc, sb = Scatter(pairs[:2]), Scatter(pairs[2:])
    go("P0")
    d_normed = d_second + keep + swap(send).astype(F32)
    d_normed = go("P1", d_normed)
    d_gain_one = jnp.sum(d_normed * hat_one, axis=0)
    d_shift_one = jnp.sum(d_normed, axis=0)
    d_first = normalize_back(hat_one, inv_one, gone_f, d_normed)
    d_attn = d_first.astype(BF16)
    d_bias_out = jnp.sum(d_attn.astype(F32), axis=0)
    da_other = swap(d_attn)
    d_ctx = dot_nn(d_attn, o_t).astype(BF16)
    sums = jnp.stack([d_bias_out, d_bias_down, d_gain_one, d_shift_one, d_gain_two, d_shift_two])
    sums = sums + swap(sums)
    d_ctx_other = dot_nn(da_other, o_t).astype(BF16)
    d_ctx_other, sums = go("P2", d_ctx_other, sums)
    d_qkv, bias = attention_backward(qkv, ctx, lse, d_ctx, d_ctx_other, seg_col, seg_row, block)
    d_qkv = go("P3", d_qkv)
    attention_parts = [((0, 1), 2, part, 0, False), ((3, 4), 5, part, 3 * part, False)]
    given = [tokens, x_other, d_qkv, d_attn, da_other, ctx]
    sa = Scatter(summed(given, attention_parts, sums, d_bias_up, bias))
    d_qkv, sa.send = go("P4", d_qkv, sa.send)
    sa.first()
    keep, send = input_gradient(d_qkv, d_first, w_all, block)
    sa.one, keep, send = go("P5", sa.one, keep, send)
    sa.second()
    input_grad = keep + swap(send).astype(F32)
    sa.two, input_grad = go("P6", sa.two, input_grad)
    sa.third()
    go("P7")
    input_grad = input_grad.astype(BF16)
    gc = sc.result()
    gb = sb.result()
    ga = sa.result()
    g_qkv = jnp.stack([ga[:piece, j * part : (j + 1) * part] for j in range(3)])
    tail = ga[piece:]
    g_bqv = lax.dynamic_slice_in_dim(tail[7, : 2 * part].reshape(2, part), place_dp * qv, qv, axis=1)
    g_bup = lax.dynamic_slice_in_dim(tail[0], place_dp * piece, piece)
    six = lax.dynamic_slice_in_dim(tail[1:7], ((place_dp * nx + which) * 2 + parity) * slim, slim, axis=1)
    return (
        layer_out,
        input_grad,
        g_qkv,
        g_bqv,
        ga[:piece, 3 * part :].T,
        gb,
        g_bup,
        gc.T,
        *[six[i] for i in range(6)],
    )


def solution(mesh):
    ndp, nt = mesh.devices.shape
    fine = Mesh(mesh.devices.reshape(ndp, nt // 2, 2), ("dp", "x", "c"))
    tensor = ("x", "c")
    every = ("dp", "x", "c")
    row = P(every, None)
    vec = P(every)
    return jax.shard_map(
        local,
        mesh=fine,
        in_specs=(
            row,
            row,
            P("dp", None),
            P(None, "dp", tensor),
            P(None, ("x", "c", "dp")),
            P(tensor, "dp"),
            P("dp", tensor),
            P(("x", "c", "dp")),
            P(tensor, "dp"),
            vec,
            vec,
            vec,
            vec,
            vec,
            vec,
        ),
        out_specs=(
            row,
            row,
            P(None, "dp", tensor),
            P(None, ("x", "c", "dp")),
            P(tensor, "dp"),
            P("dp", tensor),
            P(("x", "c", "dp")),
            P(tensor, "dp"),
            vec,
            vec,
            vec,
            vec,
            vec,
            vec,
        ),
        check_vma=False,
    )
```

```python
import functools

import jax
import jax.numpy as jnp
from jax import lax
from jax.experimental import pallas as pl
from jax.experimental.pallas import tpu as pltpu
from jax.sharding import Mesh, PartitionSpec as P

HD = 64
LANES = 128
EPSILON = 1e-05
ROOT_HALF = 0.7071067811865476
INV_ROOT_TWO_PI = 0.3989422804014327
F32 = jnp.float32
BF16 = jnp.bfloat16


def dot(a, b, dims):
    return lax.dot_general(a, b, (dims, ((), ())), preferred_element_type=F32)


def dot_nn(a, b):
    return dot(a, b, ((1,), (0,)))


def dot_nt(a, b):
    return dot(a, b, ((1,), (1,)))


def dot_tn(a, b):
    return dot(a, b, ((0,), (0,)))


CHEAP = pl.CostEstimate(flops=1000, bytes_accessed=1000, transcendentals=0)


def attention_forward_kernel(width, seg_q_ref, seg_k_ref, q_ref, k_ref, v_ref, *refs):
    ctx_ref, lse_ref = refs[-2:]
    lane = lax.broadcasted_iota(jnp.int32, (1, LANES), 1)
    bias = jnp.where(seg_q_ref[...] == seg_k_ref[...], 0.0, -1000000000.0)
    block = q_ref.shape[0]

    stats = jnp.zeros((block, LANES), F32)
    for tile in range(width // LANES):
        cols = slice(tile * LANES, (tile + 1) * LANES)
        q2 = q_ref[:, cols] * jnp.asarray(0.125, BF16)
        k2 = k_ref[:, cols]
        v2 = v_ref[:, cols]
        outs = []
        for half in range(2):
            qm = jnp.where((lane // HD) == half, q2, jnp.zeros_like(q2))
            s = dot_nt(qm, k2) + bias
            top = jnp.max(s, axis=-1, keepdims=True)
            e = jnp.exp(s - top)
            total = jnp.sum(e, axis=-1, keepdims=True)
            outs.append(dot_nn(e.astype(BF16), v2) * (1.0 / total))
            stats = jnp.where(lane == 2 * tile + half, top + jnp.log(total), stats)
        ctx_ref[:, cols] = jnp.where(lane < HD, outs[0], outs[1]).astype(BF16)
    lse_ref[...] = stats.T[: lse_ref.shape[0], :]


def attention_forward(qkv, seg_col, seg_row, block, first, count, made):
    rows, triple = qkv.shape
    width = triple // 3
    return pl.pallas_call(
        functools.partial(attention_forward_kernel, width),
        grid=(count,),
        in_specs=[
            pl.BlockSpec((block, 1), lambda i: (first + i, 0)),
            pl.BlockSpec((1, rows), lambda i: (0, 0)),
            pl.BlockSpec((block, width), lambda i: (first + i, 0)),
            pl.BlockSpec((rows, width), lambda i: (0, 1)),
            pl.BlockSpec((rows, width), lambda i: (0, 2)),
        ]
        + [pl.BlockSpec(memory_space=pl.ANY)] * len(made),
        out_specs=[
            pl.BlockSpec((block, width), lambda i: (first + i, 0)),
            pl.BlockSpec((8, block), lambda i: (0, first + i)),
        ],
        out_shape=[
            jax.ShapeDtypeStruct((rows, width), BF16),
            jax.ShapeDtypeStruct((8, rows), F32),
        ],
        input_output_aliases={5 + i: i for i in range(len(made))},
        cost_estimate=CHEAP,
        compiler_params=pltpu.CompilerParams(vmem_limit_bytes=30 * 1024 * 1024),
        name="attention_forward",
    )(seg_col, seg_row, qkv, qkv, qkv, *made)


def split_specs(block, columns, halves):
    return [
        pl.BlockSpec((block, columns), lambda i, *_: (jnp.minimum(i, halves - 1), 0)),
        pl.BlockSpec((block, columns), lambda i, *_: (jnp.maximum(i - halves, 0), 0)),
    ]


def either(step, halves, own_ref, other_ref):
    return jnp.where(step < halves, own_ref[...], other_ref[...])


def attention_backward_kernel(
    width, halves, seg_k_ref, seg_q_ref, q_ref, k_ref, v_ref, ctx_ref, lse_ref, own_ref, other_ref, out_ref, sum_ref, dk_ref, dv_ref
):
    step = pl.program_id(0)
    block = q_ref.shape[0]
    lane = lax.broadcasted_iota(jnp.int32, (1, LANES), 1)

    @pl.when(step == 0)
    def _():
        dk_ref[...] = jnp.zeros_like(dk_ref)
        dv_ref[...] = jnp.zeros_like(dv_ref)
        sum_ref[...] = jnp.zeros_like(sum_ref)

    bias = jnp.where(seg_k_ref[...] == seg_q_ref[...], 0.0, -1000000000.0)
    for pair in range(width // LANES):
        cols = slice(pair * LANES, (pair + 1) * LANES)
        q2 = q_ref[:, cols] * jnp.asarray(0.125, BF16)
        k2 = k_ref[:, cols]
        v2 = v_ref[:, cols]
        d2 = jnp.where(step < halves, own_ref[:, cols], other_ref[:, cols])
        prod = (d2.astype(F32) * ctx_ref[:, cols].astype(F32)).T
        kt = (k2 * jnp.asarray(0.125, BF16)).T
        row = lax.broadcasted_iota(jnp.int32, (LANES, 1), 0)
        dq = None
        dk = None
        dv = None
        for half in range(2):
            mine = (lane // HD) == half
            qm = jnp.where(mine, q2, jnp.zeros_like(q2))
            dm = jnp.where(mine, d2, jnp.zeros_like(d2))
            ktm = jnp.where((row // HD) == half, kt, jnp.zeros_like(kt))
            inner = jnp.sum(prod[half * HD : (half + 1) * HD, :], axis=0, keepdims=True)
            lse = lse_ref[2 * pair + half : 2 * pair + half + 1, :]
            p = jnp.exp(dot_nt(k2, qm) + bias - lse)
            dp = dot_nt(v2, dm)
            ds = (p * (dp - inner)).astype(BF16)
            dv_h = dot_nn(p.astype(BF16), dm)
            dk_h = dot_nn(ds, qm)
            dq_h = dot_nn(ktm, ds)
            dv = dv_h if dv is None else dv + dv_h
            dk = dk_h if dk is None else dk + dk_h
            dq = dq_h if dq is None else dq + dq_h
        dk_ref[:, cols] += dk
        dv_ref[:, cols] += dv
        dq = dq.T.astype(BF16)
        out_ref[pl.ds(pl.multiple_of(step * block, block), block), cols] = dq
        sum_ref[:, cols] += jnp.sum(dq.astype(F32), axis=0, keepdims=True)

    @pl.when(step == pl.num_programs(0) - 1)
    def _():
        out_ref[:, width : 2 * width] = dk_ref[...].astype(BF16)
        dv = dv_ref[...].astype(BF16)
        out_ref[:, 2 * width : 3 * width] = dv
        sum_ref[:, width : 2 * width] = jnp.sum(dv.astype(F32), axis=0, keepdims=True)


def attention_backward(qkv, ctx, lse, d_own, d_other, seg_col, seg_row, block):
    rows, triple = qkv.shape
    width = triple // 3
    halves = rows // block // 2
    return pl.pallas_call(
        functools.partial(attention_backward_kernel, width, halves),
        grid=(rows // block,),
        in_specs=[
            pl.BlockSpec((rows, 1), lambda i: (0, 0)),
            pl.BlockSpec((1, block), lambda i: (0, i)),
            pl.BlockSpec((block, width), lambda i: (i, 0)),
            pl.BlockSpec((rows, width), lambda i: (0, 1)),
            pl.BlockSpec((rows, width), lambda i: (0, 2)),
            pl.BlockSpec((block, width), lambda i: (i, 0)),
            pl.BlockSpec((8, block), lambda i: (0, i)),
            *split_specs(block, width, halves),
        ],
        out_specs=[pl.BlockSpec((rows, triple), lambda i: (0, 0)), pl.BlockSpec((1, 2 * width), lambda i: (0, 0))],
        out_shape=[jax.ShapeDtypeStruct((rows, triple), BF16), jax.ShapeDtypeStruct((1, 2 * width), F32)],
        scratch_shapes=[pltpu.VMEM((rows, width), F32), pltpu.VMEM((rows, width), F32)],
        cost_estimate=CHEAP,
        compiler_params=pltpu.CompilerParams(vmem_limit_bytes=30 * 1024 * 1024),
        name="attention_backward",
    )(seg_col, seg_row, qkv, qkv, qkv, ctx, lse, d_own, d_other)


def input_kernel(halves, d_ref, first_ref, w_ref, keep_ref, send_ref):
    step = pl.program_id(0)
    part = dot_nt(d_ref[...], w_ref[...])

    @pl.when(step < halves)
    def _():
        keep_ref[...] = first_ref[...] + part

    @pl.when(step >= halves)
    def _():
        send_ref[...] = part.astype(BF16)


def input_gradient(d_qkv, d_first, w_all, block):
    rows, model = d_first.shape
    width = d_qkv.shape[1]
    halves = rows // block
    by_row = pl.BlockSpec((block, width), lambda i: (i, 0))
    own = pl.BlockSpec((block, model), lambda i: (jnp.minimum(i, halves - 1), 0))
    return pl.pallas_call(
        functools.partial(input_kernel, halves),
        grid=(2 * halves,),
        in_specs=[by_row, own, pl.BlockSpec(w_all.shape, lambda i: (0, 0))],
        out_specs=split_specs(block, model, halves),
        out_shape=[jax.ShapeDtypeStruct((rows, model), F32), jax.ShapeDtypeStruct((rows, model), BF16)],
        cost_estimate=CHEAP,
        name="input_gradient",
    )(d_qkv, d_first, w_all)


def normalize(r):
    mean = jnp.mean(r, axis=-1, keepdims=True)
    cent = r - mean
    var = jnp.mean(cent * cent, axis=-1, keepdims=True)
    inv = lax.rsqrt(var + EPSILON)
    return cent * inv, inv


def normalize_back(hat, inv, gain, d_out):
    d_hat = d_out * gain
    first = jnp.mean(d_hat, axis=-1, keepdims=True)
    second = jnp.mean(d_hat * hat, axis=-1, keepdims=True)
    return inv * (d_hat - first - hat * second)


def column_sums(sum_ref, *rows):
    @pl.when(pl.program_id(0) == 0)
    def _():
        sum_ref[...] = jnp.zeros_like(sum_ref)

    for k, r in enumerate(rows):
        sum_ref[k : k + 1, :] += jnp.sum(r, axis=0, keepdims=True)


def second_norm_kernel(keep_ref, got_ref, hat_ref, grad_ref, vec_ref, out_ref, low_ref, d_ref, sum_ref):
    vec = vec_ref[...]
    bias, gain_one, shift_one, gain, shift = [vec[k : k + 1] for k in range(1, 6)]
    second = hat_ref[...] * gain_one + shift_one + keep_ref[...] + got_ref[...].astype(F32) + bias
    hat, inv = normalize(second)
    out_ref[...] = (hat * gain + shift).astype(BF16)
    grad = grad_ref[...].astype(F32)
    d = normalize_back(hat, inv, gain, grad)
    d_ref[...] = d
    low = d.astype(BF16)
    low_ref[...] = low
    column_sums(sum_ref, low.astype(F32), grad * hat, grad)


def first_norm_kernel(keep_ref, got_ref, d_ref, hat_ref, inv_ref, vec_ref, low_ref, out_ref, sum_ref):
    hat = hat_ref[...]
    d_normed = d_ref[...] + keep_ref[...] + got_ref[...].astype(F32)
    d = normalize_back(hat, inv_ref[...], vec_ref[2:3, :], d_normed)
    out_ref[...] = d
    low = d.astype(BF16)
    low_ref[...] = low
    column_sums(sum_ref, low.astype(F32), d_normed * hat, d_normed)


def norm_call(kernel, block, arrays, vectors, types):
    rows, model = arrays[0].shape

    def by_row(n):
        return pl.BlockSpec((block, n), lambda i: (i, 0))

    fixed = pl.BlockSpec((8, model), lambda i: (0, 0))
    return pl.pallas_call(
        kernel,
        grid=(rows // block,),
        in_specs=[by_row(a.shape[1]) for a in arrays] + [fixed],
        out_specs=[by_row(model) for _ in types] + [fixed],
        out_shape=[jax.ShapeDtypeStruct((rows, model), t) for t in types] + [jax.ShapeDtypeStruct((8, model), F32)],
        cost_estimate=CHEAP,
        compiler_params=pltpu.CompilerParams(vmem_limit_bytes=30 * 1024 * 1024),
        name=kernel.__name__,
    )(*arrays, vectors)


def swap(a):
    return lax.ppermute(a, "c", [(0, 1), (1, 0)])


def flip(a, axis, bit):
    n = lax.axis_size(axis)
    return lax.ppermute(a, axis, [(i, i ^ bit) for i in range(n)])


def turn(a, level):
    n, nx = lax.axis_size("dp"), lax.axis_size("x")
    pairs = []
    for d in range(n):
        for x in range(nx):
            for c in range(2):
                other = (d * nx + (x ^ 1)) if (c + level) % 2 == 0 else ((d ^ 1) * nx + x)
                pairs.append(((d * nx + x) * 2 + c, other * 2 + c))
    return lax.ppermute(a, ("dp", "x", "c"), pairs)


def tie(*values):
    return lax.optimization_barrier(values)


def add(*terms):
    return sum(t.astype(F32) for t in terms).astype(BF16)


def outer_bits():
    return lax.axis_size("dp").bit_length() - 2


def gather_far(near):
    parts = [near]
    for k in range(1, outer_bits()):
        held = jnp.concatenate(parts) if len(parts) > 1 else near
        parts.append(flip(held, "dp", 2 << k))
    return jnp.concatenate(parts[1:]) if len(parts) > 2 else parts[1]


OPT = {'bc': None, 'bn1': 'f2', 'bz2': 'qkv', 'bf1': 'ctx', 'bn2': 'ctx', 'bf2': 'attn', 'c1': 'P3', 'c2': 'P4', 'c3': 'P5', 'b1': 'P3', 'b2': 'P4', 'b3': 'P6', 'an2': 'f1', 'bz1': 'f1'}


def stage(name, *values, **items):
    keys = [k for k in items if OPT.get(k) == name]
    extra, spans = [], []
    for k in keys:
        v = getattr(*items[k])
        many = isinstance(v, list)
        spans.append((k, len(v) if many else 1, many))
        extra += v if many else [v]
    if len(values) + len(extra) > 1:
        out = list(tie(*values, *extra))
    else:
        out = [*values, *extra]
    res, at = out[: len(values)], len(values)
    for k, n, many in spans:
        setattr(*items[k], out[at : at + n] if many else out[at])
        at += n
    return res if len(res) > 1 else (res[0] if res else None)


class Spread:
    def __init__(self, units, outer):
        self.units, self.outer = units, outer

    def first(self):
        self.one = turn(self.units, 0)

    def second(self):
        self.two = turn(jnp.concatenate([self.units, self.one]), 1)

    def pieces(self):
        n = self.units.shape[0]
        index = [(0, u, self.outer + u, 0, 0) for u in range(n)]
        index += [(1, u, self.outer + u, 1, 0) for u in range(n)]
        index += [(2, a * n + u, self.outer + u, a, 1) for a in range(2) for u in range(n)]
        return [self.units, self.one, self.two], index


def joined(spreads):
    arrays, index = [], []
    for s in spreads:
        more, at = s.pieces()
        index += [(i + len(arrays), *rest) for i, *rest in at]
        arrays += more
    return arrays, index


def put_units(index, moves, where_ref, ins, outs, each=None):
    dp = where_ref[0]
    for parity in range(2):

        @pl.when(where_ref[1] == parity)
        def _():
            for array, unit, outer, first, second in index:
                rx, ry = (second, first) if parity else (first, second)
                to = jnp.bitwise_xor(dp, 2 * outer + ry)
                for lead, rows, col, cols, target, at in moves:
                    value = ins[array][(unit, *lead, slice(0, rows), slice(col, col + cols))]
                    outs[target][pl.ds(pl.multiple_of(to * rows, 16), rows), at[rx] : at[rx] + cols] = value
                if each is not None:
                    each(ins[array], unit, to, rx)


def prepare_kernel(piece, dp_ref, qkv_ref, out_ref, up_ref, down_ref, qv_ref, *refs):
    vectors, (a_ref, bc_ref, row_ref) = refs[:-3], refs[-3:]
    part = qkv_ref.shape[2]
    for j in range(3):
        a_ref[:piece, j * part : (j + 1) * part] = qkv_ref[j]
    a_ref[:piece, 3 * part :] = out_ref[...].T
    row_ref[...] = jnp.zeros_like(row_ref)
    at = 0
    for v in vectors:
        n = v.shape[1]
        row_ref[0:1, at : at + n] = v[...].astype(F32)
        at += n
    n = qv_ref.shape[1]
    lane = lax.broadcasted_iota(jnp.int32, (n, part), 1)
    spot = (lane == lax.broadcasted_iota(jnp.int32, (n, part), 0) + n * dp_ref[0]).astype(BF16)
    both = dot_nn(qv_ref[...], spot)
    row_ref[1:2, :part] = both[0:1]
    row_ref[1:2, part : 2 * part] = both[1:2]
    exact = row_ref[0:1, :]
    high = exact.astype(BF16).astype(F32)
    middle = (exact - high).astype(BF16).astype(F32)
    low = exact - high - middle
    line = lax.broadcasted_iota(jnp.int32, (8, 1), 0)
    rows = jnp.where(line == 0, high, 0.0) + jnp.where(line == 1, middle, 0.0)
    rows += jnp.where(line == 2, low, 0.0) + jnp.where(line == 3, row_ref[1:2, :], 0.0)
    a_ref[piece:, :] = rows.astype(BF16)
    bc_ref[0] = up_ref[...]
    bc_ref[1] = down_ref[...]


def prepare(w_qkv, w_out, w_up, w_down, b_qv, vectors):
    piece, part = w_qkv.shape[1:]
    model = w_up.shape[1]
    dp = lax.axis_index("dp").astype(jnp.int32)
    if piece % 16 == 0:

        def whole(s):
            return pl.BlockSpec(s, lambda i, d: (0,) * len(s))

        given = [w_qkv, w_out, w_up, w_down.T, b_qv, *[v[None] for v in vectors]]
        shapes = [(piece + 8, model), (2, piece, model)]
        return pl.pallas_call(
            functools.partial(prepare_kernel, piece),
            grid_spec=pltpu.PrefetchScalarGridSpec(
                num_scalar_prefetch=1,
                grid=(1,),
                in_specs=[whole(v.shape) for v in given],
                out_specs=[whole(s) for s in shapes],
                scratch_shapes=[pltpu.VMEM((8, model), F32)],
            ),
            out_shape=[jax.ShapeDtypeStruct(s, BF16) for s in shapes],
            cost_estimate=CHEAP,
            name="prepare_units",
        )(dp[None], *given)
    row = jnp.concatenate([v.astype(F32) for v in vectors])
    row = jnp.pad(row, (0, model - row.shape[0]))
    high = row.astype(BF16)
    middle = (row - high.astype(F32)).astype(BF16)
    low = (row - high.astype(F32) - middle.astype(F32)).astype(BF16)
    keep = lax.broadcasted_iota(jnp.int32, (1, part // b_qv.shape[1], 1), 1) == dp
    spot = jnp.where(keep, b_qv[:, None, :], jnp.zeros((), BF16)).reshape(-1)
    spot = jnp.pad(spot, (0, model - spot.shape[0]))
    tail = jnp.pad(jnp.stack([high, middle, low, spot]), ((0, 4), (0, 0)))
    unit = jnp.concatenate([w_qkv[0], w_qkv[1], w_qkv[2], w_out.T], axis=1)
    return jnp.concatenate([unit, tail], axis=0), jnp.stack([w_up, w_down.T])


def project_kernel(index, moves, piece, part, halves, where_ref, own_ref, other_ref, *refs):
    ins, (out_ref, w_ref, o_ref, ext_ref, bias_ref) = refs[:-5], refs[-5:]
    width = 2 * part

    @pl.when(pl.program_id(0) == 0)
    def _():
        bias_ref[...] = jnp.zeros_like(bias_ref)

        def each(source, unit, to, rx):
            value = source[unit, piece:, : 2 * part]
            ext_ref[to, :, 2 * part * rx : 2 * part * (rx + 1)] = value
            value = value.astype(F32)[3:4]
            bias_ref[0:1, rx * part : (rx + 1) * part] += value[:, :part]
            at = 2 * width + rx * part
            bias_ref[0:1, at : at + part] += value[:, part:]

        put_units(index, moves, where_ref, ins, (w_ref, o_ref), each)

    x = either(pl.program_id(0), halves, own_ref, other_ref)
    out_ref[...] = (dot_nn(x, w_ref[...]) + bias_ref[0:1, :]).astype(BF16)


def feed_kernel(index, moves, halves, where_ref, own_ref, other_ref, bias_ref, *refs):
    ins, (hidden_ref, slope_ref, keep_ref, send_ref, b_ref, c_ref) = refs[:-6], refs[-6:]
    step = pl.program_id(0)

    @pl.when(step == 0)
    def _():
        put_units(index, moves, where_ref, ins, (b_ref, c_ref))

    x = either(step, halves, own_ref, other_ref)
    hidden, slope = gelu_both(dot_nn(x, b_ref[...]) + bias_ref[...])
    hidden_ref[...] = hidden
    slope_ref[...] = slope
    part = dot_nt(hidden, c_ref[...])

    @pl.when(step < halves)
    def _():
        keep_ref[...] = part

    @pl.when(step >= halves)
    def _():
        send_ref[...] = part.astype(BF16)


def chunks(n, size=512):
    return [slice(at, min(at + size, n)) for at in range(0, n, size)]


def gelu_both(up):
    cdf = 0.5 * (1.0 + lax.erf(up * ROOT_HALF))
    slope = cdf + up * (jnp.exp(-0.5 * up * up) * INV_ROOT_TWO_PI)
    return (up * cdf).astype(BF16), slope.astype(BF16)


def feed_back_kernel(size, piece, where_ref, *refs):
    own_ref, other_ref, n_own_ref, n_other_ref, slope_ref, hidden_ref, c_ref, b_ref = refs[:8]
    keep_ref, send_ref, sum_ref, c_keep, c_send, b_keep, b_send = refs[8:15]
    d_ref, d_turned, n_turned, acc_ref, c_grad, b_grad = refs[15:]
    step, dp = pl.program_id(0), where_ref[0]
    half, model = own_ref.shape
    outer = c_keep.shape[0] // 2

    @pl.when(step == 0)
    def _():
        for at, d, n in ((0, own_ref, n_own_ref), (half, other_ref, n_other_ref)):
            d_ref[at : at + half, :] = d[...]
            d_turned[:, at : at + half] = d[...].T
            n_turned[:, at : at + half] = n[...].T

    d_up = (dot_nn(d_ref[...], c_ref[...]) * slope_ref[...].astype(F32)).astype(BF16)
    sum_ref[...] = jnp.sum(d_up.astype(F32), axis=0, keepdims=True)
    part = dot_nt(d_up, b_ref[...])

    @pl.when(step == 0)
    def _():
        acc_ref[...] = part

    @pl.when(step > 0)
    def _():
        acc_ref[...] += part

    c_grad[...] = dot_nn(d_turned[...], hidden_ref[...]).astype(BF16)
    b_grad[...] = dot_nn(n_turned[...], d_up).astype(BF16)
    width = c_ref.shape[1]
    for s in range(2 * model // width):
        for at in range(0, width, size):
            rx, to = divmod(s * width + at, model)
            for parity in range(2):

                @pl.when((step == s) & (where_ref[1] == parity))
                def _():
                    for ry in range(2):
                        first, second = (ry, rx) if parity else (rx, ry)
                        outs = ((c_send, b_send) if first else (c_keep, b_keep))

                        def move(z, carry):
                            rows = pl.ds(pl.multiple_of(jnp.bitwise_xor(dp, 2 * z + ry) * piece, 16), piece)
                            for out, grad in zip(outs, (c_grad, b_grad)):
                                out[second * outer + z, :, to : to + size] = grad[rows, at : at + size]
                            return carry

                        lax.fori_loop(0, outer, move, 0)

    @pl.when(step == pl.num_programs(0) - 1)
    def _():
        keep_ref[...] = acc_ref[:half, :]
        send_ref[...] = acc_ref[half:, :].astype(BF16)


def feed_back(d_own, d_other, n_own, n_other, slope, hidden, c, b, piece):
    rows, model = d_own.shape
    wide = b.shape[1]
    ndp = model // piece
    if piece % 16:
        d, n = jnp.concatenate([d_own, d_other]), jnp.concatenate([n_own, n_other])
        d_up = (dot_nn(d, c) * slope.astype(F32)).astype(BF16)
        part = dot_nt(d_up, b)
        sums = jnp.sum(d_up.astype(F32), axis=0, keepdims=True)
        wide_part = [((0, 1), 2, model, 0, True)]
        c_pair = summed([d_own, d_other, hidden], wide_part)
        b_pair = summed([n_own, n_other, d_up], wide_part)
        return part[:rows], part[rows:].astype(BF16), sums, *c_pair, *b_pair

    def whole(s):
        return pl.BlockSpec(s, lambda i, w: (0,) * len(s))

    def columns(n):
        return pl.BlockSpec((n, 512), lambda i, w: (0, i))

    units = (ndp, piece, model)
    return pl.pallas_call(
        functools.partial(feed_back_kernel, 256, piece),
        grid_spec=pltpu.PrefetchScalarGridSpec(
            num_scalar_prefetch=1,
            grid=(wide // 512,),
            in_specs=[whole((rows, model))] * 4 + [columns(2 * rows)] * 2 + [columns(model)] * 2,
            out_specs=[whole((rows, model))] * 2 + [columns(1)] + [whole(units)] * 4,
            scratch_shapes=[
                pltpu.VMEM((2 * rows, model), BF16),
                pltpu.VMEM((model, 2 * rows), BF16),
                pltpu.VMEM((model, 2 * rows), BF16),
                pltpu.VMEM((2 * rows, model), F32),
                pltpu.VMEM((model, 512), BF16),
                pltpu.VMEM((model, 512), BF16),
            ],
        ),
        out_shape=[
            jax.ShapeDtypeStruct((rows, model), F32),
            jax.ShapeDtypeStruct((rows, model), BF16),
            jax.ShapeDtypeStruct((1, wide), F32),
        ]
        + [jax.ShapeDtypeStruct(units, BF16)] * 4,
        cost_estimate=CHEAP,
        compiler_params=pltpu.CompilerParams(vmem_limit_bytes=52 * 1024 * 1024),
        name="feed_back",
    )(where(), d_own, d_other, n_own, n_other, slope, hidden, c, b)


def ordered(spreads, moves):
    arrays, index = joined(spreads)
    order = jnp.bitwise_xor(jnp.arange(lax.axis_size("dp")), lax.axis_index("dp"))
    made = {}
    for lead, rows, col, cols, target, at in moves:
        for rx in range(2):
            both = []
            for swapped in range(2):
                units = {}
                for array, unit, outer, first, second in index:
                    x, y = (second, first) if swapped else (first, second)
                    if x == rx:
                        units[2 * outer + y] = arrays[array][(unit, *lead)][rows, col : col + cols]
                both.append(jnp.stack([units[k] for k in sorted(units)]))
            stack = jnp.take(jnp.where(lax.axis_index("c") == 0, both[0], both[1]), order, axis=0)
            made.setdefault(target, []).append((at[rx], stack))
    return [jnp.concatenate([m for _, m in sorted(made[t], key=lambda p: p[0])], axis=-1) for t in sorted(made)]


def project(spreads, own, other, piece, part, block):
    width = 2 * part
    rows, model = own.shape
    halves = rows // block
    moves = [((), piece, j * part, part, 0, (j * width, j * width + part)) for j in range(3)]
    moves.append(((), piece, 3 * part, part, 1, (0, part)))
    if piece % 16 == 0:
        arrays, index = joined(spreads)

        def whole(s):
            return pl.BlockSpec(s, lambda i, d: (0,) * len(s))

        shapes = [(model, 3 * width), (model, width), (model // piece, 8, 2 * width)]
        return pl.pallas_call(
            functools.partial(project_kernel, index, moves, piece, part, halves),
            grid_spec=pltpu.PrefetchScalarGridSpec(
                num_scalar_prefetch=1,
                grid=(2 * halves,),
                in_specs=split_specs(block, model, halves) + [whole(a.shape) for a in arrays],
                out_specs=[pl.BlockSpec((block, 3 * width), lambda i, d: (i, 0))] + [whole(s) for s in shapes],
                scratch_shapes=[pltpu.VMEM((8, 3 * width), F32)],
            ),
            out_shape=[jax.ShapeDtypeStruct(s, BF16) for s in [(2 * rows, 3 * width), *shapes]],
            cost_estimate=CHEAP,
            name="project_kernel",
        )(where(), own, other, *arrays)
    slices = [(lead, slice(0, n), *rest) for lead, n, *rest in moves]
    slices.append(((), slice(piece, piece + 8), 0, 2 * part, 2, (0, 2 * part)))
    w, o, ext = ordered(spreads, slices)
    bias = jnp.sum(ext[:, 3].astype(F32), axis=0).reshape(2, 2, part)
    bias = jnp.concatenate([bias[:, 0].reshape(-1), jnp.zeros((width,), F32), bias[:, 1].reshape(-1)])
    w, o = w.reshape(model, -1), o.reshape(model, -1)
    return (dot_nn(jnp.concatenate([own, other]), w) + bias[None]).astype(BF16), w, o, ext


def feed(spreads, own, other, bias, piece, block):
    rows, model = own.shape
    halves = rows // block
    moves = [((k,), piece, 0, model, k, (0, model)) for k in range(2)]
    if piece % 16 == 0:
        arrays, index = joined(spreads)

        def whole(s):
            return pl.BlockSpec(s, lambda i, d: (0,) * len(s))

        wide = pl.BlockSpec((block, 2 * model), lambda i, d: (i, 0))
        return pl.pallas_call(
            functools.partial(feed_kernel, index, moves, halves),
            grid_spec=pltpu.PrefetchScalarGridSpec(
                num_scalar_prefetch=1,
                grid=(2 * halves,),
                in_specs=split_specs(block, model, halves) + [whole(a.shape) for a in [bias, *arrays]],
                out_specs=[wide, wide, *split_specs(block, model, halves)] + [whole((model, 2 * model))] * 2,
            ),
            out_shape=[jax.ShapeDtypeStruct((2 * rows, 2 * model), BF16)] * 2
            + [jax.ShapeDtypeStruct((rows, model), F32), jax.ShapeDtypeStruct((rows, model), BF16)]
            + [jax.ShapeDtypeStruct((model, 2 * model), BF16)] * 2,
            cost_estimate=CHEAP,
            name="feed_kernel",
        )(where(), own, other, bias, *arrays)
    b, c = ordered(spreads, [(lead, slice(0, n), *rest) for lead, n, *rest in moves])
    b, c = b.reshape(model, -1), c.reshape(model, -1)
    hidden, slope = gelu_both(dot_nn(jnp.concatenate([own, other]), b) + bias)
    part = dot_nt(hidden, c)
    return hidden, slope, part[:rows], part[rows:].astype(BF16), b, c


def where():
    return jnp.stack([lax.axis_index("dp"), lax.axis_index("c")]).astype(jnp.int32)


def sum_kernel(parts, piece, extra, part, where_ref, *refs):
    count = 1 + max(max(*p[0], p[1]) for p in parts)
    ins = refs[:count]
    scratch = refs[count + (3 if extra else 0) :]
    outs, left_ref, acc, ext_ref = scratch[:2], scratch[2], scratch[3], scratch[4]
    dp, step = where_ref[0], pl.program_id(0)
    outer = outs[0].shape[0] // 2
    blocked = parts[0][4]
    if extra:
        lines_ref, up_ref, bias_ref = refs[count : count + 3]
        model = lines_ref.shape[1]
        for rx in range(2):
            ext_ref[rx] = jnp.zeros(ext_ref.shape[1:], F32)
            ext_ref[rx, 0:1, :] = up_ref[0:1, rx * model : (rx + 1) * model]
            ext_ref[rx, 1:7, :] = lines_ref[0:6, :]
            for k in range(2):
                ext_ref[rx, extra - 1 : extra, k * part : (k + 1) * part] = bias_ref[
                    0:1, (2 * k + rx) * part : (2 * k + rx + 1) * part
                ]

    def turned(own, other):
        half = ins[own].shape[0]
        left_ref[:, :half] = ins[own][...].T
        left_ref[:, half:] = ins[other][...].T

    for k, ((own, other), right, width, at, by_block) in enumerate(parts):
        if by_block:

            @pl.when(step == 0)
            def _():
                turned(own, other)

            for lanes in chunks(width, 256):
                acc[:, lanes] = dot_nn(left_ref[...], ins[right][:, lanes]).astype(BF16)
        else:

            @pl.when(step == 0)
            def _():
                if k == 0 or parts[k - 1][0] != (own, other):
                    turned(own, other)
                for j in range(ins[right].shape[1] // (2 * width)):
                    both = dot_nn(left_ref[...], ins[right][:, 2 * j * width : 2 * (j + 1) * width]).astype(BF16)
                    for rx in range(2):
                        lanes = slice(rx * acc.shape[1] // 2 + at + j * width, rx * acc.shape[1] // 2 + at + (j + 1) * width)
                        acc[:, lanes] = both[:, rx * width : (rx + 1) * width]

    span = outs[0].shape[2]

    def put(rx):
        lanes = slice(0, span) if blocked else slice(rx * span, (rx + 1) * span)
        for parity in range(2):

            @pl.when(where_ref[1] == parity)
            def _():
                for ry in range(2):
                    first, second = (ry, rx) if parity else (rx, ry)

                    def move(z, carry):
                        rows = pl.ds(pl.multiple_of(jnp.bitwise_xor(dp, 2 * z + ry) * piece, 16), piece)
                        outs[first][second * outer + z, :piece, :] = acc[rows, lanes]
                        if extra:
                            outs[first][second * outer + z, piece:, :] = ext_ref[rx].astype(BF16)
                        return carry

                    lax.fori_loop(0, outer, move, 0)

    for rx in range(2):
        if blocked:
            pl.when(step == rx)(functools.partial(put, rx))
        else:
            put(rx)


def summed(arrays, parts, lines=None, bias_up=None, bias=None):
    ndp = lax.axis_size("dp")
    model = arrays[0].shape[1]
    piece = model // ndp
    blocked = parts[0][4]
    width = sum(p[2] if p[4] else arrays[p[1]].shape[1] // 2 for p in parts)
    extra = 0 if lines is None else 8
    if piece % 16 == 0:

        def whole(s):
            return pl.BlockSpec(s, lambda i, d: (0,) * len(s))

        given = list(arrays) + ([] if lines is None else [lines, bias_up, bias])
        specs = [whole(a.shape) for a in given]
        if blocked:
            right = parts[0][1]
            specs[right] = pl.BlockSpec((arrays[right].shape[0], width), lambda i, d: (0, i))
        shape = (ndp, piece + extra, width)
        return pl.pallas_call(
            functools.partial(sum_kernel, parts, piece, extra, 0 if bias is None else bias.shape[1] // 4),
            grid_spec=pltpu.PrefetchScalarGridSpec(
                num_scalar_prefetch=1,
                grid=(2 if blocked else 1,),
                in_specs=specs,
                out_specs=[whole(shape)] * 2,
                scratch_shapes=[
                    pltpu.VMEM((model, 2 * arrays[0].shape[0]), BF16),
                    pltpu.VMEM((model, width if blocked else 2 * width), BF16),
                    pltpu.VMEM((2, max(extra, 8), width), F32),
                ],
            ),
            out_shape=[jax.ShapeDtypeStruct(shape, BF16)] * 2,
            cost_estimate=CHEAP,
        compiler_params=pltpu.CompilerParams(vmem_limit_bytes=40 * 1024 * 1024),
        name="sum_units",
        )(where(), *given)
    order = jnp.bitwise_xor(jnp.arange(ndp), lax.axis_index("dp"))
    sides = []
    if extra:
        line = jnp.transpose(bias.reshape(2, 2, -1), (1, 0, 2)).reshape(2, -1)
        line = jnp.pad(line, ((0, 0), (0, width - line.shape[1]))).astype(BF16)
        both = jnp.broadcast_to(lines.astype(BF16)[None], (2, *lines.shape))
        ext = jnp.concatenate([bias_up.astype(BF16).reshape(2, 1, -1), both, line[:, None]], axis=1)
    for rx in range(2):
        g = []
        for (own, other), right, cols, _, by_block in parts:
            left = jnp.concatenate([arrays[own], arrays[other]])
            for j in range(1 if by_block else arrays[right].shape[1] // (2 * cols)):
                at = (2 * j + rx) * cols
                g.append(dot_tn(left, arrays[right][:, at : at + cols]).astype(BF16))
        g = jnp.concatenate(g, axis=1).reshape(ndp, piece, width)
        if extra:
            g = jnp.concatenate([g, jnp.broadcast_to(ext[rx][None], (ndp, extra, width))], axis=1)
        g = jnp.take(g, order, axis=0).reshape(ndp // 2, 2, piece + extra, width)
        sides.append(jnp.moveaxis(g, 1, 0))
    g = jnp.stack(sides)
    g = jnp.where(lax.axis_index("c") == 0, g, jnp.swapaxes(g, 0, 1))
    return g[0].reshape(ndp, piece + extra, width), g[1].reshape(ndp, piece + extra, width)


class Scatter:
    def __init__(self, pair):
        self.keep, self.send = pair

    def first(self):
        self.one = turn(self.send, 0)

    def second(self):
        half = self.keep.shape[0] // 2
        self.kept = add(self.keep[:half], self.one[:half])
        self.two = turn(add(self.keep[half:], self.one[half:]), 1)

    def third(self):
        total = add(self.kept, self.two)
        outer = total.shape[0]
        if outer <= 4:
            self.last = [total[0]]
            self.three = [flip(total[k], "dp", 2 * k) for k in range(1, outer)]
            return
        for k in reversed(range(outer_bits())):
            half = total.shape[0] // 2
            total = add(total[:half], flip(total[half:], "dp", 2 << k))
        self.last, self.three = [total[0]], []

    def result(self):
        return sum(t.astype(F32) for t in self.last + self.three)


def local(
    tokens, grad_out, seg_ids, w_qkv, b_qv, w_out, w_up, b_up, w_down, b_out, b_down, g_one, s_one, g_two, s_two
):
    ndp = lax.axis_size("dp")
    nx = lax.axis_size("x")
    parity = lax.axis_index("c")
    which = lax.axis_index("x")
    place_dp = lax.axis_index("dp")
    rows, model = tokens.shape
    piece = model // ndp
    part = w_qkv.shape[2]
    width = nx * part
    slim = model // (ndp * nx * 2)
    qv = part // ndp
    extra = 8
    block = 256
    tall = 512

    unit_a, unit_bc = prepare(
        w_qkv, w_out, w_up, w_down, b_qv, [b_out, b_down, g_one, s_one, g_two, s_two, b_up]
    )
    a_near = Spread(jnp.stack([unit_a, flip(unit_a, "dp", 2)]), 0)

    class Box:
        pass

    box = Box()
    box.bc = unit_bc
    a_near.units = stage("z1", a_near.units, bc=(box, "bc"))
    a_far = Spread(gather_far(a_near.units), 2)
    a_near.first()
    a_near.one = stage("n1", a_near.one, bc=(box, "bc"), az=(a_far, "units"))
    a_near.second()
    a_far.units = stage("z2", a_far.units, bc=(box, "bc"), an2=(a_near, "two"))
    a_far.first()
    bc_near = Spread(jnp.stack([box.bc, flip(box.bc, "dp", 2)]), 0)
    a_far.one = stage("f1", a_far.one, bz1=(bc_near, "units"), an2=(a_near, "two"))
    a_far.second()
    bc_far = Spread(gather_far(bc_near.units), 2)
    bc_items = lambda: dict(bn1=(bc_near, "one"), bz2=(bc_far, "units"), bn2=(bc_near, "two"), bf1=(bc_far, "one"), bf2=(bc_far, "two"))
    done = set()

    def advance(name, *values):
        res = stage(name, *values, **{k: v for k, v in bc_items().items() if hasattr(*v)})
        order = ["z2", "f1", "f2", "qkv", "ctx", "attn", "normed", "feed"]
        at = order.index(name)
        ready = lambda k: k is None or order.index(OPT.get(k, "feed")) <= at
        if "n1" not in done and order.index(OPT.get("rn1", "z2")) <= at:
            bc_near.first()
            done.add("n1")
        if "n2" not in done and "n1" in done and (ready("bn1") or name == "feed"):
            bc_near.second()
            done.add("n2")
        if "f1" not in done and (ready("bz2") or name == "feed"):
            bc_far.first()
            done.add("f1")
        if "f2" not in done and "f1" in done and (ready("bf1") or name == "feed"):
            bc_far.second()
            done.add("f2")
        return res

    advance("z2")
    a_far.two = advance("f2", a_far.two)

    seg = lax.dynamic_index_in_dim(seg_ids, which, 0, keepdims=False).reshape(2, rows)
    seg_rel = jnp.concatenate(
        [
            lax.dynamic_index_in_dim(seg, parity, 0, keepdims=False),
            lax.dynamic_index_in_dim(seg, 1 - parity, 0, keepdims=False),
        ]
    )
    seg_col = seg_rel[:, None]
    seg_row = seg_rel[None, :]
    x_other = swap(tokens)

    qkv, w_all, o_t, ext = project([a_near, a_far], tokens, x_other, piece, part, block)
    ext = ext[:, :3].astype(F32)
    ext = (ext[:, 0] + ext[:, 1] + ext[:, 2]).reshape(ndp, nx, 2 * part)
    bias_up = jnp.transpose(ext[:, :, 6 * slim : 6 * slim + piece], (1, 0, 2)).reshape(1, nx * model)
    six = ext[:, :, : 6 * slim]
    six = jnp.stack([six, swap(six)], axis=2)
    six = jnp.where(lax.broadcasted_iota(jnp.int32, (1, 1, 2, 1), 2) == parity, six[:, :, :1], six[:, :, 1:])
    six = jnp.where(which == 0, six, six[:, ::-1]).reshape(ndp * nx * 2, 6, slim)
    vectors = jnp.transpose(six, (1, 0, 2)).reshape(6, model)
    bout_f, bdown_f, gone_f, sone_f, gtwo_f, stwo_f = [vectors[i : i + 1] for i in range(6)]

    qkv = advance("qkv", qkv)
    ctx, lse = attention_forward(qkv, seg_col, seg_row, tall, 0, 2 * rows // tall, ())
    ctx = advance("ctx", ctx)
    attn_send = dot_nt(ctx[rows:], o_t).astype(BF16)
    attn = dot_nt(ctx[:rows], o_t) + swap(attn_send).astype(F32)
    attn = advance("attn", attn)
    first = tokens.astype(F32) + attn + bout_f
    hat_one, inv_one = normalize(first)
    normed = hat_one * gone_f + sone_f
    normed_low = advance("normed", normed.astype(BF16))
    normed_other = swap(normed_low)
    normed_other = advance("feed", normed_other)
    hidden, slope, keep, send, b_all, c_all = feed([bc_near, bc_far], normed_low, normed_other, bias_up, piece, block)
    vectors = jnp.pad(vectors, ((0, 2), (0, 0)))
    layer_out, d_branch, d_second, sums_two = norm_call(
        second_norm_kernel, block, [keep, swap(send), hat_one, grad_out], vectors, [BF16, BF16, F32]
    )
    db_other = swap(d_branch)

    sc = sb = sa = None
    order = ["P0", "P1", "P2", "P3", "P4", "P5", "P6", "P7"]
    sent = set()

    def go(name, *values):
        items = {}
        for k, s in (("c", sc), ("b", sb)):
            if s is not None:
                for n, f in (("1", "one"), ("2", "two"), ("3", "three")):
                    if hasattr(s, f):
                        items[k + n] = (s, f)
        res = stage(name, *values, **items)
        at = order.index(name)
        for k, s in (("c", sc), ("b", sb)):
            if s is None:
                continue
            for n, need, f in ((1, None, "first"), (2, "1", "second"), (3, "2", "third")):
                if k + str(n) in sent or (n > 1 and k + str(n - 1) not in sent):
                    continue
                if n == 1 or order.index(OPT.get(k + need, "P7")) <= at:
                    getattr(s, f)()
                    sent.add(k + str(n))
        return res

    keep, send, d_bias_up, *pairs = feed_back(
        d_branch, db_other, normed_low, normed_other, slope, hidden, c_all, b_all, piece
    )
    sc, sb = Scatter(pairs[:2]), Scatter(pairs[2:])
    go("P0")
    send = go("P1", swap(send))
    d_attn, d_first, sums_one = norm_call(
        first_norm_kernel, block, [keep, send, d_second, hat_one, inv_one], vectors, [BF16, F32]
    )
    da_other = swap(d_attn)
    d_ctx = dot_nn(d_attn, o_t).astype(BF16)
    sums = jnp.concatenate([sums_one[:1], sums_two[:1], sums_one[1:3], sums_two[1:3]])
    sums = sums + swap(sums)
    d_ctx_other = dot_nn(da_other, o_t).astype(BF16)
    d_ctx_other, sums = go("P2", d_ctx_other, sums)
    d_qkv, bias = attention_backward(qkv, ctx, lse, d_ctx, d_ctx_other, seg_col, seg_row, block)
    d_qkv = go("P3", d_qkv)
    attention_parts = [((0, 1), 2, part, 0, False), ((3, 4), 5, part, 3 * part, False)]
    given = [tokens, x_other, d_qkv, d_attn, da_other, ctx]
    sa = Scatter(summed(given, attention_parts, sums, d_bias_up, bias))
    d_qkv, sa.send = go("P4", d_qkv, sa.send)
    sa.first()
    keep, send = input_gradient(d_qkv, d_first, w_all, block)
    sa.one, keep, send = go("P5", sa.one, keep, send)
    sa.second()
    input_grad = keep + swap(send).astype(F32)
    sa.two, input_grad = go("P6", sa.two, input_grad)
    sa.third()
    go("P7")
    input_grad = input_grad.astype(BF16)
    gc = sc.result()
    gb = sb.result()
    ga = sa.result()
    g_qkv = jnp.stack([ga[:piece, j * part : (j + 1) * part] for j in range(3)])
    tail = ga[piece:]
    g_bqv = lax.dynamic_slice_in_dim(tail[7, : 2 * part].reshape(2, part), place_dp * qv, qv, axis=1)
    g_bup = lax.dynamic_slice_in_dim(tail[0], place_dp * piece, piece)
    six = lax.dynamic_slice_in_dim(tail[1:7], ((place_dp * nx + which) * 2 + parity) * slim, slim, axis=1)
    return (
        layer_out,
        input_grad,
        g_qkv,
        g_bqv,
        ga[:piece, 3 * part :].T,
        gb,
        g_bup,
        gc.T,
        *[six[i] for i in range(6)],
    )


def solution(mesh):
    ndp, nt = mesh.devices.shape
    fine = Mesh(mesh.devices.reshape(ndp, nt // 2, 2), ("dp", "x", "c"))
    tensor = ("x", "c")
    every = ("dp", "x", "c")
    row = P(every, None)
    vec = P(every)
    return jax.shard_map(
        local,
        mesh=fine,
        in_specs=(
            row,
            row,
            P("dp", None),
            P(None, "dp", tensor),
            P(None, ("x", "c", "dp")),
            P(tensor, "dp"),
            P("dp", tensor),
            P(("x", "c", "dp")),
            P(tensor, "dp"),
            vec,
            vec,
            vec,
            vec,
            vec,
            vec,
        ),
        out_specs=(
            row,
            row,
            P(None, "dp", tensor),
            P(None, ("x", "c", "dp")),
            P(tensor, "dp"),
            P("dp", tensor),
            P(("x", "c", "dp")),
            P(tensor, "dp"),
            vec,
            vec,
            vec,
            vec,
            vec,
            vec,
        ),
        check_vma=False,
    )
```
